128 devices in a mesh: rows: 8 (over x, core), cols: 16 (over z, y).
Axes of the slice: x: 4, y: 4, z: 4, core: 2. Of those that a mesh axis runs over, the one named last changes fastest.
Arguments:
- low_feats: bfloat16 [128, 512, 256], P('rows', 'cols'), may hold values from -6 to 6
- skip_feats: bfloat16 [256, 1024, 256], P('rows', 'cols'), may hold values from -6 to 6
- tissue_mask: int32 [64, 256], P('rows', 'cols'), may hold values 0 or 1
- owner_slot: int32 [64, 256], P('rows', 'cols'), may hold values from 0 to 16383, as said below
- filter_one: bfloat16 [32, 3, 3, 256], replicated, may hold values from -0.125 to 0.125
- filter_two: bfloat16 [32, 3, 3, 256], replicated, may hold values from -0.125 to 0.125
- out_grad: bfloat16 [256, 1024, 256], P('rows', 'cols'), may hold values from -6 to 6
Outputs:
- output: bfloat16 [256, 1024, 256], P('rows', 'cols')
- skip_grad: bfloat16 [16384, 4, 4, 256], P(('rows', 'cols'))
- low_grad: bfloat16 [128, 512, 256], P('rows', 'cols')
- filter_grad_one: float32 [32, 3, 3, 256], replicated
- filter_grad_two: float32 [32, 3, 3, 256], replicated
The draws below stay inside these ranges and needn't reach their ends.
Inputs may be any that keep to these rules, and one draw needn't show every extreme that they name: `owner_slot`: all values are distinct, so every encoder slot receives exactly one tile: each owner gets exactly 128 tiles. At most 2 tiles of one device go to one owner, and every device sends exactly 2 tiles to some owner.
All inputs are finite; a program needn't handle non-finite values. No bound on the sum of `tissue_mask` on one device may be relied on, other than what follows from the above.
Results may differ from the reference program's by a relative error of at most 0.006.
Values may be sent and summed in bfloat16 or wider, within the bound.
No kernel may reach another device: no remote copies, remote signals or barrier semaphores. Data moves between devices by JAX's collectives and lax.ppermute only.
A program may use at most 128 MiB of HBM per device.

```python
import math
import jax
import jax.numpy as jnp
import numpy as np
from jax import lax

C = 32
G = 8
P_SIZE = 4
TR = 8
TC = 16
TILES_DEV = 128
OWNERS = 128
CAP = 2
NTR = 64
NTC = 256
HEIGHT = 256
BREADTH = 1024
FEAT = 256
ENC_TILES = 16384
N_ROWS = 8
N_COLS = 16


def draw_owner_slot(key, part):
    key_count, key_order, key_source, key_owner, key_tiles = jax.random.split(key, 5)
    half = CAP // 2
    heavy = jax.random.randint(key_count, (), 1, OWNERS // 2 + 1)
    order = jax.random.permutation(key_order, OWNERS)
    position = jnp.zeros((OWNERS,), jnp.int32).at[order].set(jnp.arange(OWNERS, dtype=jnp.int32))
    counts = jnp.where(position < heavy, CAP, jnp.where(position < 2 * heavy, 0, half)).astype(jnp.int32)
    ends = jnp.cumsum(counts)
    slot_ids = jnp.arange(TILES_DEV, dtype=jnp.int32)
    group_of = jnp.sum((ends[None, :] <= slot_ids[:, None]).astype(jnp.int32), axis=1)
    source_shift = jax.random.permutation(key_source, OWNERS)
    owner_order = jax.random.permutation(key_owner, OWNERS)
    tile_keys = jax.random.split(key_tiles, OWNERS)
    shuffled = jax.vmap(lambda one_key: jax.random.permutation(one_key, TILES_DEV))(tile_keys)
    groups = group_of[shuffled]
    owner = owner_order[(source_shift[:, None] + groups) % OWNERS]
    flat_slot = owner * TILES_DEV + shuffled
    laid = flat_slot.reshape(N_ROWS, N_COLS, TR, TC).transpose(0, 2, 1, 3)
    return laid.reshape(N_ROWS * TR, N_COLS * TC).astype(jnp.int32)


def set_ends(entries, key, smallest, high):
    place = [jax.random.randint(jax.random.fold_in(key, axis), (), 0, length) for axis, length in enumerate(entries.shape)]
    widest = entries.shape.index(max(entries.shape))
    next_to = place[:widest] + [(place[widest] + 1) % entries.shape[widest]] + place[widest + 1:]
    return entries.at[tuple(place)].set(smallest).at[tuple(next_to)].set(high)


def steps_of(key, shape, cuts, least, top_value):
    gain, own = 1.0, jax.random.fold_in(key, 6)
    for axis_at, blocks in cuts:
        heights = jnp.exp(jax.random.uniform(jax.random.fold_in(own, axis_at), (blocks,), jnp.float32, least / len(cuts), top_value / len(cuts)))
        gain = gain * jnp.repeat(heights, shape[axis_at] // blocks).reshape([-1 if axis == axis_at else 1 for axis in range(len(shape))])
    return gain


def centred(stream_key, shape, deviation, limit, pieces=(), kind=jnp.bfloat16):
    level = steps_of(stream_key, shape, pieces, -0.22, 0.18) if pieces else 1.0
    entries = jax.random.normal(stream_key, shape, jnp.float32) * deviation * level
    return jnp.minimum(jnp.maximum(entries, -limit), limit).astype(kind)


def setup_inputs(seed: int = 0) -> dict:
    key_of = jax.random.split(jax.random.key(seed), 8)
    return {
        "low_feats": centred(key_of[0], (HEIGHT // 2, BREADTH // 2, FEAT), 1.0, 6.0, ((0, 8), (1, 16))),
        "skip_feats": centred(key_of[1], (HEIGHT, BREADTH, FEAT), 1.0, 6.0, ((0, 8), (1, 16))),
        "tissue_mask": set_ends((jax.random.randint(key_of[2], (NTR, NTC), 0, 4) < 3).astype(jnp.int32), jax.random.fold_in(key_of[2], 1), 0, 1),
        "owner_slot": draw_owner_slot(jax.random.fold_in(key_of[7], 71), 0),
        "filter_one": centred(key_of[4], (C, 3, 3, FEAT), (9 * FEAT) ** -0.5, 0.125),
        "filter_two": centred(key_of[5], (C, 3, 3, FEAT), (9 * FEAT) ** -0.5, 0.125),
        "out_grad": centred(key_of[6], (HEIGHT, BREADTH, FEAT), 1.0, 6.0, ((0, 8), (1, 16))),
    }


def element_inverse(element):
    mirror = element // 4
    turns = element % 4
    return np.where(mirror == 0, (4 - turns) % 4, element)

def element_product(first, second):
    mirror = (first // 4 + second // 4) % 2
    turns = (first % 4 + (1 - 2 * (first // 4)) * (second % 4)) % 4
    return mirror * 4 + turns

def element_act(element, row_off, col_off):
    mirror = element // 4
    turns = element % 4
    col_now = np.where(mirror == 1, -col_off, col_off)
    row_now = row_off
    for step in range(3):
        rotated_row = -col_now
        rotated_col = row_now
        row_now = np.where(turns > step, rotated_row, row_now)
        col_now = np.where(turns > step, rotated_col, col_now)
    return (row_now, col_now)

def group_index(channels):
    features = channels * G
    row_in, col_in, feat_in, out_chan, out_elem = np.meshgrid(np.arange(3), np.arange(3), np.arange(features), np.arange(channels), np.arange(G), indexing='ij')
    inverse = element_inverse(out_elem)
    moved_row, moved_col = element_act(inverse, row_in - 1, col_in - 1)
    moved_elem = element_product(inverse, feat_in % G)
    flat_index = ((out_chan * 3 + moved_row + 1) * 3 + moved_col + 1) * features + feat_in // G * G + moved_elem
    return flat_index.reshape(3, 3, features, features).astype(np.int32)

def expand(base):
    channels = base.shape[0]
    features = base.shape[3]
    table = jnp.asarray(group_index(channels).reshape(-1))
    return base.reshape(-1)[table].reshape(3, 3, features, features)

def fold_filter(grad_full, channels):
    features = channels * G
    table = jnp.asarray(group_index(channels).reshape(-1))
    summed = jax.ops.segment_sum(grad_full.reshape(-1), table, num_segments=channels * 9 * features)
    return summed.reshape(channels, 3, 3, features)

def pad_cycle(field):
    return jnp.pad(field, ((1, 1), (1, 1), (0, 0)))

def conv_valid(padded, kernel):
    result = lax.conv_general_dilated(padded[None].astype(jnp.float32), kernel.astype(jnp.float32), (1, 1), 'VALID', dimension_numbers=('NHWC', 'HWIO', 'NHWC'), precision=lax.Precision.HIGHEST)
    return result[0]

def flipped(kernel):
    return jnp.flip(kernel, (0, 1)).transpose(0, 1, 3, 2)

def filter_terms(padded, grad_out):
    height = grad_out.shape[0]
    breadth = grad_out.shape[1]
    flat_grad = grad_out.reshape(-1, grad_out.shape[2]).astype(jnp.float32)
    stacked = []
    for row_off in range(3):
        for col_off in range(3):
            window = padded[row_off:row_off + height, col_off:col_off + breadth].reshape(-1, padded.shape[2]).astype(jnp.float32)
            stacked.append(lax.dot_general(window, flat_grad, (((0,), (0,)), ((), ())), precision=lax.Precision.HIGHEST, preferred_element_type=jnp.float32))
    return jnp.stack(stacked).reshape(3, 3, padded.shape[2], grad_out.shape[2])

def silu_slope(value):
    sigma = jax.nn.sigmoid(value)
    return sigma * (1.0 + value * (1.0 - sigma))

def reference(low_feats, skip_feats, tissue_mask, owner_slot, filter_one, filter_two, out_grad):
    pixel_mask = jnp.repeat(jnp.repeat(tissue_mask, P_SIZE, 0), P_SIZE, 1).astype(jnp.float32)[:, :, None]
    upsampled = jnp.repeat(jnp.repeat(low_feats, 2, 0), 2, 1).astype(jnp.float32)
    merged = ((upsampled + skip_feats.astype(jnp.float32)) * pixel_mask).astype(jnp.bfloat16)
    kernel_one = expand(filter_one)
    kernel_two = expand(filter_two)
    padded_merged = pad_cycle(merged)
    pre_one = conv_valid(padded_merged, kernel_one)
    hidden = (jax.nn.silu(pre_one) * pixel_mask).astype(jnp.bfloat16)
    padded_hidden = pad_cycle(hidden)
    output = (conv_valid(padded_hidden, kernel_two) * pixel_mask).astype(jnp.bfloat16)
    grad_two = (out_grad.astype(jnp.float32) * pixel_mask).astype(jnp.bfloat16)
    grad_hidden = conv_valid(pad_cycle(grad_two), flipped(kernel_two))
    grad_pre = (grad_hidden * silu_slope(pre_one) * pixel_mask).astype(jnp.bfloat16)
    grad_merged = conv_valid(pad_cycle(grad_pre), flipped(kernel_one)) * pixel_mask
    low_grad = grad_merged.reshape(HEIGHT // 2, 2, BREADTH // 2, 2, FEAT).sum(axis=(1, 3)).astype(jnp.bfloat16)
    skip_tiles = grad_merged.astype(jnp.bfloat16).reshape(NTR, P_SIZE, NTC, P_SIZE, FEAT).transpose(0, 2, 1, 3, 4).reshape(NTR * NTC, P_SIZE, P_SIZE, FEAT)
    skip_grad = jnp.zeros((ENC_TILES, P_SIZE, P_SIZE, FEAT), jnp.bfloat16).at[owner_slot.reshape(-1).astype(jnp.int32)].set(skip_tiles)
    scale = 1.0 / math.sqrt(HEIGHT * BREADTH)
    filter_grad_one = fold_filter(filter_terms(padded_merged, grad_pre), C) * scale
    filter_grad_two = fold_filter(filter_terms(padded_hidden, grad_two), C) * scale
    return (output, skip_grad, low_grad, filter_grad_one, filter_grad_two)
```

```python
import functools
import math

import jax
import jax.numpy as jnp
import numpy as np
from jax import lax
from jax.experimental import pallas as pl
from jax.experimental.pallas import tpu as pltpu
from jax.sharding import PartitionSpec as P

G = 8
F = 256
ROWS = 32
WIDE = 64
STRIP = 48
MASK_ROWS = 16
BF = jnp.bfloat16
F32 = jnp.float32
VMEM = pl.BlockSpec(memory_space=pltpu.VMEM)
SMEM = pl.BlockSpec(memory_space=pltpu.SMEM)


def inverse_of(element):
    return (4 - element % 4) % 4 if element < 4 else element


def product(first, second):
    mirror = (first // 4 + second // 4) % 2
    turns = (first % 4 + (1 - 2 * (first // 4)) * (second % 4)) % 4
    return mirror * 4 + turns


def act(element, row, col):
    if element // 4:
        col = -col
    for _ in range(element % 4):
        row, col = -col, row
    return row, col


def source_cell(elem, pos):
    row, col = act(inverse_of(elem), pos // 3 - 1, pos % 3 - 1)
    return (row + 1) * 3 + col + 1


def iota(shape, dim):
    return lax.broadcasted_iota(jnp.int32, shape, dim)


def one_hot(cond):
    return jnp.where(cond, 1.0, 0.0).astype(BF)


def permuted_index(index, elem):
    inverse = inverse_of(elem)
    mirror, turns = inverse // 4, inverse % 4
    second = index & 7
    new_mirror = (second >> 2) ^ mirror
    spin = second & 3
    new_turns = (turns + (-spin if mirror else spin)) & 3
    return (index & ~7) | (new_mirror << 2) | new_turns


def dot(lhs, rhs):
    return jnp.dot(lhs, rhs, preferred_element_type=F32)


def dot_nt(lhs, rhs):
    return lax.dot_general(lhs, rhs, (((1,), (1,)), ((), ())), preferred_element_type=F32)


def call(kernel, out_shape, n_in, scratch=(), specs=None, flops=1 << 30, limit=40 << 20, name=None):
    return pl.pallas_call(
        kernel,
        out_shape=out_shape,
        in_specs=specs or [VMEM] * n_in,
        out_specs=jax.tree.map(lambda _: VMEM, out_shape),
        scratch_shapes=list(scratch),
        compiler_params=pltpu.CompilerParams(vmem_limit_bytes=limit),
        cost_estimate=pl.CostEstimate(flops=flops, bytes_accessed=4 << 20, transcendentals=0),
        name=name,
    )


def shape(dims, dtype=BF):
    return jax.ShapeDtypeStruct(dims, dtype)


def prep_kernel(low, skip, grad, mask_rows, merged, grad_two, up, down):
    spread = one_hot((iota((WIDE, 16), 0) >> 2) == iota((WIDE, 16), 1))
    twice = one_hot((iota((WIDE, 32), 0) >> 1) == iota((WIDE, 32), 1))
    for tile_row in range(8):
        mask = dot(spread, mask_rows[tile_row * 16 : tile_row * 16 + 16, :].astype(BF))
        for half in range(2):
            low_row = tile_row * 2 + half
            coarse = dot(twice, low[low_row * 32 : low_row * 32 + 32, :])
            for sub in range(2):
                here = pl.ds((low_row * 2 + sub) * WIDE, WIDE)
                merged[here, :] = ((coarse + skip[here, :].astype(F32)) * mask).astype(BF)
                grad_two[here, :] = (grad[here, :].astype(F32) * mask).astype(BF)
    two = 2 * WIDE
    up[0:two, :] = merged[0:two, :]
    up[two : 2 * two, :] = grad_two[0:two, :]
    up[2 * two : 2 * two + 16, :] = mask_rows[0:16, :].astype(BF)
    last = ROWS * WIDE - two
    down[0:two, :] = merged[last : last + two, :]
    down[two : 2 * two, :] = grad_two[last : last + two, :]
    down[2 * two : 2 * two + 16, :] = mask_rows[112:128, :].astype(BF)


def expand_kernel(filter_one, filter_two, fwd_one, fwd_two, bwd_one, bwd_two):
    across = iota((F, F), 0)
    along = iota((F, F), 1)
    weave = one_hot(((across & 7) * 32 + (across >> 3)) == along)
    perms = [one_hot(across == permuted_index(along, elem)) for elem in range(G)]
    for base, fwd, bwd in ((filter_one, fwd_one, bwd_one), (filter_two, fwd_two, bwd_two)):
        turned = [dot(base[...], perms[elem]).astype(BF) for elem in range(G)]
        for pos in range(9):
            rows = []
            for elem in range(G):
                cell = source_cell(elem, pos)
                rows.append(turned[elem][cell * 32 : cell * 32 + 32, :])
            gathered = jnp.concatenate(rows, axis=0)
            woven = dot(weave, gathered)
            bwd[(8 - pos) * F : (9 - pos) * F, :] = woven.astype(BF)
            fwd[pos * F : (pos + 1) * F, :] = woven.T.astype(BF)


def edge_kernel(merged, grad_two, top, bottom, mask_rows, left, right, tall, masks):
    two = 2 * WIDE
    tall[:, 36 * 16 : 48 * 16, :] = jnp.zeros((2, 12 * 16, 128), F32)

    def keep(row, values):
        for half in range(2):
            tall[half, row * 16 : row * 16 + 16, :] = values[:, half * 128 : half * 128 + 128].astype(F32)

    for side, (target, offset, picks, tile_col) in enumerate(
        ((left, 0, (0, 1), 0), (right, 48, (14, 15), 15))
    ):
        for image, source in enumerate((merged, grad_two)):
            for row in range(2):
                place = image * two + row * WIDE + offset
                keep(row, top[place : place + 16, :])
                keep(34 + row, bottom[place : place + 16, :])
            for row in range(ROWS):
                place = row * WIDE + offset
                keep(row + 2, source[place : place + 16, :])
            for col in range(2):
                strip = (image * 2 + col) * STRIP
                for half in range(2):
                    target[strip : strip + STRIP, half * 128 : half * 128 + 128] = tall[
                        half, pl.ds(picks[col], STRIP, stride=16), :
                    ].astype(BF)
        masks[...] = jnp.zeros((STRIP, F), F32)
        above = top[2 * two : 2 * two + 16, :].astype(F32)
        below = bottom[2 * two : 2 * two + 16, :].astype(F32)
        masks[0:2, :] = jnp.broadcast_to(above[tile_col : tile_col + 1, :], (2, F))
        masks[34:36, :] = jnp.broadcast_to(below[tile_col : tile_col + 1, :], (2, F))
        for tile_row in range(8):
            at = tile_row * 16 + tile_col
            masks[2 + 4 * tile_row : 6 + 4 * tile_row, :] = jnp.broadcast_to(mask_rows[at : at + 1, :], (4, F))
        target[4 * STRIP : 5 * STRIP, :] = masks[...].astype(BF)


def shifted_store(target, at, value, plain, before, after):
    row = iota((WIDE, F), 0)
    target[pl.ds(at, WIDE), 0:F] = jnp.where(row == 0, before, pltpu.roll(value, 1, 0)).astype(BF)
    target[pl.ds(at, WIDE), F : 2 * F] = plain
    target[pl.ds(at, WIDE), 2 * F : 3 * F] = jnp.where(
        row == WIDE - 1, after, pltpu.roll(value, WIDE - 1, 0)
    ).astype(BF)


def conv(shifted, start, count, weight):
    lhs = jnp.concatenate([shifted[pl.ds(start + ky * WIDE, count), :] for ky in range(3)], axis=1)
    return dot(lhs, weight[...])


def main_kernel(
    slots, merged, grad_two, top, bottom, left, right, from_left, from_right, mask_rows,
    fwd_one, fwd_two, bwd_one, bwd_two,
    output, low_grad, send, slot_rows, merged_shift, hidden_shift, grad_pre,
    grad_shift, pre_shift, strips, edge, mask_wide, pre, grad_hidden, pair, tiles, count,
):
    two = 2 * WIDE
    spread = one_hot((iota((WIDE, 16), 0) >> 2) == iota((WIDE, 16), 1))
    mask_wide[0:WIDE, :] = dot(spread, top[2 * two : 2 * two + 16, :])
    mask_wide[9 * WIDE : 10 * WIDE, :] = dot(spread, bottom[2 * two : 2 * two + 16, :])
    for tile_row in range(8):
        mask_wide[(tile_row + 1) * WIDE : (tile_row + 2) * WIDE, :] = dot(
            spread, mask_rows[tile_row * 16 : tile_row * 16 + 16, :].astype(BF)
        )
    strip_pre = []
    for image, (source, target, weight) in enumerate(
        ((merged, merged_shift, fwd_one), (grad_two, grad_shift, bwd_two))
    ):
        first = image * 2 * STRIP
        columns = (
            from_left[first : first + STRIP, :],
            from_left[first + STRIP : first + 2 * STRIP, :],
            left[first : first + STRIP, :],
            right[first + STRIP : first + 2 * STRIP, :],
            from_right[first : first + STRIP, :],
            from_right[first + STRIP : first + 2 * STRIP, :],
        )
        for index, column in enumerate(columns):
            strips[index * STRIP : (index + 1) * STRIP, :] = column.astype(F32)
        for row in range(2):
            at = image * two + row * WIDE
            for halo, place in ((top, row), (bottom, 34 + row)):
                plain = halo[at : at + WIDE, :]
                shifted_store(
                    target, place * WIDE, plain.astype(F32), plain,
                    strips[STRIP + place : STRIP + place + 1, :],
                    strips[4 * STRIP + place : 4 * STRIP + place + 1, :],
                )

        def shift_row(row, _, source=source, target=target):
            plain = source[pl.ds(pl.multiple_of(row * WIDE, WIDE), WIDE), :]
            shifted_store(
                target, pl.multiple_of((row + 2) * WIDE, WIDE), plain.astype(F32), plain,
                strips[pl.ds(STRIP + 2 + row, 1), :],
                strips[pl.ds(4 * STRIP + 2 + row, 1), :],
            )
            return 0

        lax.fori_loop(0, ROWS, shift_row, 0)
        parts = []
        for ky in range(3):
            for kx in range(3):
                parts.append(
                    jnp.concatenate(
                        [
                            strips[kx * STRIP + ky : kx * STRIP + ky + 40, :],
                            strips[(kx + 3) * STRIP + ky : (kx + 3) * STRIP + ky + 40, :],
                        ],
                        axis=0,
                    ).astype(BF)
                )
        strip_pre.append(dot(jnp.concatenate(parts, axis=1), weight[...]))
    strips[0:STRIP, :] = from_left[4 * STRIP : 5 * STRIP, :].astype(F32)
    strips[STRIP : 2 * STRIP, :] = from_right[4 * STRIP : 5 * STRIP, :].astype(F32)
    strip_mask = jnp.concatenate([strips[1:41, :], strips[STRIP + 1 : STRIP + 41, :]], axis=0)
    sigma = jax.nn.sigmoid(strip_pre[0])
    edge[0:80, :] = (strip_pre[0] * sigma * strip_mask).astype(BF).astype(F32)
    edge[80:160, :] = (
        (strip_pre[1] * (sigma * (1.0 + strip_pre[0] * (1.0 - sigma))) * strip_mask).astype(BF).astype(F32)
    )

    def first_convs(step, _):
        at = pl.multiple_of(step * 544, 16)
        pre[pl.ds(at, 544), :] = conv(merged_shift, at, 544, fwd_one)
        grad_hidden[pl.ds(at, 544), :] = conv(grad_shift, at, 544, bwd_two)
        return 0

    lax.fori_loop(0, 4, first_convs, 0)

    def activate(row, _):
        at = pl.multiple_of(row * WIDE, WIDE)
        mask = mask_wide[pl.ds(pl.multiple_of(((row + 3) >> 2) * WIDE, WIDE), WIDE), :]
        value = pre[pl.ds(at, WIDE), :]
        sigma = jax.nn.sigmoid(value)
        hidden = value * sigma * mask
        slope = sigma * (1.0 + value * (1.0 - sigma))
        grad_value = grad_hidden[pl.ds(at, WIDE), :] * slope * mask
        shifted_store(
            hidden_shift, at, hidden, hidden.astype(BF), edge[pl.ds(row, 1), :], edge[pl.ds(40 + row, 1), :]
        )
        shifted_store(
            pre_shift, at, grad_value, grad_value.astype(BF),
            edge[pl.ds(80 + row, 1), :], edge[pl.ds(120 + row, 1), :],
        )
        return 0

    lax.fori_loop(0, ROWS + 2, activate, 0)
    grad_pre[...] = pre_shift[WIDE : 33 * WIDE, F : 2 * F]

    order = iota((F, F), 0)
    tile_order = one_hot(
        iota((F, F), 1) == (((order >> 2) & 3) * WIDE + (order >> 4) * 4 + (order & 3))
    )

    def second_convs(step, _):
        at = pl.multiple_of(step * 512, 512)
        masks = []
        for tile_row in range(2):
            mask = mask_wide[pl.ds(pl.multiple_of((step * 2 + tile_row + 1) * WIDE, WIDE), WIDE), :]
            masks.append(jnp.concatenate([mask] * 4, axis=0))
        mask = jnp.concatenate(masks, axis=0)
        output[pl.ds(at, 512), :] = (conv(hidden_shift, at, 512, fwd_two) * mask).astype(BF)
        grad_merged = conv(pre_shift, at, 512, bwd_one) * mask
        rounded = grad_merged.astype(BF)
        for tile_row in range(2):
            tiles[pl.ds(at + tile_row * F, F), :] = dot(
                tile_order, rounded[tile_row * F : (tile_row + 1) * F, :]
            ).astype(BF)
        for row in range(4):
            both = grad_merged[row * two : row * two + WIDE, :] + grad_merged[row * two + WIDE : row * two + two, :]
            for half in range(2):
                pair[half, row * WIDE : (row + 1) * WIDE, :] = both[:, half * 128 : half * 128 + 128]
        for half in range(2):
            low_grad[pl.ds(pl.multiple_of(step * 128, 128), 128), half * 128 : half * 128 + 128] = (
                pair[half, pl.ds(0, 128, stride=2), :] + pair[half, pl.ds(1, 128, stride=2), :]
            ).astype(BF)
        return 0

    lax.fori_loop(0, 4, second_convs, 0)

    def clear(index, _):
        count[index] = 0
        return 0

    lax.fori_loop(0, 128, clear, 0)
    slot_rows[...] = jnp.full((128, 128), -1.0, F32)
    lane = iota((1, 128), 1)

    def pack(tile, _):
        flat = slots[tile >> 4, tile & 15]
        owner = flat >> 7
        used = count[owner]
        count[owner] = used + 1
        send[pl.ds(pl.multiple_of((owner * 2 + used) * 16, 16), 16), :] = tiles[
            pl.ds(pl.multiple_of(tile * 16, 16), 16), :
        ]
        local = (flat & 127).astype(F32)
        slot_rows[pl.ds(owner, 1), :] = jnp.where(lane == used, local, slot_rows[pl.ds(owner, 1), :])
        return 0

    lax.fori_loop(0, 128, pack, 0)


def filter_kernel(merged_shift, hidden_shift, grad_pre, grad_two, slot_rows, message, folded):
    across = iota((F, F), 0)
    along = iota((F, F), 1)
    unweave = one_hot(((along & 7) * 32 + (along >> 3)) == across)
    perms = [one_hot(along == permuted_index(across, elem)) for elem in range(G)]
    back = jnp.concatenate(perms, axis=0)
    for index, (values, grads, skip) in enumerate(
        ((merged_shift, grad_pre, WIDE), (hidden_shift, grad_two, 0))
    ):
        turned = dot_nt(unweave, grads[...]).astype(BF)
        full = []
        for ky in range(3):
            start = skip + ky * WIDE
            full.append(dot(turned, values[start : start + ROWS * WIDE, :]).astype(BF))
        pieces = []
        for elem in range(G):
            of_cell = {source_cell(elem, pos): pos for pos in range(9)}
            rows = []
            for cell in range(9):
                pos = of_cell[cell]
                kx = pos % 3
                rows.append(full[pos // 3][elem * 32 : elem * 32 + 32, kx * F : (kx + 1) * F])
            pieces.append(jnp.concatenate(rows, axis=0))
        folded[index * 288 : (index + 1) * 288, :] = dot(jnp.concatenate(pieces, axis=1), back)
    folded[576:592, :] = jnp.zeros((16, F), F32)
    row = iota((16, 128), 0)
    for part in range(128):
        start, lanes = 9 * (part % 64), (part // 64) * 128
        data = folded[start : start + 16, lanes : lanes + 128]
        message[part, :, :] = jnp.where(row == 9, slot_rows[part : part + 1, :], data).astype(BF)


def sum_kernel(got, message, slots):
    total = jnp.zeros((16, 128), F32)
    for part in range(128):
        total = total + got[part, :, :].astype(F32)
    rounded = total.astype(BF)
    for part in range(128):
        message[part, :, :] = rounded
    slots[...] = got[:, 9, :].astype(F32).astype(jnp.int32)


def place_kernel(scale, slots, got, sums, skip_grad, one, two, folded):
    def put(index, _):
        for which in range(2):
            slot = slots[index, which]

            @pl.when(slot >= 0)
            def _():
                skip_grad[pl.ds(pl.multiple_of(slot * 16, 16), 16), :] = got[
                    pl.ds(pl.multiple_of((index * 2 + which) * 16, 16), 16), :
                ]

        return 0

    lax.fori_loop(0, 128, put, 0)
    for part in range(128):
        start, lanes = 9 * (part % 64), (part // 64) * 128
        folded[start : start + 16, lanes : lanes + 128] = sums[part, :, :].astype(F32) * scale
    one[...] = folded[0:288, :]
    two[...] = folded[288:576, :]


def shift(values, axis, step):
    size = lax.axis_size(axis)
    if step > 0:
        pairs = [(i, i + 1) for i in range(size - 1)]
    else:
        pairs = [(i + 1, i) for i in range(size - 1)]
    return lax.ppermute(values, axis, pairs)


def on_device(low_feats, skip_feats, tissue_mask, owner_slot, filter_one, filter_two, out_grad):
    everyone = ("rows", "cols")
    height, breadth, features = skip_feats.shape
    pixels = height * breadth
    mask_rows = jnp.broadcast_to(tissue_mask.astype(F32).reshape(128, 1), (128, F))
    merged, grad_two, up, down = call(
        prep_kernel,
        [shape((pixels, F)), shape((pixels, F)), shape((272, F)), shape((272, F))],
        4, name="prep",
    )(
        low_feats.reshape(-1, F), skip_feats.reshape(pixels, F), out_grad.reshape(pixels, F), mask_rows
    )
    bottom = shift(up, "rows", -1)
    top = shift(down, "rows", 1)
    bases = [f.transpose(1, 2, 0, 3).reshape(288, F) for f in (filter_one, filter_two)]
    fwd_one, fwd_two, bwd_one, bwd_two = call(
        expand_kernel, [shape((9 * F, F))] * 4, 2, name="expand"
    )(*bases)
    left, right = call(
        edge_kernel,
        [shape((5 * STRIP, F))] * 2,
        5, [pltpu.VMEM((2, 48 * 16, 128), F32), pltpu.VMEM((STRIP, F), F32)], name="edge",
    )(merged, grad_two, top, bottom, mask_rows)
    from_right = shift(left, "cols", -1)
    from_left = shift(right, "cols", 1)
    output, low_grad, send, slot_rows, merged_shift, hidden_shift, grad_pre = call(
        main_kernel,
        [
            shape((pixels, F)), shape((pixels // 4, F)), shape((4096, F)), shape((128, 128), F32),
            shape((36 * WIDE, 3 * F)), shape((34 * WIDE, 3 * F)), shape((pixels, F)),
        ],
        14,
        [
            pltpu.VMEM((36 * WIDE, 3 * F), BF), pltpu.VMEM((34 * WIDE, 3 * F), BF),
            pltpu.VMEM((6 * STRIP, F), F32), pltpu.VMEM((160, F), F32), pltpu.VMEM((10 * WIDE, F), F32),
            pltpu.VMEM((34 * WIDE, F), F32), pltpu.VMEM((34 * WIDE, F), F32),
            pltpu.VMEM((2, 4 * WIDE, 128), F32), pltpu.VMEM((pixels, F), BF), pltpu.SMEM((128,), jnp.int32),
        ],
        specs=[SMEM] + [VMEM] * 13, flops=10 << 30, name="convs",
    )(
        owner_slot, merged, grad_two, top, bottom, left, right, from_left, from_right, mask_rows,
        fwd_one, fwd_two, bwd_one, bwd_two,
    )
    got_tiles = lax.all_to_all(send.reshape(128, 32, F), everyone, 0, 0, tiled=True)
    message = call(
        filter_kernel, shape((128, 16, 128)), 5, [pltpu.VMEM((592, F), F32)], flops=6 << 30, name="filters"
    )(merged_shift, hidden_shift, grad_pre, grad_two, slot_rows)
    got_terms = lax.all_to_all(message, everyone, 0, 0, tiled=True)
    sums, slots = call(
        sum_kernel, [shape((128, 16, 128)), shape((128, 128), jnp.int32)], 1, name="sums"
    )(got_terms)
    got_sums = lax.all_to_all(sums, everyone, 0, 0, tiled=True)
    scale = 1.0 / math.sqrt(pixels * lax.axis_size("rows") * lax.axis_size("cols"))
    skip_grad, one, two = call(
        functools.partial(place_kernel, scale),
        [shape((2048, F)), shape((288, F), F32), shape((288, F), F32)],
        3, [pltpu.VMEM((592, F), F32)], specs=[SMEM, VMEM, VMEM], name="place",
    )(slots, got_tiles.reshape(4096, F), got_sums)
    return (
        output.reshape(height, breadth, F),
        skip_grad.reshape(128, 4, 4, F),
        low_grad.reshape(height // 2, breadth // 2, F),
        one.reshape(3, 3, 32, F).transpose(2, 0, 1, 3),
        two.reshape(3, 3, 32, F).transpose(2, 0, 1, 3),
    )


def solution(mesh):
    placed = (
        P("rows", "cols", None),
        P("rows", "cols", None),
        P("rows", "cols"),
        P("rows", "cols"),
        P(),
        P(),
        P("rows", "cols", None),
    )
    return jax.shard_map(
        on_device,
        mesh=mesh,
        in_specs=placed,
        out_specs=(
            P("rows", "cols", None),
            P(("rows", "cols"), None, None, None),
            P("rows", "cols", None),
            P(),
            P(),
        ),
        check_vma=False,
    )
```

```python
import functools
import math

import jax
import jax.numpy as jnp
import numpy as np
from jax import lax
from jax.experimental import pallas as pl
from jax.experimental.pallas import tpu as pltpu
from jax.sharding import PartitionSpec as P

G = 8
F = 256
ROWS = 32
WIDE = 64
STRIP = 48
MASK_ROWS = 16
BF = jnp.bfloat16
F32 = jnp.float32
VMEM = pl.BlockSpec(memory_space=pltpu.VMEM)
SMEM = pl.BlockSpec(memory_space=pltpu.SMEM)


def inverse_of(element):
    return (4 - element % 4) % 4 if element < 4 else element


def product(first, second):
    mirror = (first // 4 + second // 4) % 2
    turns = (first % 4 + (1 - 2 * (first // 4)) * (second % 4)) % 4
    return mirror * 4 + turns


def act(element, row, col):
    if element // 4:
        col = -col
    for _ in range(element % 4):
        row, col = -col, row
    return row, col


def source_cell(elem, pos):
    row, col = act(inverse_of(elem), pos // 3 - 1, pos % 3 - 1)
    return (row + 1) * 3 + col + 1


def iota(shape, dim):
    return lax.broadcasted_iota(jnp.int32, shape, dim)


def one_hot(cond):
    return jnp.where(cond, 1.0, 0.0).astype(BF)


def permuted_index(index, elem):
    inverse = inverse_of(elem)
    mirror, turns = inverse // 4, inverse % 4
    second = index & 7
    new_mirror = (second >> 2) ^ mirror
    spin = second & 3
    new_turns = (turns + (-spin if mirror else spin)) & 3
    return (index & ~7) | (new_mirror << 2) | new_turns


def dot(lhs, rhs):
    return jnp.dot(lhs, rhs, preferred_element_type=F32)


def dot_nt(lhs, rhs):
    return lax.dot_general(lhs, rhs, (((1,), (1,)), ((), ())), preferred_element_type=F32)


def call(kernel, out_shape, n_in, scratch=(), specs=None, flops=1 << 30, limit=40 << 20, name=None):
    return pl.pallas_call(
        kernel,
        out_shape=out_shape,
        in_specs=specs or [VMEM] * n_in,
        out_specs=jax.tree.map(lambda _: VMEM, out_shape),
        scratch_shapes=list(scratch),
        compiler_params=pltpu.CompilerParams(vmem_limit_bytes=limit),
        cost_estimate=pl.CostEstimate(flops=flops, bytes_accessed=4 << 20, transcendentals=0),
        name=name,
    )


def shape(dims, dtype=BF):
    return jax.ShapeDtypeStruct(dims, dtype)


def prep_kernel(low, skip, grad, mask_rows, merged, grad_two, up, down):
    spread = one_hot((iota((WIDE, 16), 0) >> 2) == iota((WIDE, 16), 1))
    twice = one_hot((iota((WIDE, 32), 0) >> 1) == iota((WIDE, 32), 1))
    for tile_row in range(8):
        mask = dot(spread, mask_rows[tile_row * 16 : tile_row * 16 + 16, :].astype(BF))
        for half in range(2):
            low_row = tile_row * 2 + half
            coarse = dot(twice, low[low_row * 32 : low_row * 32 + 32, :])
            for sub in range(2):
                here = pl.ds((low_row * 2 + sub) * WIDE, WIDE)
                merged[here, :] = ((coarse + skip[here, :].astype(F32)) * mask).astype(BF)
                grad_two[here, :] = (grad[here, :].astype(F32) * mask).astype(BF)
    two = 2 * WIDE
    up[0:two, :] = merged[0:two, :]
    up[two : 2 * two, :] = grad_two[0:two, :]
    up[2 * two : 2 * two + 16, :] = mask_rows[0:16, :].astype(BF)
    last = ROWS * WIDE - two
    down[0:two, :] = merged[last : last + two, :]
    down[two : 2 * two, :] = grad_two[last : last + two, :]
    down[2 * two : 2 * two + 16, :] = mask_rows[112:128, :].astype(BF)


def expand_kernel(filter_one, filter_two, fwd_one, fwd_two, bwd_one, bwd_two):
    across = iota((F, F), 0)
    along = iota((F, F), 1)
    weave = one_hot(((across & 7) * 32 + (across >> 3)) == along)
    perms = [one_hot(across == permuted_index(along, elem)) for elem in range(G)]
    for base, fwd, bwd in ((filter_one, fwd_one, bwd_one), (filter_two, fwd_two, bwd_two)):
        turned = [dot(base[...], perms[elem]).astype(BF) for elem in range(G)]
        for pos in range(9):
            rows = []
            for elem in range(G):
                cell = source_cell(elem, pos)
                rows.append(turned[elem][cell * 32 : cell * 32 + 32, :])
            gathered = jnp.concatenate(rows, axis=0)
            woven = dot(weave, gathered)
            bwd[(8 - pos) * F : (9 - pos) * F, :] = woven.astype(BF)
            fwd[pos * F : (pos + 1) * F, :] = woven.T.astype(BF)


def edge_kernel(merged, grad_two, top, bottom, mask_rows, left, right, tall, masks):
    two = 2 * WIDE
    tall[:, 36 * 16 : 48 * 16, :] = jnp.zeros((2, 12 * 16, 128), F32)

    def keep(row, values):
        for half in range(2):
            tall[half, row * 16 : row * 16 + 16, :] = values[:, half * 128 : half * 128 + 128].astype(F32)

    for side, (target, offset, picks, tile_col) in enumerate(
        ((left, 0, (0, 1), 0), (right, 48, (14, 15), 15))
    ):
        for image, source in enumerate((merged, grad_two)):
            for row in range(2):
                place = image * two + row * WIDE + offset
                keep(row, top[place : place + 16, :])
                keep(34 + row, bottom[place : place + 16, :])
            for row in range(ROWS):
                place = row * WIDE + offset
                keep(row + 2, source[place : place + 16, :])
            for col in range(2):
                strip = (image * 2 + col) * STRIP
                for half in range(2):
                    target[strip : strip + STRIP, half * 128 : half * 128 + 128] = tall[
                        half, pl.ds(picks[col], STRIP, stride=16), :
                    ].astype(BF)
        masks[...] = jnp.zeros((STRIP, F), F32)
        above = top[2 * two : 2 * two + 16, :].astype(F32)
        below = bottom[2 * two : 2 * two + 16, :].astype(F32)
        masks[0:2, :] = jnp.broadcast_to(above[tile_col : tile_col + 1, :], (2, F))
        masks[34:36, :] = jnp.broadcast_to(below[tile_col : tile_col + 1, :], (2, F))
        for tile_row in range(8):
            at = tile_row * 16 + tile_col
            masks[2 + 4 * tile_row : 6 + 4 * tile_row, :] = jnp.broadcast_to(mask_rows[at : at + 1, :], (4, F))
        target[4 * STRIP : 5 * STRIP, :] = masks[...].astype(BF)


def shifted_store(target, at, value, plain, before, after):
    row = iota((WIDE, F), 0)
    target[pl.ds(at, WIDE), 0:F] = jnp.where(row == 0, before, pltpu.roll(value, 1, 0)).astype(BF)
    target[pl.ds(at, WIDE), F : 2 * F] = plain
    target[pl.ds(at, WIDE), 2 * F : 3 * F] = jnp.where(
        row == WIDE - 1, after, pltpu.roll(value, WIDE - 1, 0)
    ).astype(BF)


def conv(shifted, start, count, weight):
    lhs = jnp.concatenate([shifted[pl.ds(start + ky * WIDE, count), :] for ky in range(3)], axis=1)
    return dot(lhs, weight[...])


def main_kernel(
    slots, merged, grad_two, top, bottom, left, right, from_left, from_right, mask_rows,
    fwd_one, fwd_two, bwd_one, bwd_two,
    output, low_grad, send,
    merged_shift, hidden_shift, grad_shift, pre_shift, strips, edge, mask_wide, pre, grad_hidden,
    pair, tiles, slot_rows, folded, count,
):
    two = 2 * WIDE
    spread = one_hot((iota((WIDE, 16), 0) >> 2) == iota((WIDE, 16), 1))
    mask_wide[0:WIDE, :] = dot(spread, top[2 * two : 2 * two + 16, :])
    mask_wide[9 * WIDE : 10 * WIDE, :] = dot(spread, bottom[2 * two : 2 * two + 16, :])
    for tile_row in range(8):
        mask_wide[(tile_row + 1) * WIDE : (tile_row + 2) * WIDE, :] = dot(
            spread, mask_rows[tile_row * 16 : tile_row * 16 + 16, :].astype(BF)
        )
    strip_pre = []
    for image, (source, target, weight) in enumerate(
        ((merged, merged_shift, fwd_one), (grad_two, grad_shift, bwd_two))
    ):
        first = image * 2 * STRIP
        columns = (
            from_left[first : first + STRIP, :],
            from_left[first + STRIP : first + 2 * STRIP, :],
            left[first : first + STRIP, :],
            right[first + STRIP : first + 2 * STRIP, :],
            from_right[first : first + STRIP, :],
            from_right[first + STRIP : first + 2 * STRIP, :],
        )
        for index, column in enumerate(columns):
            strips[index * STRIP : (index + 1) * STRIP, :] = column.astype(F32)
        for row in range(2):
            at = image * two + row * WIDE
            for halo, place in ((top, row), (bottom, 34 + row)):
                plain = halo[at : at + WIDE, :]
                shifted_store(
                    target, place * WIDE, plain.astype(F32), plain,
                    strips[STRIP + place : STRIP + place + 1, :],
                    strips[4 * STRIP + place : 4 * STRIP + place + 1, :],
                )

        def shift_row(row, _, source=source, target=target):
            plain = source[pl.ds(pl.multiple_of(row * WIDE, WIDE), WIDE), :]
            shifted_store(
                target, pl.multiple_of((row + 2) * WIDE, WIDE), plain.astype(F32), plain,
                strips[pl.ds(STRIP + 2 + row, 1), :],
                strips[pl.ds(4 * STRIP + 2 + row, 1), :],
            )
            return 0

        lax.fori_loop(0, ROWS, shift_row, 0)
        parts = []
        for ky in range(3):
            for kx in range(3):
                parts.append(
                    jnp.concatenate(
                        [
                            strips[kx * STRIP + ky : kx * STRIP + ky + 40, :],
                            strips[(kx + 3) * STRIP + ky : (kx + 3) * STRIP + ky + 40, :],
                        ],
                        axis=0,
                    ).astype(BF)
                )
        strip_pre.append(dot(jnp.concatenate(parts, axis=1), weight[...]))
    strips[0:STRIP, :] = from_left[4 * STRIP : 5 * STRIP, :].astype(F32)
    strips[STRIP : 2 * STRIP, :] = from_right[4 * STRIP : 5 * STRIP, :].astype(F32)
    strip_mask = jnp.concatenate([strips[1:41, :], strips[STRIP + 1 : STRIP + 41, :]], axis=0)
    sigma = jax.nn.sigmoid(strip_pre[0])
    edge[0:80, :] = (strip_pre[0] * sigma * strip_mask).astype(BF).astype(F32)
    edge[80:160, :] = (
        (strip_pre[1] * (sigma * (1.0 + strip_pre[0] * (1.0 - sigma))) * strip_mask).astype(BF).astype(F32)
    )

    def first_convs(step, _):
        at = pl.multiple_of(step * 544, 16)
        pre[pl.ds(at, 544), :] = conv(merged_shift, at, 544, fwd_one)
        grad_hidden[pl.ds(at, 544), :] = conv(grad_shift, at, 544, bwd_two)
        return 0

    lax.fori_loop(0, 4, first_convs, 0)

    def activate(row, _):
        at = pl.multiple_of(row * WIDE, WIDE)
        mask = mask_wide[pl.ds(pl.multiple_of(((row + 3) >> 2) * WIDE, WIDE), WIDE), :]
        value = pre[pl.ds(at, WIDE), :]
        sigma = jax.nn.sigmoid(value)
        hidden = value * sigma * mask
        slope = sigma * (1.0 + value * (1.0 - sigma))
        grad_value = grad_hidden[pl.ds(at, WIDE), :] * slope * mask
        shifted_store(
            hidden_shift, at, hidden, hidden.astype(BF), edge[pl.ds(row, 1), :], edge[pl.ds(40 + row, 1), :]
        )
        shifted_store(
            pre_shift, at, grad_value, grad_value.astype(BF),
            edge[pl.ds(80 + row, 1), :], edge[pl.ds(120 + row, 1), :],
        )
        return 0

    lax.fori_loop(0, ROWS + 2, activate, 0)
    order = iota((F, F), 0)
    tile_order = one_hot(
        iota((F, F), 1) == (((order >> 2) & 3) * WIDE + (order >> 4) * 4 + (order & 3))
    )

    def second_convs(step, _):
        at = pl.multiple_of(step * 512, 512)
        masks = []
        for tile_row in range(2):
            mask = mask_wide[pl.ds(pl.multiple_of((step * 2 + tile_row + 1) * WIDE, WIDE), WIDE), :]
            masks.append(jnp.concatenate([mask] * 4, axis=0))
        mask = jnp.concatenate(masks, axis=0)
        output[pl.ds(at, 512), :] = (conv(hidden_shift, at, 512, fwd_two) * mask).astype(BF)
        grad_merged = conv(pre_shift, at, 512, bwd_one) * mask
        rounded = grad_merged.astype(BF)
        for tile_row in range(2):
            tiles[pl.ds(at + tile_row * F, F), :] = dot(
                tile_order, rounded[tile_row * F : (tile_row + 1) * F, :]
            ).astype(BF)
        for row in range(4):
            both = grad_merged[row * two : row * two + WIDE, :] + grad_merged[row * two + WIDE : row * two + two, :]
            for half in range(2):
                pair[half, row * WIDE : (row + 1) * WIDE, :] = both[:, half * 128 : half * 128 + 128]
        for half in range(2):
            low_grad[pl.ds(pl.multiple_of(step * 128, 128), 128), half * 128 : half * 128 + 128] = (
                pair[half, pl.ds(0, 128, stride=2), :] + pair[half, pl.ds(1, 128, stride=2), :]
            ).astype(BF)
        return 0

    lax.fori_loop(0, 4, second_convs, 0)

    def clear(index, _):
        count[index] = 0
        return 0

    lax.fori_loop(0, 128, clear, 0)
    slot_rows[...] = jnp.full((128, 128), -1.0, F32)
    lane = iota((1, 128), 1)

    def pack(tile, _):
        flat = slots[tile >> 4, tile & 15]
        owner = flat >> 7
        used = count[owner]
        count[owner] = used + 1
        send[owner, pl.ds(pl.multiple_of(used * 16, 16), 16), :] = tiles[
            pl.ds(pl.multiple_of(tile * 16, 16), 16), :
        ]
        local = (flat & 127).astype(F32)
        slot_rows[pl.ds(owner, 1), :] = jnp.where(lane == used, local, slot_rows[pl.ds(owner, 1), :])
        return 0

    lax.fori_loop(0, 128, pack, 0)

    across = iota((F, F), 0)
    along = iota((F, F), 1)
    unweave = one_hot(((along & 7) * 32 + (along >> 3)) == across)
    perms = [one_hot(along == permuted_index(across, elem)) for elem in range(G)]
    back = jnp.concatenate(perms, axis=0)
    for index, (values, grads, skip) in enumerate(
        (
            (merged_shift, pre_shift[WIDE : 33 * WIDE, F : 2 * F], WIDE),
            (hidden_shift, grad_two[...], 0),
        )
    ):
        turned = dot_nt(unweave, grads).astype(BF)
        full = []
        for ky in range(3):
            start = skip + ky * WIDE
            full.append(dot(turned, values[start : start + ROWS * WIDE, :]).astype(BF))
        pieces = []
        for elem in range(G):
            of_cell = {source_cell(elem, pos): pos for pos in range(9)}
            rows = []
            for cell in range(9):
                pos = of_cell[cell]
                kx = pos % 3
                rows.append(full[pos // 3][elem * 32 : elem * 32 + 32, kx * F : (kx + 1) * F])
            pieces.append(jnp.concatenate(rows, axis=0))
        folded[index * 288 : (index + 1) * 288, :] = dot(jnp.concatenate(pieces, axis=1), back)
    folded[576:592, :] = jnp.zeros((16, F), F32)
    for part in range(128):
        start, lanes = 9 * (part % 64), (part // 64) * 128
        send[part, 32:40, 0:128] = folded[start : start + 8, lanes : lanes + 128].astype(BF)
        tail = jnp.concatenate(
            [
                folded[start + 8 : start + 9, lanes : lanes + 128],
                slot_rows[part : part + 1, :],
                jnp.zeros((6, 128), F32),
            ],
            axis=0,
        )
        send[part, 32:40, 128:256] = tail.astype(BF)


def sum_kernel(got, message, slots, gathered):
    total = jnp.zeros((8, F), F32)
    for part in range(128):
        terms = got[part, 32:40, :].astype(F32)
        total = total + terms
        gathered[part : part + 1, :] = terms[1:2, 128:256]
    rounded = jnp.concatenate([total[:, 0:128], total[:, 128:256]], axis=0).astype(BF)
    for part in range(128):
        message[part, :, :] = rounded
    slots[...] = gathered[...].T[0:8, :].astype(jnp.int32)


def place_kernel(slots, got, skip_grad):
    def put(index, _):
        for which in range(2):
            slot = slots[which, index]

            @pl.when(slot >= 0)
            def _():
                skip_grad[pl.ds(pl.multiple_of(slot * 16, 16), 16), :] = got[
                    index, which * 16 : which * 16 + 16, :
                ]

        return 0

    lax.fori_loop(0, 128, put, 0)


def finish_kernel(scale, sums, one, two, folded):
    for part in range(128):
        start, lanes = 9 * (part % 64), (part // 64) * 128
        folded[start : start + 16, lanes : lanes + 128] = sums[part, :, :].astype(F32) * scale
    one[...] = folded[0:288, :]
    two[...] = folded[288:576, :]


def shift(values, axis, step):
    size = lax.axis_size(axis)
    if step > 0:
        pairs = [(i, i + 1) for i in range(size - 1)]
    else:
        pairs = [(i + 1, i) for i in range(size - 1)]
    return lax.ppermute(values, axis, pairs)


def on_device(low_feats, skip_feats, tissue_mask, owner_slot, filter_one, filter_two, out_grad):
    everyone = ("rows", "cols")
    height, breadth, features = skip_feats.shape
    pixels = height * breadth
    mask_rows = jnp.broadcast_to(tissue_mask.astype(F32).reshape(128, 1), (128, F))
    merged, grad_two, up, down = call(
        prep_kernel,
        [shape((pixels, F)), shape((pixels, F)), shape((272, F)), shape((272, F))],
        4, name="prep",
    )(
        low_feats.reshape(-1, F), skip_feats.reshape(pixels, F), out_grad.reshape(pixels, F), mask_rows
    )
    bottom = shift(up, "rows", -1)
    top = shift(down, "rows", 1)
    bases = [f.transpose(1, 2, 0, 3).reshape(288, F) for f in (filter_one, filter_two)]
    fwd_one, fwd_two, bwd_one, bwd_two = call(
        expand_kernel, [shape((9 * F, F))] * 4, 2, name="expand"
    )(*bases)
    left, right = call(
        edge_kernel,
        [shape((5 * STRIP, F))] * 2,
        5, [pltpu.VMEM((2, 48 * 16, 128), F32), pltpu.VMEM((STRIP, F), F32)], name="edge",
    )(merged, grad_two, top, bottom, mask_rows)
    from_right = shift(left, "cols", -1)
    from_left = shift(right, "cols", 1)
    output, low_grad, send = call(
        main_kernel,
        [shape((pixels, F)), shape((pixels // 4, F)), shape((128, 40, F))],
        14,
        [
            pltpu.VMEM((36 * WIDE, 3 * F), BF), pltpu.VMEM((34 * WIDE, 3 * F), BF),
            pltpu.VMEM((36 * WIDE, 3 * F), BF), pltpu.VMEM((34 * WIDE, 3 * F), BF),
            pltpu.VMEM((6 * STRIP, F), F32), pltpu.VMEM((160, F), F32), pltpu.VMEM((10 * WIDE, F), F32),
            pltpu.VMEM((34 * WIDE, F), F32), pltpu.VMEM((34 * WIDE, F), F32),
            pltpu.VMEM((2, 4 * WIDE, 128), F32), pltpu.VMEM((pixels, F), BF),
            pltpu.VMEM((128, 128), F32), pltpu.VMEM((592, F), F32), pltpu.SMEM((128,), jnp.int32),
        ],
        specs=[SMEM] + [VMEM] * 13, flops=16 << 30, name="convs",
    )(
        owner_slot, merged, grad_two, top, bottom, left, right, from_left, from_right, mask_rows,
        fwd_one, fwd_two, bwd_one, bwd_two,
    )
    got = lax.all_to_all(send, everyone, 0, 0, tiled=True)
    sums, slots = call(
        sum_kernel, [shape((128, 16, 128)), shape((8, 128), jnp.int32)], 1,
        [pltpu.VMEM((128, 128), F32)], name="sums",
    )(got)
    got_sums = lax.all_to_all(sums, everyone, 0, 0, tiled=True)
    skip_grad = call(place_kernel, shape((2048, F)), 2, specs=[SMEM, VMEM], name="place")(slots, got)
    scale = 1.0 / math.sqrt(pixels * lax.axis_size("rows") * lax.axis_size("cols"))
    one, two = call(
        functools.partial(finish_kernel, scale),
        [shape((288, F), F32), shape((288, F), F32)], 1, [pltpu.VMEM((592, F), F32)], name="finish",
    )(got_sums)
    return (
        output.reshape(height, breadth, F),
        skip_grad.reshape(128, 4, 4, F),
        low_grad.reshape(height // 2, breadth // 2, F),
        one.reshape(3, 3, 32, F).transpose(2, 0, 1, 3),
        two.reshape(3, 3, 32, F).transpose(2, 0, 1, 3),
    )


def solution(mesh):
    placed = (
        P("rows", "cols", None),
        P("rows", "cols", None),
        P("rows", "cols"),
        P("rows", "cols"),
        P(),
        P(),
        P("rows", "cols", None),
    )
    return jax.shard_map(
        on_device,
        mesh=mesh,
        in_specs=placed,
        out_specs=(
            P("rows", "cols", None),
            P(("rows", "cols"), None, None, None),
            P("rows", "cols", None),
            P(),
            P(),
        ),
        check_vma=False,
    )
```

```python
import functools
import math

import jax
import jax.numpy as jnp
import numpy as np
from jax import lax
from jax.experimental import pallas as pl
from jax.experimental.pallas import tpu as pltpu
from jax.sharding import PartitionSpec as P

G = 8
F = 256
ROWS = 32
WIDE = 64
STRIP = 48
MASK_ROWS = 16
BF = jnp.bfloat16
F32 = jnp.float32
VMEM = pl.BlockSpec(memory_space=pltpu.VMEM)
SMEM = pl.BlockSpec(memory_space=pltpu.SMEM)
HBM = pl.BlockSpec(memory_space=pltpu.HBM)


def inverse_of(element):
    return (4 - element % 4) % 4 if element < 4 else element


def product(first, second):
    mirror = (first // 4 + second // 4) % 2
    turns = (first % 4 + (1 - 2 * (first // 4)) * (second % 4)) % 4
    return mirror * 4 + turns


def act(element, row, col):
    if element // 4:
        col = -col
    for _ in range(element % 4):
        row, col = -col, row
    return row, col


def source_cell(elem, pos):
    row, col = act(inverse_of(elem), pos // 3 - 1, pos % 3 - 1)
    return (row + 1) * 3 + col + 1


def iota(shape, dim):
    return lax.broadcasted_iota(jnp.int32, shape, dim)


def one_hot(cond):
    return jnp.where(cond, 1.0, 0.0).astype(BF)


def permuted_index(index, elem):
    inverse = inverse_of(elem)
    mirror, turns = inverse // 4, inverse % 4
    second = index & 7
    new_mirror = (second >> 2) ^ mirror
    spin = second & 3
    new_turns = (turns + (-spin if mirror else spin)) & 3
    return (index & ~7) | (new_mirror << 2) | new_turns


def dot(lhs, rhs):
    return jnp.dot(lhs, rhs, preferred_element_type=F32)


def dot_nt(lhs, rhs):
    return lax.dot_general(lhs, rhs, (((1,), (1,)), ((), ())), preferred_element_type=F32)


def call(
    kernel, out_shape, n_in, scratch=(), specs=None, outs=None, flops=1 << 30, limit=24 << 20, name=None
):
    return pl.pallas_call(
        kernel,
        out_shape=out_shape,
        in_specs=specs or [VMEM] * n_in,
        out_specs=outs or jax.tree.map(lambda _: VMEM, out_shape),
        scratch_shapes=list(scratch),
        compiler_params=pltpu.CompilerParams(vmem_limit_bytes=limit),
        cost_estimate=pl.CostEstimate(flops=flops, bytes_accessed=4 << 20, transcendentals=0),
        name=name,
    )


def shape(dims, dtype=BF):
    return jax.ShapeDtypeStruct(dims, dtype)


def far(dims):
    return pltpu.HBM(dims, BF)


def kept(values):
    return pltpu.with_memory_space_constraint(values, pltpu.HBM)


def start_copies(pairs, semaphores):
    copies = [pltpu.make_async_copy(src, dst, semaphores.at[i]) for i, (src, dst) in enumerate(pairs)]
    for copy in copies:
        copy.start()
    return copies


def prep_kernel(
    low_in, skip_in, grad_in, tissue, merged, grad_two, up, down, mask_rows, low, skip, grad, semaphores
):
    pairs = []
    for part in range(4):
        fine, coarse = pl.ds(part * 512, 512), pl.ds(part * 128, 128)
        pairs.append((low_in.at[coarse], low.at[coarse]))
        pairs.append((skip_in.at[fine], skip.at[fine]))
        pairs.append((grad_in.at[fine], grad.at[fine]))
    copies = start_copies(pairs, semaphores)
    spread = one_hot((iota((WIDE, 16), 0) >> 2) == iota((WIDE, 16), 1))
    twice = one_hot((iota((WIDE, 32), 0) >> 1) == iota((WIDE, 32), 1))
    same = iota((16, 16), 0) == iota((16, 16), 1)
    for tile_row in range(8):
        values = jnp.broadcast_to(tissue[tile_row : tile_row + 1, :].astype(F32), (16, 16))
        column = jnp.sum(jnp.where(same, values, 0.0), axis=1, keepdims=True)
        mask_rows[tile_row * 16 : tile_row * 16 + 16, :] = jnp.broadcast_to(column, (16, F))
    for tile_row in range(8):
        if tile_row % 2 == 0:
            for copy in copies[tile_row // 2 * 3 : tile_row // 2 * 3 + 3]:
                copy.wait()
        mask = dot(spread, mask_rows[tile_row * 16 : tile_row * 16 + 16, :].astype(BF))
        for half in range(2):
            low_row = tile_row * 2 + half
            coarse = dot(twice, low[low_row * 32 : low_row * 32 + 32, :])
            for sub in range(2):
                here = pl.ds((low_row * 2 + sub) * WIDE, WIDE)
                merged[here, :] = ((coarse + skip[here, :].astype(F32)) * mask).astype(BF)
                grad_two[here, :] = (grad[here, :].astype(F32) * mask).astype(BF)
    two = 2 * WIDE
    up[0:two, :] = merged[0:two, :]
    up[two : 2 * two, :] = grad_two[0:two, :]
    up[2 * two : 2 * two + 16, :] = mask_rows[0:16, :].astype(BF)
    last = ROWS * WIDE - two
    down[0:two, :] = merged[last : last + two, :]
    down[two : 2 * two, :] = grad_two[last : last + two, :]
    down[2 * two : 2 * two + 16, :] = mask_rows[112:128, :].astype(BF)


def expand_kernel(
    slots, filter_one, filter_two, fwd_one, bwd_two, fwd_two_out, bwd_one_out, places, slot_rows,
    fwd_two, bwd_one, semaphores,
):
    flat = jnp.concatenate([slots[row : row + 1, :] for row in range(8)], axis=1)
    owner, local = flat >> 7, (flat & 127).astype(F32)
    tile = iota((128, 128), 1)
    match = owner == iota((128, 128), 0)
    index = tile.astype(F32)
    first = jnp.min(jnp.where(match, index, 1000.0), axis=1, keepdims=True)
    second = match & (index > first)
    used = jnp.sum(jnp.where(second, 1.0, 0.0), axis=0, keepdims=True)
    places[...] = jnp.broadcast_to(owner * 2 + used.astype(jnp.int32), (8, 128))
    slot_one = jnp.sum(jnp.where(match & (index == first), local + 1.0, 0.0), axis=1, keepdims=True)
    slot_two = jnp.sum(jnp.where(second, local + 1.0, 0.0), axis=1, keepdims=True)
    slot_rows[...] = jnp.where(tile == 0, slot_one, jnp.where(tile == 1, slot_two, 0.0)) - 1.0
    across = iota((F, F), 0)
    along = iota((F, F), 1)
    weave = one_hot(((across & 7) * 32 + (across >> 3)) == along)
    perms = [one_hot(across == permuted_index(along, elem)) for elem in range(G)]
    for base, fwd, bwd in ((filter_one, fwd_one, bwd_one), (filter_two, fwd_two, bwd_two)):
        turned = [dot(base[...], perms[elem]).astype(BF) for elem in range(G)]
        for pos in range(9):
            rows = []
            for elem in range(G):
                cell = source_cell(elem, pos)
                rows.append(turned[elem][cell * 32 : cell * 32 + 32, :])
            gathered = jnp.concatenate(rows, axis=0)
            woven = dot(weave, gathered)
            bwd[(8 - pos) * F : (9 - pos) * F, :] = woven.astype(BF)
            fwd[pos * F : (pos + 1) * F, :] = woven.T.astype(BF)
    for copy in start_copies([(fwd_two, fwd_two_out), (bwd_one, bwd_one_out)], semaphores):
        copy.wait()


def edge_kernel(merged, grad_two, above_in, below_in, mask_rows, left, right, top, bottom, tall, masks):
    two = 2 * WIDE
    at_top = lax.axis_index("rows") == 0
    at_bottom = lax.axis_index("rows") == lax.axis_size("rows") - 1
    top[...] = jnp.where(at_top, jnp.zeros_like(above_in), above_in[...])
    bottom[...] = jnp.where(at_bottom, jnp.zeros_like(below_in), below_in[...])
    tall[:, 36 * 16 : 48 * 16, :] = jnp.zeros((2, 12 * 16, 128), F32)

    def keep(row, values):
        for half in range(2):
            tall[half, row * 16 : row * 16 + 16, :] = values[:, half * 128 : half * 128 + 128].astype(F32)

    for side, (target, offset, picks, tile_col) in enumerate(
        ((left, 0, (0, 1), 0), (right, 48, (14, 15), 15))
    ):
        for image, source in enumerate((merged, grad_two)):
            for row in range(2):
                place = image * two + row * WIDE + offset
                keep(row, top[place : place + 16, :])
                keep(34 + row, bottom[place : place + 16, :])
            for row in range(ROWS):
                place = row * WIDE + offset
                keep(row + 2, source[place : place + 16, :])
            for col in range(2):
                strip = (image * 2 + col) * STRIP
                for half in range(2):
                    target[strip : strip + STRIP, half * 128 : half * 128 + 128] = tall[
                        half, pl.ds(picks[col], STRIP, stride=16), :
                    ].astype(BF)
        masks[...] = jnp.zeros((STRIP, F), F32)
        above = top[2 * two : 2 * two + 16, :].astype(F32)
        below = bottom[2 * two : 2 * two + 16, :].astype(F32)
        masks[0:2, :] = jnp.broadcast_to(above[tile_col : tile_col + 1, :], (2, F))
        masks[34:36, :] = jnp.broadcast_to(below[tile_col : tile_col + 1, :], (2, F))
        for tile_row in range(8):
            at = tile_row * 16 + tile_col
            masks[2 + 4 * tile_row : 6 + 4 * tile_row, :] = jnp.broadcast_to(mask_rows[at : at + 1, :], (4, F))
        target[4 * STRIP : 5 * STRIP, :] = masks[...].astype(BF)


def shifted_store(target, at, value, plain, before, after):
    row = iota((WIDE, F), 0)
    target[pl.ds(at, WIDE), 0:F] = jnp.where(row == 0, before, pltpu.roll(value, 1, 0)).astype(BF)
    target[pl.ds(at, WIDE), F : 2 * F] = plain
    target[pl.ds(at, WIDE), 2 * F : 3 * F] = jnp.where(
        row == WIDE - 1, after, pltpu.roll(value, WIDE - 1, 0)
    ).astype(BF)


def conv(shifted, start, count, weight):
    lhs = jnp.concatenate([shifted[pl.ds(start + ky * WIDE, count), :] for ky in range(3)], axis=1)
    return dot(lhs, weight[...])


def first_kernel(
    merged, grad_two, top, bottom, left, right, from_left, from_right, mask_rows, fwd_one, bwd_two,
    hidden_out, pre_out, edge, message,
    hidden_shift, pre_shift, mask_wide, merged_shift, grad_shift, strips, pre, grad_hidden, folded, semaphores,
):
    at_left = lax.axis_index("cols") == 0
    at_right = lax.axis_index("cols") == lax.axis_size("cols") - 1
    zero = jnp.zeros((STRIP, F), F32)

    def left_strip(index):
        return jnp.where(at_left, zero, from_left[index * STRIP : (index + 1) * STRIP, :].astype(F32))

    def right_strip(index):
        return jnp.where(at_right, zero, from_right[index * STRIP : (index + 1) * STRIP, :].astype(F32))

    two = 2 * WIDE
    spread = one_hot((iota((WIDE, 16), 0) >> 2) == iota((WIDE, 16), 1))
    mask_wide[0:WIDE, :] = dot(spread, top[2 * two : 2 * two + 16, :])
    mask_wide[9 * WIDE : 10 * WIDE, :] = dot(spread, bottom[2 * two : 2 * two + 16, :])
    for tile_row in range(8):
        mask_wide[(tile_row + 1) * WIDE : (tile_row + 2) * WIDE, :] = dot(
            spread, mask_rows[tile_row * 16 : tile_row * 16 + 16, :].astype(BF)
        )
    strip_pre = []
    for image, (source, target, weight) in enumerate(
        ((merged, merged_shift, fwd_one), (grad_two, grad_shift, bwd_two))
    ):
        first = image * 2
        columns = (
            left_strip(first),
            left_strip(first + 1),
            left[first * STRIP : (first + 1) * STRIP, :].astype(F32),
            right[(first + 1) * STRIP : (first + 2) * STRIP, :].astype(F32),
            right_strip(first),
            right_strip(first + 1),
        )
        for index, column in enumerate(columns):
            strips[index * STRIP : (index + 1) * STRIP, :] = column
        for row in range(2):
            at = image * two + row * WIDE
            for halo, place in ((top, row), (bottom, 34 + row)):
                plain = halo[at : at + WIDE, :]
                shifted_store(
                    target, place * WIDE, plain.astype(F32), plain,
                    strips[STRIP + place : STRIP + place + 1, :],
                    strips[4 * STRIP + place : 4 * STRIP + place + 1, :],
                )

        def shift_row(row, _, source=source, target=target):
            plain = source[pl.ds(pl.multiple_of(row * WIDE, WIDE), WIDE), :]
            shifted_store(
                target, pl.multiple_of((row + 2) * WIDE, WIDE), plain.astype(F32), plain,
                strips[pl.ds(STRIP + 2 + row, 1), :],
                strips[pl.ds(4 * STRIP + 2 + row, 1), :],
            )
            return 0

        lax.fori_loop(0, ROWS, shift_row, 0)
        parts = []
        for ky in range(3):
            for kx in range(3):
                parts.append(
                    jnp.concatenate(
                        [
                            strips[kx * STRIP + ky : kx * STRIP + ky + 40, :],
                            strips[(kx + 3) * STRIP + ky : (kx + 3) * STRIP + ky + 40, :],
                        ],
                        axis=0,
                    ).astype(BF)
                )
        strip_pre.append(dot(jnp.concatenate(parts, axis=1), weight[...]))
    strips[0:STRIP, :] = left_strip(4)
    strips[STRIP : 2 * STRIP, :] = right_strip(4)
    strip_mask = jnp.concatenate([strips[1:41, :], strips[STRIP + 1 : STRIP + 41, :]], axis=0)
    sigma = jax.nn.sigmoid(strip_pre[0])
    edge[0:80, :] = (strip_pre[0] * sigma * strip_mask).astype(BF).astype(F32)
    edge[80:160, :] = (
        (strip_pre[1] * (sigma * (1.0 + strip_pre[0] * (1.0 - sigma))) * strip_mask).astype(BF).astype(F32)
    )

    def first_convs(step, _):
        at = pl.multiple_of(step * 544, 16)
        pre[pl.ds(at, 544), :] = conv(merged_shift, at, 544, fwd_one)
        grad_hidden[pl.ds(at, 544), :] = conv(grad_shift, at, 544, bwd_two)
        return 0

    lax.fori_loop(0, 4, first_convs, 0)

    def activate(row, _):
        at = pl.multiple_of(row * WIDE, WIDE)
        mask = mask_wide[pl.ds(pl.multiple_of(((row + 3) >> 2) * WIDE, WIDE), WIDE), :]
        value = pre[pl.ds(at, WIDE), :]
        sigma = jax.nn.sigmoid(value)
        hidden = value * sigma * mask
        slope = sigma * (1.0 + value * (1.0 - sigma))
        grad_value = grad_hidden[pl.ds(at, WIDE), :] * slope * mask
        shifted_store(
            hidden_shift, at, hidden, hidden.astype(BF), edge[pl.ds(row, 1), :], edge[pl.ds(40 + row, 1), :]
        )
        shifted_store(
            pre_shift, at, grad_value, grad_value.astype(BF),
            edge[pl.ds(80 + row, 1), :], edge[pl.ds(120 + row, 1), :],
        )
        return 0

    lax.fori_loop(0, ROWS + 2, activate, 0)
    copies = start_copies(
        [(hidden_shift.at[:, F : 2 * F], hidden_out), (pre_shift.at[:, F : 2 * F], pre_out)], semaphores
    )
    across = iota((F, F), 0)
    along = iota((F, F), 1)
    unweave = one_hot(((along & 7) * 32 + (along >> 3)) == across)
    perms = [one_hot(along == permuted_index(across, elem)) for elem in range(G)]
    back = jnp.concatenate(perms, axis=0)
    for index, (values, grads, skip) in enumerate(
        (
            (merged_shift, pre_shift[WIDE : 33 * WIDE, F : 2 * F], WIDE),
            (hidden_shift, grad_two[...], 0),
        )
    ):
        turned = dot_nt(unweave, grads).astype(BF)
        full = []
        for ky in range(3):
            start = skip + ky * WIDE
            full.append(dot(turned, values[start : start + ROWS * WIDE, :]).astype(BF))
        pieces = []
        for elem in range(G):
            of_cell = {source_cell(elem, pos): pos for pos in range(9)}
            rows = []
            for cell in range(9):
                pos = of_cell[cell]
                kx = pos % 3
                rows.append(full[pos // 3][elem * 32 : elem * 32 + 32, kx * F : (kx + 1) * F])
            pieces.append(jnp.concatenate(rows, axis=0))
        folded[index * 288 : (index + 1) * 288, :] = dot(jnp.concatenate(pieces, axis=1), back)
    folded[576:592, :] = jnp.zeros((16, F), F32)
    for part in range(128):
        start, lanes = 9 * (part % 64), (part // 64) * 128
        message[part, :, :] = folded[start : start + 16, lanes : lanes + 128].astype(BF)
    for copy in copies:
        copy.wait()


def wide_mask(mask_rows, step):
    spread = one_hot((iota((WIDE, 16), 0) >> 2) == iota((WIDE, 16), 1))
    parts = []
    for tile_row in range(2):
        at = pl.multiple_of((step * 2 + tile_row) * 16, 16)
        parts.extend([dot(spread, mask_rows[pl.ds(at, 16), :].astype(BF))] * 4)
    return jnp.concatenate(parts, axis=0)


def load_shifted(values, weight, edges, base, plain, held, shifted, semaphores):
    cuts = (0, 640, 1152, 1664, 2176)
    pairs = [(weight.at[pl.ds(part * 768, 768)], held.at[pl.ds(part * 768, 768)]) for part in range(3)]
    for first, last in zip(cuts[:-1], cuts[1:]):
        pairs.append((values.at[pl.ds(first, last - first)], plain.at[pl.ds(first, last - first)]))
    copies = start_copies(pairs, semaphores)

    def row_of(row, _):
        at = pl.multiple_of(row * WIDE, WIDE)
        value = plain[pl.ds(at, WIDE), :]
        shifted_store(
            shifted, at, value.astype(F32), value,
            edges[pl.ds(base + row, 1), :], edges[pl.ds(base + 40 + row, 1), :],
        )
        return 0

    for part in range(4):
        copies[3 + part].wait()
        lax.fori_loop(cuts[part] // WIDE, cuts[part + 1] // WIDE, row_of, 0)
    for copy in copies[:3]:
        copy.wait()


def backward_kernel(
    pre_in, weight_in, edges, mask_rows, tiles, low_grad, pair, plain, bwd_one, pre_shift, semaphores
):
    two = 2 * WIDE
    load_shifted(pre_in, weight_in, edges, 80, plain, bwd_one, pre_shift, semaphores)
    order = iota((F, F), 0)
    tile_order = one_hot(
        iota((F, F), 1) == (((order >> 2) & 3) * WIDE + (order >> 4) * 4 + (order & 3))
    )

    def body(step, _):
        at = pl.multiple_of(step * 512, 512)
        grad_merged = conv(pre_shift, at, 512, bwd_one) * wide_mask(mask_rows, step)
        rounded = grad_merged.astype(BF)
        for tile_row in range(2):
            tiles[pl.ds(at + tile_row * F, F), :] = dot(
                tile_order, rounded[tile_row * F : (tile_row + 1) * F, :]
            ).astype(BF)
        for row in range(4):
            both = grad_merged[row * two : row * two + WIDE, :] + grad_merged[row * two + WIDE : row * two + two, :]
            for half in range(2):
                pair[half, row * WIDE : (row + 1) * WIDE, :] = both[:, half * 128 : half * 128 + 128]
        for half in range(2):
            low_grad[pl.ds(pl.multiple_of(step * 128, 128), 128), half * 128 : half * 128 + 128] = (
                pair[half, pl.ds(0, 128, stride=2), :] + pair[half, pl.ds(1, 128, stride=2), :]
            ).astype(BF)
        return 0

    lax.fori_loop(0, 4, body, 0)


def forward_kernel(
    hidden_in, weight_in, edges, mask_rows, output, plain, fwd_two, hidden_shift, semaphores
):
    load_shifted(hidden_in, weight_in, edges, 0, plain, fwd_two, hidden_shift, semaphores)

    def body(step, _):
        at = pl.multiple_of(step * 512, 512)
        output[pl.ds(at, 512), :] = (
            conv(hidden_shift, at, 512, fwd_two) * wide_mask(mask_rows, step)
        ).astype(BF)
        return 0

    lax.fori_loop(0, 4, body, 0)


def pack_kernel(places, tiles, got, slot_rows, send):
    def copy(group, _):
        for sub in range(8):
            tile = group * 8 + sub
            place = places[0, tile]
            send[place >> 1, pl.ds(pl.multiple_of((place & 1) * 16, 16), 16), :] = tiles[
                pl.ds(pl.multiple_of(tile * 16, 16), 16), :
            ]
        return 0

    lax.fori_loop(0, 16, copy, 0)
    total = jnp.zeros((16, 128), F32)
    for part in range(128):
        total = total + got[part, :, :].astype(F32)
    low = total[0:8, :].astype(BF)
    high = jnp.where(iota((8, 128), 0) == 0, total[8:16, :], 0.0)
    for part in range(128):
        send[part, 32:40, 0:128] = low
        send[part, 32:40, 128:256] = jnp.where(
            iota((8, 128), 0) == 1, slot_rows[part : part + 1, :], high
        ).astype(BF)


def place_kernel(scale, got, skip_grad, one, two, gathered, sources, folded, table, semaphore):
    for part in range(128):
        terms = got[part, 32:40, :].astype(F32) * scale
        start, lanes = 9 * (part % 64), (part // 64) * 128
        folded[start : start + 8, lanes : lanes + 128] = terms[:, 0:128]
        folded[start + 8 : start + 9, lanes : lanes + 128] = terms[0:1, 128:256]
        gathered[part : part + 1, :] = terms[1:2, 128:256] / scale
    one[...] = folded[0:288, :]
    two[...] = folded[288:576, :]
    slots = gathered[...].T
    wanted = iota((128, 128), 0).astype(F32)
    index = iota((128, 128), 1).astype(F32)
    source = jnp.zeros((128, 128), F32)
    for which in range(2):
        source = source + jnp.where(slots[which : which + 1, :] == wanted, index * 2.0 + which, 0.0)
    sources[...] = jnp.broadcast_to(jnp.sum(source, axis=1, keepdims=True), (128, 128)).T[0:8, :].astype(jnp.int32)
    copy = pltpu.make_async_copy(sources, table, semaphore)
    copy.start()
    copy.wait()

    def put(group, _):
        for sub in range(8):
            slot = group * 8 + sub
            place = table[0, slot]
            tile = got[place >> 1, pl.ds(pl.multiple_of((place & 1) * 16, 16), 16), :]
            skip_grad[slot] = tile.reshape(4, 4, F)
        return 0

    lax.fori_loop(0, 16, put, 0)


def shift(values, axis, step):
    size = lax.axis_size(axis)
    pairs = [(i, (i + step) % size) for i in range(size)]
    return lax.ppermute(values, axis, pairs)


def on_device(low_feats, skip_feats, tissue_mask, owner_slot, filter_one, filter_two, out_grad):
    everyone = ("rows", "cols")
    height, breadth, features = skip_feats.shape
    pixels = height * breadth
    merged, grad_two, up, down, mask_rows = call(
        prep_kernel,
        [shape((pixels, F)), shape((pixels, F)), shape((272, F)), shape((272, F)), shape((128, F), F32)],
        4,
        [
            pltpu.VMEM((pixels // 4, F), BF), pltpu.VMEM((pixels, F), BF), pltpu.VMEM((pixels, F), BF),
            pltpu.SemaphoreType.DMA((12,)),
        ],
        specs=[HBM, HBM, HBM, VMEM], name="prep",
    )(
        kept(low_feats.reshape(-1, F)), kept(skip_feats.reshape(pixels, F)),
        kept(out_grad.reshape(pixels, F)), tissue_mask,
    )
    below = shift(up, "rows", -1)
    above = shift(down, "rows", 1)
    bases = [f.transpose(1, 2, 0, 3).reshape(288, F) for f in (filter_one, filter_two)]
    weights = shape((9 * F, F))
    fwd_one, bwd_two, fwd_two, bwd_one, places, slot_rows = call(
        expand_kernel,
        [weights] * 2 + [far((9 * F, F))] * 2 + [shape((8, 128), jnp.int32), shape((128, 128), F32)],
        3,
        [pltpu.VMEM((9 * F, F), BF), pltpu.VMEM((9 * F, F), BF), pltpu.SemaphoreType.DMA((2,))],
        outs=[VMEM, VMEM, HBM, HBM, VMEM, VMEM], name="expand",
    )(owner_slot, *bases)
    left, right, top, bottom = call(
        edge_kernel,
        [shape((5 * STRIP, F))] * 2 + [shape((272, F))] * 2,
        5, [pltpu.VMEM((2, 48 * 16, 128), F32), pltpu.VMEM((STRIP, F), F32)], name="edge",
    )(merged, grad_two, above, below, mask_rows)
    from_right = shift(left, "cols", -1)
    from_left = shift(right, "cols", 1)
    hidden, grad_pre, edges, message = call(
        first_kernel,
        [far((34 * WIDE, F)), far((34 * WIDE, F)), shape((160, F), F32), shape((128, 16, 128))],
        11,
        [
            pltpu.VMEM((34 * WIDE, 3 * F), BF), pltpu.VMEM((34 * WIDE, 3 * F), BF),
            pltpu.VMEM((10 * WIDE, F), F32),
            pltpu.VMEM((36 * WIDE, 3 * F), BF), pltpu.VMEM((36 * WIDE, 3 * F), BF),
            pltpu.VMEM((6 * STRIP, F), F32),
            pltpu.VMEM((34 * WIDE, F), F32), pltpu.VMEM((34 * WIDE, F), F32),
            pltpu.VMEM((592, F), F32), pltpu.SemaphoreType.DMA((2,)),
        ],
        outs=[HBM, HBM, VMEM, VMEM], flops=10 << 30, limit=36 << 20, name="first",
    )(merged, grad_two, top, bottom, left, right, from_left, from_right, mask_rows, fwd_one, bwd_two)
    got_terms = lax.all_to_all(message, everyone, 0, 0, tiled=True)
    loading = [
        pltpu.VMEM((34 * WIDE, F), BF), pltpu.VMEM((9 * F, F), BF), pltpu.VMEM((34 * WIDE, 3 * F), BF),
        pltpu.SemaphoreType.DMA((7,)),
    ]
    tiles, low_grad = call(
        backward_kernel, [shape((pixels, F)), shape((pixels // 4, F))], 4,
        [pltpu.VMEM((2, 4 * WIDE, 128), F32)] + loading, specs=[HBM, HBM, VMEM, VMEM],
        flops=3 << 30, name="backward",
    )(kept(grad_pre), kept(bwd_one), edges, mask_rows)
    output = call(
        forward_kernel, shape((pixels, F)), 4, loading, specs=[HBM, HBM, VMEM, VMEM],
        flops=3 << 30, name="forward",
    )(kept(hidden), kept(fwd_two), edges, mask_rows)
    send = call(
        pack_kernel, shape((128, 40, F)), 4, specs=[SMEM, VMEM, VMEM, VMEM], name="pack"
    )(places, tiles, got_terms, slot_rows)
    got = lax.all_to_all(send, everyone, 0, 0, tiled=True)
    scale = 1.0 / math.sqrt(pixels * lax.axis_size("rows") * lax.axis_size("cols"))
    skip_grad, one, two = call(
        functools.partial(place_kernel, scale),
        [shape((128, 4, 4, F)), shape((288, F), F32), shape((288, F), F32)], 1,
        [
            pltpu.VMEM((128, 128), F32), pltpu.VMEM((8, 128), jnp.int32), pltpu.VMEM((592, F), F32),
            pltpu.SMEM((8, 128), jnp.int32), pltpu.SemaphoreType.DMA,
        ],
        name="place",
    )(got)
    return (
        output.reshape(height, breadth, F),
        skip_grad,
        low_grad.reshape(height // 2, breadth // 2, F),
        one.reshape(3, 3, 32, F).transpose(2, 0, 1, 3),
        two.reshape(3, 3, 32, F).transpose(2, 0, 1, 3),
    )


def solution(mesh):
    placed = (
        P("rows", "cols", None),
        P("rows", "cols", None),
        P("rows", "cols"),
        P("rows", "cols"),
        P(),
        P(),
        P("rows", "cols", None),
    )
    return jax.shard_map(
        on_device,
        mesh=mesh,
        in_specs=placed,
        out_specs=(
            P("rows", "cols", None),
            P(("rows", "cols"), None, None, None),
            P("rows", "cols", None),
            P(),
            P(),
        ),
        check_vma=False,
    )
```

```python
import functools
import math

import jax
import jax.numpy as jnp
import numpy as np
from jax import lax
from jax.experimental import pallas as pl
from jax.experimental.pallas import tpu as pltpu
from jax.sharding import PartitionSpec as P

G = 8
F = 256
ROWS = 32
WIDE = 64
STRIP = 48
MASK_ROWS = 16
BF = jnp.bfloat16
F32 = jnp.float32
VMEM = pl.BlockSpec(memory_space=pltpu.VMEM)
SMEM = pl.BlockSpec(memory_space=pltpu.SMEM)
HBM = pl.BlockSpec(memory_space=pltpu.HBM)


def inverse_of(element):
    return (4 - element % 4) % 4 if element < 4 else element


def product(first, second):
    mirror = (first // 4 + second // 4) % 2
    turns = (first % 4 + (1 - 2 * (first // 4)) * (second % 4)) % 4
    return mirror * 4 + turns


def act(element, row, col):
    if element // 4:
        col = -col
    for _ in range(element % 4):
        row, col = -col, row
    return row, col


def source_cell(elem, pos):
    row, col = act(inverse_of(elem), pos // 3 - 1, pos % 3 - 1)
    return (row + 1) * 3 + col + 1


def iota(shape, dim):
    return lax.broadcasted_iota(jnp.int32, shape, dim)


def one_hot(cond):
    return jnp.where(cond, 1.0, 0.0).astype(BF)


def permuted_index(index, elem):
    inverse = inverse_of(elem)
    mirror, turns = inverse // 4, inverse % 4
    second = index & 7
    new_mirror = (second >> 2) ^ mirror
    spin = second & 3
    new_turns = (turns + (-spin if mirror else spin)) & 3
    return (index & ~7) | (new_mirror << 2) | new_turns


def dot(lhs, rhs):
    return jnp.dot(lhs, rhs, preferred_element_type=F32)


def dot_nt(lhs, rhs):
    return lax.dot_general(lhs, rhs, (((1,), (1,)), ((), ())), preferred_element_type=F32)


def call(
    kernel, out_shape, n_in, scratch=(), specs=None, outs=None, flops=1 << 30, limit=24 << 20, name=None
):
    return pl.pallas_call(
        kernel,
        out_shape=out_shape,
        in_specs=specs or [VMEM] * n_in,
        out_specs=outs or jax.tree.map(lambda _: VMEM, out_shape),
        scratch_shapes=list(scratch),
        compiler_params=pltpu.CompilerParams(vmem_limit_bytes=limit),
        cost_estimate=pl.CostEstimate(flops=flops, bytes_accessed=4 << 20, transcendentals=0),
        name=name,
    )


def shape(dims, dtype=BF):
    return jax.ShapeDtypeStruct(dims, dtype)


def far(dims):
    return pltpu.HBM(dims, BF)


def kept(values):
    return pltpu.with_memory_space_constraint(values, pltpu.HBM)


def start_copies(pairs, semaphores):
    copies = [pltpu.make_async_copy(src, dst, semaphores.at[i]) for i, (src, dst) in enumerate(pairs)]
    for copy in copies:
        copy.start()
    return copies


def fill_mask_rows(tissue, mask_rows, tile_rows):
    same = iota((16, 16), 0) == iota((16, 16), 1)
    for tile_row in tile_rows:
        values = jnp.broadcast_to(tissue[tile_row : tile_row + 1, :].astype(F32), (16, 16))
        column = jnp.sum(jnp.where(same, values, 0.0), axis=1, keepdims=True)
        mask_rows[tile_row * 16 : tile_row * 16 + 16, :] = jnp.broadcast_to(column, (16, F))


def masked_rows(tile_row, half, low, skip, grad, mask_rows, low_at, at, merged, grad_two, put):
    spread = one_hot((iota((WIDE, 16), 0) >> 2) == iota((WIDE, 16), 1))
    twice = one_hot((iota((WIDE, 32), 0) >> 1) == iota((WIDE, 32), 1))
    mask = dot(spread, mask_rows[tile_row * 16 : tile_row * 16 + 16, :].astype(BF))
    coarse = dot(twice, low[low_at : low_at + 32, :])
    for sub in range(2):
        here, there = pl.ds(at + sub * WIDE, WIDE), pl.ds(put + sub * WIDE, WIDE)
        merged[there, :] = ((coarse + skip[here, :].astype(F32)) * mask).astype(BF)
        grad_two[there, :] = (grad[here, :].astype(F32) * mask).astype(BF)


def head_kernel(
    low_in, skip_in, grad_in, tissue_in, near, far_side, low, skip, grad, tissue, mask_rows, merged, grad_two,
    semaphores,
):
    two = 2 * WIDE
    last = ROWS * WIDE - two
    pairs = [(tissue_in, tissue)]
    for part in range(2):
        pairs.append((low_in.at[pl.ds(part * 480, 32)], low.at[pl.ds(part * 32, 32)]))
        pairs.append((skip_in.at[pl.ds(part * last, two)], skip.at[pl.ds(part * two, two)]))
        pairs.append((grad_in.at[pl.ds(part * last, two)], grad.at[pl.ds(part * two, two)]))
    for copy in start_copies(pairs, semaphores):
        copy.wait()
    fill_mask_rows(tissue, mask_rows, (0, 7))
    for part in range(2):
        masked_rows(
            part * 7, part, low, skip, grad, mask_rows, part * 32, part * two, merged, grad_two, part * two
        )
    odd = lax.axis_index("rows") % 2 == 1
    for at, source in ((0, merged), (two, grad_two)):
        head, tail = source[0:two, :], source[two : 2 * two, :]
        near[at : at + two, :] = jnp.where(odd, head, tail)
        far_side[at : at + two, :] = jnp.where(odd, tail, head)
    head, tail = mask_rows[0:16, :].astype(BF), mask_rows[112:128, :].astype(BF)
    near[2 * two : 2 * two + 16, :] = jnp.where(odd, head, tail)
    far_side[2 * two : 2 * two + 16, :] = jnp.where(odd, tail, head)


def prep_kernel(
    low_in, skip_in, grad_in, tissue_in, merged, grad_two, mask_rows, low, skip, grad, tissue, semaphores
):
    pairs = [(tissue_in, tissue)]
    for part in range(4):
        fine, coarse = pl.ds(part * 512, 512), pl.ds(part * 128, 128)
        pairs.append((low_in.at[coarse], low.at[coarse]))
        pairs.append((skip_in.at[fine], skip.at[fine]))
        pairs.append((grad_in.at[fine], grad.at[fine]))
    copies = start_copies(pairs, semaphores)
    copies[0].wait()
    fill_mask_rows(tissue, mask_rows, range(8))
    for tile_row in range(8):
        if tile_row % 2 == 0:
            for copy in copies[tile_row // 2 * 3 + 1 : tile_row // 2 * 3 + 4]:
                copy.wait()
        for half in range(2):
            low_row = tile_row * 2 + half
            at = low_row * 2 * WIDE
            masked_rows(tile_row, half, low, skip, grad, mask_rows, low_row * 32, at, merged, grad_two, at)


def expand_kernel(
    slots, filter_one, filter_two, fwd_one, bwd_two, fwd_two_out, bwd_one_out, places, slot_rows,
    fwd_two, bwd_one, semaphores,
):
    flat = jnp.concatenate([slots[row : row + 1, :] for row in range(8)], axis=1)
    owner, local = flat >> 7, (flat & 127).astype(F32)
    tile = iota((128, 128), 1)
    match = owner == iota((128, 128), 0)
    index = tile.astype(F32)
    first = jnp.min(jnp.where(match, index, 1000.0), axis=1, keepdims=True)
    second = match & (index > first)
    used = jnp.sum(jnp.where(second, 1.0, 0.0), axis=0, keepdims=True)
    places[...] = jnp.broadcast_to(owner * 2 + used.astype(jnp.int32), (8, 128))
    slot_one = jnp.sum(jnp.where(match & (index == first), local + 1.0, 0.0), axis=1, keepdims=True)
    slot_two = jnp.sum(jnp.where(second, local + 1.0, 0.0), axis=1, keepdims=True)
    slot_rows[...] = jnp.where(tile == 0, slot_one, jnp.where(tile == 1, slot_two, 0.0)) - 1.0
    across = iota((F, F), 0)
    along = iota((F, F), 1)
    weave = one_hot(((across & 7) * 32 + (across >> 3)) == along)
    perms = [one_hot(across == permuted_index(along, elem)) for elem in range(G)]
    for base, fwd, bwd in ((filter_one, fwd_one, bwd_one), (filter_two, fwd_two, bwd_two)):
        turned = [dot(base[...], perms[elem]).astype(BF) for elem in range(G)]
        for pos in range(9):
            rows = []
            for elem in range(G):
                cell = source_cell(elem, pos)
                rows.append(turned[elem][cell * 32 : cell * 32 + 32, :])
            gathered = jnp.concatenate(rows, axis=0)
            woven = dot(weave, gathered)
            bwd[(8 - pos) * F : (9 - pos) * F, :] = woven.astype(BF)
            fwd[pos * F : (pos + 1) * F, :] = woven.T.astype(BF)
    for copy in start_copies([(fwd_two, fwd_two_out), (bwd_one, bwd_one_out)], semaphores):
        copy.wait()


def edge_kernel(
    merged, grad_two, near_in, far_in, mask_rows, left, right, top, bottom, near, far_side, tall, masks
):
    two = 2 * WIDE
    at_top = lax.axis_index("rows") == 0
    at_bottom = lax.axis_index("rows") == lax.axis_size("rows") - 1
    odd = lax.axis_index("rows") % 2 == 1
    zero = jnp.zeros((272, F), BF)
    top[...] = jnp.where(at_top, zero, jnp.where(odd, near_in[...], far_in[...]))
    bottom[...] = jnp.where(at_bottom, zero, jnp.where(odd, far_in[...], near_in[...]))
    tall[:, 36 * 16 : 48 * 16, :] = jnp.zeros((2, 12 * 16, 128), F32)

    def keep(row, values):
        for half in range(2):
            tall[half, row * 16 : row * 16 + 16, :] = values[:, half * 128 : half * 128 + 128].astype(F32)

    for side, (target, offset, picks, tile_col) in enumerate(
        ((left, 0, (0, 1), 0), (right, 48, (14, 15), 15))
    ):
        for image, source in enumerate((merged, grad_two)):
            for row in range(2):
                place = image * two + row * WIDE + offset
                keep(row, top[place : place + 16, :])
                keep(34 + row, bottom[place : place + 16, :])
            for row in range(ROWS):
                place = row * WIDE + offset
                keep(row + 2, source[place : place + 16, :])
            for col in range(2):
                strip = (image * 2 + col) * STRIP
                for half in range(2):
                    target[strip : strip + STRIP, half * 128 : half * 128 + 128] = tall[
                        half, pl.ds(picks[col], STRIP, stride=16), :
                    ].astype(BF)
        masks[...] = jnp.zeros((STRIP, F), F32)
        above = top[2 * two : 2 * two + 16, :].astype(F32)
        below = bottom[2 * two : 2 * two + 16, :].astype(F32)
        masks[0:2, :] = jnp.broadcast_to(above[tile_col : tile_col + 1, :], (2, F))
        masks[34:36, :] = jnp.broadcast_to(below[tile_col : tile_col + 1, :], (2, F))
        for tile_row in range(8):
            at = tile_row * 16 + tile_col
            masks[2 + 4 * tile_row : 6 + 4 * tile_row, :] = jnp.broadcast_to(mask_rows[at : at + 1, :], (4, F))
        target[4 * STRIP : 5 * STRIP, :] = masks[...].astype(BF)
    odd = lax.axis_index("cols") % 2 == 1
    near[...] = jnp.where(odd, left[...], right[...])
    far_side[...] = jnp.where(odd, right[...], left[...])


def shifted_store(target, at, value, plain, before, after):
    row = iota((WIDE, F), 0)
    target[pl.ds(at, WIDE), 0:F] = jnp.where(row == 0, before, pltpu.roll(value, 1, 0)).astype(BF)
    target[pl.ds(at, WIDE), F : 2 * F] = plain
    target[pl.ds(at, WIDE), 2 * F : 3 * F] = jnp.where(
        row == WIDE - 1, after, pltpu.roll(value, WIDE - 1, 0)
    ).astype(BF)


def conv(shifted, start, count, weight):
    lhs = jnp.concatenate([shifted[pl.ds(start + ky * WIDE, count), :] for ky in range(3)], axis=1)
    return dot(lhs, weight[...])


def interior_kernel(
    merged, grad_two, fwd_one, bwd_two, merged_shift, pre, grad_hidden, grad_ends, grad_shift
):
    nothing = jnp.zeros((1, F), F32)
    for source, target in ((merged, merged_shift), (grad_two, grad_shift)):

        def shift_row(row, _, source=source, target=target):
            at = pl.multiple_of(row * WIDE, WIDE)
            plain = source[pl.ds(at, WIDE), :]
            shifted_store(target, at, plain.astype(F32), plain, nothing, nothing)
            return 0

        lax.fori_loop(0, ROWS, shift_row, 0)

    def convs(step, _):
        at = pl.multiple_of(step * 480, 16)
        pre[pl.ds(at, 480), :] = conv(merged_shift, at, 480, fwd_one)
        grad_hidden[pl.ds(at, 480), :] = conv(grad_shift, at, 480, bwd_two)
        return 0

    lax.fori_loop(0, 4, convs, 0)
    grad_ends[0 : 2 * WIDE, :] = grad_shift[0 : 2 * WIDE, :]
    grad_ends[2 * WIDE : 4 * WIDE, :] = grad_shift[30 * WIDE : 32 * WIDE, :]


def patched_copy(source, source_at, target, target_at, before, after):
    row = iota((16, F), 0)
    target[pl.ds(target_at, WIDE), :] = source[pl.ds(source_at, WIDE), :]
    first = source[pl.ds(source_at, 16), 0:F].astype(F32)
    target[pl.ds(target_at, 16), 0:F] = jnp.where(row == 0, before, first).astype(BF)
    last = source[pl.ds(source_at + 48, 16), 2 * F : 3 * F].astype(F32)
    target[pl.ds(target_at + 48, 16), 2 * F : 3 * F] = jnp.where(row == 15, after, last).astype(BF)


def first_kernel(
    merged, grad_two, top, bottom, left, right, near, far_side, mask_rows, fwd_one, bwd_two,
    merged_inner, pre, grad_hidden, grad_ends,
    hidden_out, pre_out, edge, message,
    hidden_shift, pre_shift, mask_wide, merged_shift, grad_edges, strips, pre_edge, grad_edge, correction, folded, semaphores,
):
    at_left = lax.axis_index("cols") == 0
    at_right = lax.axis_index("cols") == lax.axis_size("cols") - 1
    odd = lax.axis_index("cols") % 2 == 1
    zero = jnp.zeros((STRIP, F), F32)

    def left_strip(index):
        here = slice(index * STRIP, (index + 1) * STRIP)
        value = jnp.where(odd, near[here, :], far_side[here, :])
        return jnp.where(at_left, zero, value.astype(F32))

    def right_strip(index):
        here = slice(index * STRIP, (index + 1) * STRIP)
        value = jnp.where(odd, far_side[here, :], near[here, :])
        return jnp.where(at_right, zero, value.astype(F32))

    two = 2 * WIDE
    spread = one_hot((iota((WIDE, 16), 0) >> 2) == iota((WIDE, 16), 1))
    mask_wide[0:WIDE, :] = dot(spread, top[2 * two : 2 * two + 16, :])
    mask_wide[9 * WIDE : 10 * WIDE, :] = dot(spread, bottom[2 * two : 2 * two + 16, :])
    for tile_row in range(8):
        mask_wide[(tile_row + 1) * WIDE : (tile_row + 2) * WIDE, :] = dot(
            spread, mask_rows[tile_row * 16 : tile_row * 16 + 16, :].astype(BF)
        )
    strip_pre = []
    quad = 4 * WIDE
    for image, (weight, result) in enumerate(((fwd_one, pre_edge), (bwd_two, grad_edge))):
        first = image * 2
        columns = (
            left_strip(first),
            left_strip(first + 1),
            left[first * STRIP : (first + 1) * STRIP, :].astype(F32),
            right[(first + 1) * STRIP : (first + 2) * STRIP, :].astype(F32),
            right_strip(first),
            right_strip(first + 1),
        )
        for index, column in enumerate(columns):
            strips[index * STRIP : (index + 1) * STRIP, :] = column

        def before(row):
            return strips[pl.ds(STRIP + row, 1), :]

        def after(row):
            return strips[pl.ds(4 * STRIP + row, 1), :]

        for row in range(2):
            at = image * two + row * WIDE
            for halo, place, edge_at in ((top, row, row), (bottom, 34 + row, 6 + row)):
                plain = halo[at : at + WIDE, :]
                target, where_to = (grad_edges, edge_at) if image else (merged_shift, place)
                shifted_store(
                    target, where_to * WIDE, plain.astype(F32), plain, before(place), after(place)
                )
        if image:
            for row in range(4):
                place = (2, 3, 32, 33)[row]
                patched_copy(grad_ends, row * WIDE, grad_edges, (2 + row) * WIDE, before(place), after(place))
            ends = [grad_edges[ky * WIDE : ky * WIDE + two, :] for ky in range(3)]
            tails = [grad_edges[quad + ky * WIDE : quad + ky * WIDE + two, :] for ky in range(3)]
        else:

            def patch(row, _):
                patched_copy(
                    merged_inner, pl.multiple_of(row * WIDE, WIDE), merged_shift,
                    pl.multiple_of((row + 2) * WIDE, WIDE), before(row + 2), after(row + 2),
                )
                return 0

            lax.fori_loop(0, ROWS, patch, 0)
            ends = [merged_shift[ky * WIDE : ky * WIDE + two, :] for ky in range(3)]
            tails = [merged_shift[(32 + ky) * WIDE : (32 + ky) * WIDE + two, :] for ky in range(3)]
        lhs = jnp.concatenate([jnp.concatenate(ends, axis=1), jnp.concatenate(tails, axis=1)], axis=0)
        result[...] = dot(lhs, weight[...])
        row = iota((40, F), 0)
        inner = (row >= 2) & (row < 32)
        for side, (index, kx) in enumerate(((1, 0), (4, 2))):
            column = jnp.concatenate(
                [strips[index * STRIP + ky : index * STRIP + ky + 40, :] for ky in range(3)], axis=1
            ).astype(BF)
            taps = jnp.concatenate(
                [weight[(ky * 3 + kx) * F : (ky * 3 + kx + 1) * F, :] for ky in range(3)], axis=0
            )
            at = (image * 2 + side) * 40
            correction[at : at + 40, :] = jnp.where(inner, dot(column, taps), 0.0)
        parts = []
        for ky in range(3):
            for kx in range(3):
                parts.append(
                    jnp.concatenate(
                        [
                            strips[kx * STRIP + ky : kx * STRIP + ky + 40, :],
                            strips[(kx + 3) * STRIP + ky : (kx + 3) * STRIP + ky + 40, :],
                        ],
                        axis=0,
                    ).astype(BF)
                )
        strip_pre.append(dot(jnp.concatenate(parts, axis=1), weight[...]))
    strips[0:STRIP, :] = left_strip(4)
    strips[STRIP : 2 * STRIP, :] = right_strip(4)
    strip_mask = jnp.concatenate([strips[1:41, :], strips[STRIP + 1 : STRIP + 41, :]], axis=0)
    sigma = jax.nn.sigmoid(strip_pre[0])
    edge[0:80, :] = (strip_pre[0] * sigma * strip_mask).astype(BF).astype(F32)
    edge[80:160, :] = (
        (strip_pre[1] * (sigma * (1.0 + strip_pre[0] * (1.0 - sigma))) * strip_mask).astype(BF).astype(F32)
    )

    column = iota((WIDE, F), 0)

    def activate(row, _, pre_from=None, grad_from=None, source_row=0):
        at = pl.multiple_of(row * WIDE, WIDE)
        here = pl.ds(pl.multiple_of((row - source_row) * WIDE, WIDE), WIDE)

        def corrected(value, base):
            value = jnp.where(column == 0, value + correction[pl.ds(base + row, 1), :], value)
            return jnp.where(column == WIDE - 1, value + correction[pl.ds(base + 40 + row, 1), :], value)

        mask = mask_wide[pl.ds(pl.multiple_of(((row + 3) >> 2) * WIDE, WIDE), WIDE), :]
        value = corrected(pre_from[here, :], 0)
        sigma = jax.nn.sigmoid(value)
        hidden = value * sigma * mask
        slope = sigma * (1.0 + value * (1.0 - sigma))
        grad_value = corrected(grad_from[here, :], 80) * slope * mask
        shifted_store(
            hidden_shift, at, hidden, hidden.astype(BF), edge[pl.ds(row, 1), :], edge[pl.ds(40 + row, 1), :]
        )
        shifted_store(
            pre_shift, at, grad_value, grad_value.astype(BF),
            edge[pl.ds(80 + row, 1), :], edge[pl.ds(120 + row, 1), :],
        )
        return 0

    ends = functools.partial(activate, pre_from=pre_edge, grad_from=grad_edge)
    lax.fori_loop(0, 2, functools.partial(ends, source_row=0), 0)
    lax.fori_loop(2, 32, functools.partial(activate, pre_from=pre, grad_from=grad_hidden, source_row=2), 0)
    lax.fori_loop(32, 34, functools.partial(ends, source_row=30), 0)
    copies = start_copies(
        [(hidden_shift.at[:, F : 2 * F], hidden_out), (pre_shift.at[:, F : 2 * F], pre_out)], semaphores
    )
    across = iota((F, F), 0)
    along = iota((F, F), 1)
    unweave = one_hot(((along & 7) * 32 + (along >> 3)) == across)
    perms = [one_hot(along == permuted_index(across, elem)) for elem in range(G)]
    back = jnp.concatenate(perms, axis=0)
    for index, (values, grads, skip) in enumerate(
        (
            (merged_shift, pre_shift[WIDE : 33 * WIDE, F : 2 * F], WIDE),
            (hidden_shift, grad_two[...], 0),
        )
    ):
        turned = dot_nt(unweave, grads).astype(BF)
        full = []
        for ky in range(3):
            start = skip + ky * WIDE
            full.append(dot(turned, values[start : start + ROWS * WIDE, :]).astype(BF))
        pieces = []
        for elem in range(G):
            of_cell = {source_cell(elem, pos): pos for pos in range(9)}
            rows = []
            for cell in range(9):
                pos = of_cell[cell]
                kx = pos % 3
                rows.append(full[pos // 3][elem * 32 : elem * 32 + 32, kx * F : (kx + 1) * F])
            pieces.append(jnp.concatenate(rows, axis=0))
        folded[index * 288 : (index + 1) * 288, :] = dot(jnp.concatenate(pieces, axis=1), back)
    folded[576:592, :] = jnp.zeros((16, F), F32)
    for part in range(128):
        start, lanes = 9 * (part % 64), (part // 64) * 128
        message[part, :, :] = folded[start : start + 16, lanes : lanes + 128].astype(BF)
    for copy in copies:
        copy.wait()


def wide_mask(mask_rows, step):
    spread = one_hot((iota((WIDE, 16), 0) >> 2) == iota((WIDE, 16), 1))
    parts = []
    for tile_row in range(2):
        at = pl.multiple_of((step * 2 + tile_row) * 16, 16)
        parts.extend([dot(spread, mask_rows[pl.ds(at, 16), :].astype(BF))] * 4)
    return jnp.concatenate(parts, axis=0)


def load_shifted(values, weight, edges, base, plain, held, shifted, semaphores):
    cuts = (0, 640, 1152, 1664, 2176)
    pairs = [(weight.at[pl.ds(part * 768, 768)], held.at[pl.ds(part * 768, 768)]) for part in range(3)]
    for first, last in zip(cuts[:-1], cuts[1:]):
        pairs.append((values.at[pl.ds(first, last - first)], plain.at[pl.ds(first, last - first)]))
    copies = start_copies(pairs, semaphores)

    def row_of(row, _):
        at = pl.multiple_of(row * WIDE, WIDE)
        value = plain[pl.ds(at, WIDE), :]
        shifted_store(
            shifted, at, value.astype(F32), value,
            edges[pl.ds(base + row, 1), :], edges[pl.ds(base + 40 + row, 1), :],
        )
        return 0

    for part in range(4):
        copies[3 + part].wait()
        lax.fori_loop(cuts[part] // WIDE, cuts[part + 1] // WIDE, row_of, 0)
    for copy in copies[:3]:
        copy.wait()


def backward_kernel(
    pre_in, weight_in, edges, mask_rows, tiles, low_grad, pair, plain, bwd_one, pre_shift, semaphores
):
    two = 2 * WIDE
    load_shifted(pre_in, weight_in, edges, 80, plain, bwd_one, pre_shift, semaphores)
    order = iota((F, F), 0)
    tile_order = one_hot(
        iota((F, F), 1) == (((order >> 2) & 3) * WIDE + (order >> 4) * 4 + (order & 3))
    )

    def body(step, _):
        at = pl.multiple_of(step * 512, 512)
        grad_merged = conv(pre_shift, at, 512, bwd_one) * wide_mask(mask_rows, step)
        rounded = grad_merged.astype(BF)
        for tile_row in range(2):
            tiles[pl.ds(at + tile_row * F, F), :] = dot(
                tile_order, rounded[tile_row * F : (tile_row + 1) * F, :]
            ).astype(BF)
        for row in range(4):
            both = grad_merged[row * two : row * two + WIDE, :] + grad_merged[row * two + WIDE : row * two + two, :]
            for half in range(2):
                pair[half, row * WIDE : (row + 1) * WIDE, :] = both[:, half * 128 : half * 128 + 128]
        for half in range(2):
            low_grad[pl.ds(pl.multiple_of(step * 128, 128), 128), half * 128 : half * 128 + 128] = (
                pair[half, pl.ds(0, 128, stride=2), :] + pair[half, pl.ds(1, 128, stride=2), :]
            ).astype(BF)
        return 0

    lax.fori_loop(0, 4, body, 0)


def forward_kernel(
    hidden_in, weight_in, edges, mask_rows, output, plain, fwd_two, hidden_shift, semaphores
):
    load_shifted(hidden_in, weight_in, edges, 0, plain, fwd_two, hidden_shift, semaphores)

    def body(step, _):
        at = pl.multiple_of(step * 512, 512)
        output[pl.ds(at, 512), :] = (
            conv(hidden_shift, at, 512, fwd_two) * wide_mask(mask_rows, step)
        ).astype(BF)
        return 0

    lax.fori_loop(0, 4, body, 0)


def pack_kernel(places, tiles, got, slot_rows, send):
    def copy(group, _):
        for sub in range(8):
            tile = group * 8 + sub
            place = places[0, tile]
            send[place >> 1, pl.ds(pl.multiple_of((place & 1) * 16, 16), 16), :] = tiles[
                pl.ds(pl.multiple_of(tile * 16, 16), 16), :
            ]
        return 0

    lax.fori_loop(0, 16, copy, 0)
    total = jnp.zeros((16, 128), F32)
    for part in range(128):
        total = total + got[part, :, :].astype(F32)
    low = total[0:8, :].astype(BF)
    high = jnp.where(iota((8, 128), 0) == 0, total[8:16, :], 0.0)
    for part in range(128):
        send[part, 32:40, 0:128] = low
        send[part, 32:40, 128:256] = jnp.where(
            iota((8, 128), 0) == 1, slot_rows[part : part + 1, :], high
        ).astype(BF)


def place_kernel(scale, got, skip_grad, one, two, gathered, sources, folded, table, semaphore):
    for part in range(128):
        terms = got[part, 32:40, :].astype(F32) * scale
        start, lanes = 9 * (part % 64), (part // 64) * 128
        folded[start : start + 8, lanes : lanes + 128] = terms[:, 0:128]
        folded[start + 8 : start + 9, lanes : lanes + 128] = terms[0:1, 128:256]
        gathered[part : part + 1, :] = terms[1:2, 128:256] / scale
    one[...] = folded[0:288, :]
    two[...] = folded[288:576, :]
    slots = gathered[...].T
    wanted = iota((128, 128), 0).astype(F32)
    index = iota((128, 128), 1).astype(F32)
    source = jnp.zeros((128, 128), F32)
    for which in range(2):
        source = source + jnp.where(slots[which : which + 1, :] == wanted, index * 2.0 + which, 0.0)
    sources[...] = jnp.broadcast_to(jnp.sum(source, axis=1, keepdims=True), (128, 128)).T[0:8, :].astype(jnp.int32)
    copy = pltpu.make_async_copy(sources, table, semaphore)
    copy.start()
    copy.wait()

    def put(group, _):
        for sub in range(8):
            slot = group * 8 + sub
            place = table[0, slot]
            tile = got[place >> 1, pl.ds(pl.multiple_of((place & 1) * 16, 16), 16), :]
            skip_grad[slot] = tile.reshape(4, 4, F)
        return 0

    lax.fori_loop(0, 16, put, 0)


def swap(values, axis, first):
    size = lax.axis_size(axis)
    partner = list(range(size))
    for index in range(first, size - 1, 2):
        partner[index], partner[index + 1] = index + 1, index
    return lax.ppermute(values, axis, list(enumerate(partner)))


def on_device(low_feats, skip_feats, tissue_mask, owner_slot, filter_one, filter_two, out_grad):
    everyone = ("rows", "cols")
    height, breadth, features = skip_feats.shape
    pixels = height * breadth
    given = (
        kept(low_feats.reshape(-1, F)), kept(skip_feats.reshape(pixels, F)),
        kept(out_grad.reshape(pixels, F)), kept(tissue_mask),
    )
    near, far_side = call(
        head_kernel, [shape((272, F))] * 2, 4,
        [
            pltpu.VMEM((64, F), BF), pltpu.VMEM((4 * WIDE, F), BF), pltpu.VMEM((4 * WIDE, F), BF),
            pltpu.VMEM((8, 16), jnp.int32), pltpu.VMEM((128, F), F32), pltpu.VMEM((4 * WIDE, F), BF),
            pltpu.VMEM((4 * WIDE, F), BF), pltpu.SemaphoreType.DMA((7,)),
        ],
        specs=[HBM] * 4, name="head",
    )(*given)
    merged, grad_two, mask_rows = call(
        prep_kernel,
        [shape((pixels, F)), shape((pixels, F)), shape((128, F), F32)],
        4,
        [
            pltpu.VMEM((pixels // 4, F), BF), pltpu.VMEM((pixels, F), BF), pltpu.VMEM((pixels, F), BF),
            pltpu.VMEM((8, 16), jnp.int32), pltpu.SemaphoreType.DMA((13,)),
        ],
        specs=[HBM] * 4, name="prep",
    )(*given)
    near_rows = swap(near, "rows", 0)
    far_rows = swap(far_side, "rows", 1)
    bases = [f.transpose(1, 2, 0, 3).reshape(288, F) for f in (filter_one, filter_two)]
    weights = shape((9 * F, F))
    fwd_one, bwd_two, fwd_two, bwd_one, places, slot_rows = call(
        expand_kernel,
        [weights] * 2 + [far((9 * F, F))] * 2 + [shape((8, 128), jnp.int32), shape((128, 128), F32)],
        3,
        [pltpu.VMEM((9 * F, F), BF), pltpu.VMEM((9 * F, F), BF), pltpu.SemaphoreType.DMA((2,))],
        outs=[VMEM, VMEM, HBM, HBM, VMEM, VMEM], name="expand",
    )(owner_slot, *bases)
    left, right, top, bottom, near, far_side = call(
        edge_kernel,
        [shape((5 * STRIP, F))] * 2 + [shape((272, F))] * 2 + [shape((5 * STRIP, F))] * 2,
        5, [pltpu.VMEM((2, 48 * 16, 128), F32), pltpu.VMEM((STRIP, F), F32)], name="edge",
    )(merged, grad_two, near_rows, far_rows, mask_rows)
    near_cols = swap(near, "cols", 0)
    far_cols = swap(far_side, "cols", 1)
    inner = call(
        interior_kernel,
        [
            shape((pixels, 3 * F)), shape((30 * WIDE, F), F32), shape((30 * WIDE, F), F32),
            shape((4 * WIDE, 3 * F)),
        ],
        4, [pltpu.VMEM((pixels, 3 * F), BF)], flops=5 << 30, limit=16 << 20, name="interior",
    )(merged, grad_two, fwd_one, bwd_two)
    hidden, grad_pre, edges, message = call(
        first_kernel,
        [far((34 * WIDE, F)), far((34 * WIDE, F)), shape((160, F), F32), shape((128, 16, 128))],
        15,
        [
            pltpu.VMEM((34 * WIDE, 3 * F), BF), pltpu.VMEM((34 * WIDE, 3 * F), BF),
            pltpu.VMEM((10 * WIDE, F), F32),
            pltpu.VMEM((36 * WIDE, 3 * F), BF), pltpu.VMEM((8 * WIDE, 3 * F), BF),
            pltpu.VMEM((6 * STRIP, F), F32),
            pltpu.VMEM((4 * WIDE, F), F32), pltpu.VMEM((4 * WIDE, F), F32), pltpu.VMEM((160, F), F32),
            pltpu.VMEM((592, F), F32), pltpu.SemaphoreType.DMA((2,)),
        ],
        outs=[HBM, HBM, VMEM, VMEM], flops=10 << 30, limit=36 << 20, name="first",
    )(merged, grad_two, top, bottom, left, right, near_cols, far_cols, mask_rows, fwd_one, bwd_two, *inner)
    got_terms = lax.all_to_all(message, everyone, 0, 0, tiled=True)
    loading = [
        pltpu.VMEM((34 * WIDE, F), BF), pltpu.VMEM((9 * F, F), BF), pltpu.VMEM((34 * WIDE, 3 * F), BF),
        pltpu.SemaphoreType.DMA((7,)),
    ]
    tiles, low_grad = call(
        backward_kernel, [shape((pixels, F)), shape((pixels // 4, F))], 4,
        [pltpu.VMEM((2, 4 * WIDE, 128), F32)] + loading, specs=[HBM, HBM, VMEM, VMEM],
        flops=3 << 30, name="backward",
    )(kept(grad_pre), kept(bwd_one), edges, mask_rows)
    output = call(
        forward_kernel, shape((pixels, F)), 4, loading, specs=[HBM, HBM, VMEM, VMEM],
        flops=3 << 30, name="forward",
    )(kept(hidden), kept(fwd_two), edges, mask_rows)
    send = call(
        pack_kernel, shape((128, 40, F)), 4, specs=[SMEM, VMEM, VMEM, VMEM], name="pack"
    )(places, tiles, got_terms, slot_rows)
    got = lax.all_to_all(send, everyone, 0, 0, tiled=True)
    scale = 1.0 / math.sqrt(pixels * lax.axis_size("rows") * lax.axis_size("cols"))
    skip_grad, one, two = call(
        functools.partial(place_kernel, scale),
        [shape((128, 4, 4, F)), shape((288, F), F32), shape((288, F), F32)], 1,
        [
            pltpu.VMEM((128, 128), F32), pltpu.VMEM((8, 128), jnp.int32), pltpu.VMEM((592, F), F32),
            pltpu.SMEM((8, 128), jnp.int32), pltpu.SemaphoreType.DMA,
        ],
        name="place",
    )(got)
    return (
        output.reshape(height, breadth, F),
        skip_grad,
        low_grad.reshape(height // 2, breadth // 2, F),
        one.reshape(3, 3, 32, F).transpose(2, 0, 1, 3),
        two.reshape(3, 3, 32, F).transpose(2, 0, 1, 3),
    )


def solution(mesh):
    placed = (
        P("rows", "cols", None),
        P("rows", "cols", None),
        P("rows", "cols"),
        P("rows", "cols"),
        P(),
        P(),
        P("rows", "cols", None),
    )
    return jax.shard_map(
        on_device,
        mesh=mesh,
        in_specs=placed,
        out_specs=(
            P("rows", "cols", None),
            P(("rows", "cols"), None, None, None),
            P("rows", "cols", None),
            P(),
            P(),
        ),
        check_vma=False,
    )
```

```python
import functools
import math

import jax
import jax.numpy as jnp
import numpy as np
from jax import lax
from jax.experimental import pallas as pl
from jax.experimental.pallas import tpu as pltpu
from jax.sharding import PartitionSpec as P

G = 8
F = 256
ROWS = 32
WIDE = 64
STRIP = 48
MASK_ROWS = 16
BF = jnp.bfloat16
F32 = jnp.float32
VMEM = pl.BlockSpec(memory_space=pltpu.VMEM)
SMEM = pl.BlockSpec(memory_space=pltpu.SMEM)
HBM = pl.BlockSpec(memory_space=pltpu.HBM)


def inverse_of(element):
    return (4 - element % 4) % 4 if element < 4 else element


def product(first, second):
    mirror = (first // 4 + second // 4) % 2
    turns = (first % 4 + (1 - 2 * (first // 4)) * (second % 4)) % 4
    return mirror * 4 + turns


def act(element, row, col):
    if element // 4:
        col = -col
    for _ in range(element % 4):
        row, col = -col, row
    return row, col


def source_cell(elem, pos):
    row, col = act(inverse_of(elem), pos // 3 - 1, pos % 3 - 1)
    return (row + 1) * 3 + col + 1


def iota(shape, dim):
    return lax.broadcasted_iota(jnp.int32, shape, dim)


def one_hot(cond):
    return jnp.where(cond, 1.0, 0.0).astype(BF)


def permuted_index(index, elem):
    inverse = inverse_of(elem)
    mirror, turns = inverse // 4, inverse % 4
    second = index & 7
    new_mirror = (second >> 2) ^ mirror
    spin = second & 3
    new_turns = (turns + (-spin if mirror else spin)) & 3
    return (index & ~7) | (new_mirror << 2) | new_turns


def dot(lhs, rhs):
    return jnp.dot(lhs, rhs, preferred_element_type=F32)


def dot_nt(lhs, rhs):
    return lax.dot_general(lhs, rhs, (((1,), (1,)), ((), ())), preferred_element_type=F32)


def call(
    kernel, out_shape, n_in, scratch=(), specs=None, outs=None, flops=1 << 30, limit=24 << 20, name=None
):
    return pl.pallas_call(
        kernel,
        out_shape=out_shape,
        in_specs=specs or [VMEM] * n_in,
        out_specs=outs or jax.tree.map(lambda _: VMEM, out_shape),
        scratch_shapes=list(scratch),
        compiler_params=pltpu.CompilerParams(vmem_limit_bytes=limit),
        cost_estimate=pl.CostEstimate(flops=flops, bytes_accessed=4 << 20, transcendentals=0),
        name=name,
    )


def shape(dims, dtype=BF):
    return jax.ShapeDtypeStruct(dims, dtype)


def far(dims):
    return pltpu.HBM(dims, BF)


def kept(values):
    return pltpu.with_memory_space_constraint(values, pltpu.HBM)


def start_copies(pairs, semaphores):
    copies = [pltpu.make_async_copy(src, dst, semaphores.at[i]) for i, (src, dst) in enumerate(pairs)]
    for copy in copies:
        copy.start()
    return copies


def fill_mask_rows(tissue, mask_rows, tile_rows):
    same = iota((16, 16), 0) == iota((16, 16), 1)
    for tile_row in tile_rows:
        values = jnp.broadcast_to(tissue[tile_row : tile_row + 1, :].astype(F32), (16, 16))
        column = jnp.sum(jnp.where(same, values, 0.0), axis=1, keepdims=True)
        mask_rows[tile_row * 16 : tile_row * 16 + 16, :] = jnp.broadcast_to(column, (16, F))


def masked_rows(tile_row, half, low, skip, grad, mask_rows, low_at, at, merged, grad_two, put):
    spread = one_hot((iota((WIDE, 16), 0) >> 2) == iota((WIDE, 16), 1))
    twice = one_hot((iota((WIDE, 32), 0) >> 1) == iota((WIDE, 32), 1))
    mask = dot(spread, mask_rows[tile_row * 16 : tile_row * 16 + 16, :].astype(BF))
    coarse = dot(twice, low[low_at : low_at + 32, :])
    for sub in range(2):
        here, there = pl.ds(at + sub * WIDE, WIDE), pl.ds(put + sub * WIDE, WIDE)
        merged[there, :] = ((coarse + skip[here, :].astype(F32)) * mask).astype(BF)
        grad_two[there, :] = (grad[here, :].astype(F32) * mask).astype(BF)


def head_kernel(
    low_in, skip_in, grad_in, tissue_in, near, far_side, low, skip, grad, tissue, mask_rows, merged, grad_two,
    semaphores,
):
    two = 2 * WIDE
    last = ROWS * WIDE - two
    pairs = [(tissue_in, tissue)]
    for part in range(2):
        pairs.append((low_in.at[pl.ds(part * 480, 32)], low.at[pl.ds(part * 32, 32)]))
        pairs.append((skip_in.at[pl.ds(part * last, two)], skip.at[pl.ds(part * two, two)]))
        pairs.append((grad_in.at[pl.ds(part * last, two)], grad.at[pl.ds(part * two, two)]))
    for copy in start_copies(pairs, semaphores):
        copy.wait()
    fill_mask_rows(tissue, mask_rows, (0, 7))
    for part in range(2):
        masked_rows(
            part * 7, part, low, skip, grad, mask_rows, part * 32, part * two, merged, grad_two, part * two
        )
    odd = lax.axis_index("rows") % 2 == 1
    for at, source in ((0, merged), (two, grad_two)):
        head, tail = source[0:two, :], source[two : 2 * two, :]
        near[at : at + two, :] = jnp.where(odd, head, tail)
        far_side[at : at + two, :] = jnp.where(odd, tail, head)
    head, tail = mask_rows[0:16, :].astype(BF), mask_rows[112:128, :].astype(BF)
    near[2 * two : 2 * two + 16, :] = jnp.where(odd, head, tail)
    far_side[2 * two : 2 * two + 16, :] = jnp.where(odd, tail, head)


def build_weight(base, weight, forward):
    across = iota((F, F), 0)
    along = iota((F, F), 1)
    weave = one_hot(((across & 7) * 32 + (across >> 3)) == along)
    turned = [dot(base[...], one_hot(across == permuted_index(along, elem))).astype(BF) for elem in range(G)]
    for pos in range(9):
        rows = []
        for elem in range(G):
            cell = source_cell(elem, pos)
            rows.append(turned[elem][cell * 32 : cell * 32 + 32, :])
        woven = dot(weave, jnp.concatenate(rows, axis=0))
        if forward:
            weight[pos * F : (pos + 1) * F, :] = woven.T.astype(BF)
        else:
            weight[(8 - pos) * F : (9 - pos) * F, :] = woven.astype(BF)


def prepare_kernel(
    low_in, skip_in, grad_in, tissue_in, slots, filter_one, filter_two,
    merged, grad_two, mask_rows, fwd_one, bwd_two, places, slot_rows,
    low, skip, grad, tissue, semaphores,
):
    pairs = [(tissue_in, tissue)]
    for part in range(4):
        fine, coarse = pl.ds(part * 512, 512), pl.ds(part * 128, 128)
        pairs.append((low_in.at[coarse], low.at[coarse]))
        pairs.append((skip_in.at[fine], skip.at[fine]))
        pairs.append((grad_in.at[fine], grad.at[fine]))
    copies = start_copies(pairs, semaphores)
    flat = jnp.concatenate([slots[row : row + 1, :] for row in range(8)], axis=1)
    owner, local = flat >> 7, (flat & 127).astype(F32)
    tile = iota((128, 128), 1)
    match = owner == iota((128, 128), 0)
    index = tile.astype(F32)
    first = jnp.min(jnp.where(match, index, 1000.0), axis=1, keepdims=True)
    second = match & (index > first)
    used = jnp.sum(jnp.where(second, 1.0, 0.0), axis=0, keepdims=True)
    places[...] = jnp.broadcast_to(owner * 2 + used.astype(jnp.int32), (8, 128))
    slot_one = jnp.sum(jnp.where(match & (index == first), local + 1.0, 0.0), axis=1, keepdims=True)
    slot_two = jnp.sum(jnp.where(second, local + 1.0, 0.0), axis=1, keepdims=True)
    slot_rows[...] = jnp.where(tile == 0, slot_one, jnp.where(tile == 1, slot_two, 0.0)) - 1.0
    build_weight(filter_one, fwd_one, True)
    build_weight(filter_two, bwd_two, False)
    copies[0].wait()
    fill_mask_rows(tissue, mask_rows, range(8))
    for copy in copies[1:]:
        copy.wait()
    for low_row in range(16):
        at = low_row * 2 * WIDE
        masked_rows(
            low_row // 2, low_row % 2, low, skip, grad, mask_rows, low_row * 32, at, merged, grad_two, at
        )


def edge_kernel(
    merged, grad_two, near_in, far_in, mask_rows, left, right, top, bottom, near, far_side, tall, masks
):
    two = 2 * WIDE
    at_top = lax.axis_index("rows") == 0
    at_bottom = lax.axis_index("rows") == lax.axis_size("rows") - 1
    odd = lax.axis_index("rows") % 2 == 1
    zero = jnp.zeros((272, F), BF)
    top[...] = jnp.where(at_top, zero, jnp.where(odd, near_in[...], far_in[...]))
    bottom[...] = jnp.where(at_bottom, zero, jnp.where(odd, far_in[...], near_in[...]))
    tall[:, 36 * 16 : 48 * 16, :] = jnp.zeros((2, 12 * 16, 128), F32)

    def keep(row, values):
        for half in range(2):
            tall[half, row * 16 : row * 16 + 16, :] = values[:, half * 128 : half * 128 + 128].astype(F32)

    for side, (target, offset, picks, tile_col) in enumerate(
        ((left, 0, (0, 1), 0), (right, 48, (14, 15), 15))
    ):
        for image, source in enumerate((merged, grad_two)):
            for row in range(2):
                place = image * two + row * WIDE + offset
                keep(row, top[place : place + 16, :])
                keep(34 + row, bottom[place : place + 16, :])
            for row in range(ROWS):
                place = row * WIDE + offset
                keep(row + 2, source[place : place + 16, :])
            for col in range(2):
                strip = (image * 2 + col) * STRIP
                for half in range(2):
                    target[strip : strip + STRIP, half * 128 : half * 128 + 128] = tall[
                        half, pl.ds(picks[col], STRIP, stride=16), :
                    ].astype(BF)
        masks[...] = jnp.zeros((STRIP, F), F32)
        above = top[2 * two : 2 * two + 16, :].astype(F32)
        below = bottom[2 * two : 2 * two + 16, :].astype(F32)
        masks[0:2, :] = jnp.broadcast_to(above[tile_col : tile_col + 1, :], (2, F))
        masks[34:36, :] = jnp.broadcast_to(below[tile_col : tile_col + 1, :], (2, F))
        for tile_row in range(8):
            at = tile_row * 16 + tile_col
            masks[2 + 4 * tile_row : 6 + 4 * tile_row, :] = jnp.broadcast_to(mask_rows[at : at + 1, :], (4, F))
        target[4 * STRIP : 5 * STRIP, :] = masks[...].astype(BF)
    odd = lax.axis_index("cols") % 2 == 1
    near[...] = jnp.where(odd, left[...], right[...])
    far_side[...] = jnp.where(odd, right[...], left[...])


def shifted_store(target, at, value, plain, before, after):
    row = iota((WIDE, F), 0)
    target[pl.ds(at, WIDE), 0:F] = jnp.where(row == 0, before, pltpu.roll(value, 1, 0)).astype(BF)
    target[pl.ds(at, WIDE), F : 2 * F] = plain
    target[pl.ds(at, WIDE), 2 * F : 3 * F] = jnp.where(
        row == WIDE - 1, after, pltpu.roll(value, WIDE - 1, 0)
    ).astype(BF)


def conv(shifted, start, count, weight):
    lhs = jnp.concatenate([shifted[pl.ds(start + ky * WIDE, count), :] for ky in range(3)], axis=1)
    return dot(lhs, weight[...])


def interior_kernel(
    merged, grad_two, fwd_one, bwd_two, merged_shift, pre, grad_hidden, grad_ends, grad_shift
):
    nothing = jnp.zeros((1, F), F32)
    for source, target in ((merged, merged_shift), (grad_two, grad_shift)):

        def shift_row(row, _, source=source, target=target):
            at = pl.multiple_of(row * WIDE, WIDE)
            plain = source[pl.ds(at, WIDE), :]
            shifted_store(target, at, plain.astype(F32), plain, nothing, nothing)
            return 0

        lax.fori_loop(0, ROWS, shift_row, 0)

    pre[...] = conv(merged_shift, 0, 30 * WIDE, fwd_one)
    grad_hidden[...] = conv(grad_shift, 0, 30 * WIDE, bwd_two)
    grad_ends[0 : 2 * WIDE, :] = grad_shift[0 : 2 * WIDE, :]
    grad_ends[2 * WIDE : 4 * WIDE, :] = grad_shift[30 * WIDE : 32 * WIDE, :]


def patched_copy(source, source_at, target, target_at, before, after):
    row = iota((16, F), 0)
    target[pl.ds(target_at, WIDE), :] = source[pl.ds(source_at, WIDE), :]
    first = source[pl.ds(source_at, 16), 0:F].astype(F32)
    target[pl.ds(target_at, 16), 0:F] = jnp.where(row == 0, before, first).astype(BF)
    last = source[pl.ds(source_at + 48, 16), 2 * F : 3 * F].astype(F32)
    target[pl.ds(target_at + 48, 16), 2 * F : 3 * F] = jnp.where(row == 15, after, last).astype(BF)


def first_kernel(
    merged, grad_two, top, bottom, left, right, near, far_side, mask_rows, fwd_one, bwd_two,
    merged_inner, pre, grad_hidden, grad_ends,
    hidden_out, pre_out, edge, message,
    hidden_shift, pre_shift, mask_wide, merged_shift, grad_edges, strips, pre_edge, grad_edge, correction, folded, semaphores,
):
    at_left = lax.axis_index("cols") == 0
    at_right = lax.axis_index("cols") == lax.axis_size("cols") - 1
    odd = lax.axis_index("cols") % 2 == 1
    zero = jnp.zeros((STRIP, F), F32)

    def left_strip(index):
        here = slice(index * STRIP, (index + 1) * STRIP)
        value = jnp.where(odd, near[here, :], far_side[here, :])
        return jnp.where(at_left, zero, value.astype(F32))

    def right_strip(index):
        here = slice(index * STRIP, (index + 1) * STRIP)
        value = jnp.where(odd, far_side[here, :], near[here, :])
        return jnp.where(at_right, zero, value.astype(F32))

    two = 2 * WIDE
    spread = one_hot((iota((WIDE, 16), 0) >> 2) == iota((WIDE, 16), 1))
    mask_wide[0:WIDE, :] = dot(spread, top[2 * two : 2 * two + 16, :])
    mask_wide[9 * WIDE : 10 * WIDE, :] = dot(spread, bottom[2 * two : 2 * two + 16, :])
    for tile_row in range(8):
        mask_wide[(tile_row + 1) * WIDE : (tile_row + 2) * WIDE, :] = dot(
            spread, mask_rows[tile_row * 16 : tile_row * 16 + 16, :].astype(BF)
        )
    strip_pre = []
    quad = 4 * WIDE
    for image, (weight, result) in enumerate(((fwd_one, pre_edge), (bwd_two, grad_edge))):
        first = image * 2
        columns = (
            left_strip(first),
            left_strip(first + 1),
            left[first * STRIP : (first + 1) * STRIP, :].astype(F32),
            right[(first + 1) * STRIP : (first + 2) * STRIP, :].astype(F32),
            right_strip(first),
            right_strip(first + 1),
        )
        for index, column in enumerate(columns):
            strips[index * STRIP : (index + 1) * STRIP, :] = column

        def before(row):
            return strips[pl.ds(STRIP + row, 1), :]

        def after(row):
            return strips[pl.ds(4 * STRIP + row, 1), :]

        for row in range(2):
            at = image * two + row * WIDE
            for halo, place, edge_at in ((top, row, row), (bottom, 34 + row, 6 + row)):
                plain = halo[at : at + WIDE, :]
                target, where_to = (grad_edges, edge_at) if image else (merged_shift, place)
                shifted_store(
                    target, where_to * WIDE, plain.astype(F32), plain, before(place), after(place)
                )
        if image:
            for row in range(4):
                place = (2, 3, 32, 33)[row]
                patched_copy(grad_ends, row * WIDE, grad_edges, (2 + row) * WIDE, before(place), after(place))
            ends = [grad_edges[ky * WIDE : ky * WIDE + two, :] for ky in range(3)]
            tails = [grad_edges[quad + ky * WIDE : quad + ky * WIDE + two, :] for ky in range(3)]
        else:

            def patch(row, _):
                patched_copy(
                    merged_inner, pl.multiple_of(row * WIDE, WIDE), merged_shift,
                    pl.multiple_of((row + 2) * WIDE, WIDE), before(row + 2), after(row + 2),
                )
                return 0

            lax.fori_loop(0, ROWS, patch, 0)
            ends = [merged_shift[ky * WIDE : ky * WIDE + two, :] for ky in range(3)]
            tails = [merged_shift[(32 + ky) * WIDE : (32 + ky) * WIDE + two, :] for ky in range(3)]
        lhs = jnp.concatenate([jnp.concatenate(ends, axis=1), jnp.concatenate(tails, axis=1)], axis=0)
        result[...] = dot(lhs, weight[...])
        row = iota((40, F), 0)
        inner = (row >= 2) & (row < 32)
        for side, (index, kx) in enumerate(((1, 0), (4, 2))):
            column = jnp.concatenate(
                [strips[index * STRIP + ky : index * STRIP + ky + 40, :] for ky in range(3)], axis=1
            ).astype(BF)
            taps = jnp.concatenate(
                [weight[(ky * 3 + kx) * F : (ky * 3 + kx + 1) * F, :] for ky in range(3)], axis=0
            )
            at = (image * 2 + side) * 40
            correction[at : at + 40, :] = jnp.where(inner, dot(column, taps), 0.0)
        parts = []
        for ky in range(3):
            for kx in range(3):
                parts.append(
                    jnp.concatenate(
                        [
                            strips[kx * STRIP + ky : kx * STRIP + ky + 40, :],
                            strips[(kx + 3) * STRIP + ky : (kx + 3) * STRIP + ky + 40, :],
                        ],
                        axis=0,
                    ).astype(BF)
                )
        strip_pre.append(dot(jnp.concatenate(parts, axis=1), weight[...]))
    strips[0:STRIP, :] = left_strip(4)
    strips[STRIP : 2 * STRIP, :] = right_strip(4)
    strip_mask = jnp.concatenate([strips[1:41, :], strips[STRIP + 1 : STRIP + 41, :]], axis=0)
    sigma = jax.nn.sigmoid(strip_pre[0])
    edge[0:80, :] = (strip_pre[0] * sigma * strip_mask).astype(BF).astype(F32)
    edge[80:160, :] = (
        (strip_pre[1] * (sigma * (1.0 + strip_pre[0] * (1.0 - sigma))) * strip_mask).astype(BF).astype(F32)
    )

    column = iota((WIDE, F), 0)

    def activate(row, _, pre_from=None, grad_from=None, source_row=0):
        at = pl.multiple_of(row * WIDE, WIDE)
        here = pl.ds(pl.multiple_of((row - source_row) * WIDE, WIDE), WIDE)

        def corrected(value, base):
            value = jnp.where(column == 0, value + correction[pl.ds(base + row, 1), :], value)
            return jnp.where(column == WIDE - 1, value + correction[pl.ds(base + 40 + row, 1), :], value)

        mask = mask_wide[pl.ds(pl.multiple_of(((row + 3) >> 2) * WIDE, WIDE), WIDE), :]
        value = corrected(pre_from[here, :], 0)
        sigma = jax.nn.sigmoid(value)
        hidden = value * sigma * mask
        slope = sigma * (1.0 + value * (1.0 - sigma))
        grad_value = corrected(grad_from[here, :], 80) * slope * mask
        shifted_store(
            hidden_shift, at, hidden, hidden.astype(BF), edge[pl.ds(row, 1), :], edge[pl.ds(40 + row, 1), :]
        )
        shifted_store(
            pre_shift, at, grad_value, grad_value.astype(BF),
            edge[pl.ds(80 + row, 1), :], edge[pl.ds(120 + row, 1), :],
        )
        return 0

    ends = functools.partial(activate, pre_from=pre_edge, grad_from=grad_edge)
    lax.fori_loop(0, 2, functools.partial(ends, source_row=0), 0)
    lax.fori_loop(2, 32, functools.partial(activate, pre_from=pre, grad_from=grad_hidden, source_row=2), 0)
    lax.fori_loop(32, 34, functools.partial(ends, source_row=30), 0)
    copies = start_copies(
        [(hidden_shift.at[:, F : 2 * F], hidden_out), (pre_shift.at[:, F : 2 * F], pre_out)], semaphores
    )
    across = iota((F, F), 0)
    along = iota((F, F), 1)
    unweave = one_hot(((along & 7) * 32 + (along >> 3)) == across)
    perms = [one_hot(along == permuted_index(across, elem)) for elem in range(G)]
    back = jnp.concatenate(perms, axis=0)
    for index, (values, grads, skip) in enumerate(
        (
            (merged_shift, pre_shift[WIDE : 33 * WIDE, F : 2 * F], WIDE),
            (hidden_shift, grad_two[...], 0),
        )
    ):
        turned = dot_nt(unweave, grads).astype(BF)
        full = []
        for ky in range(3):
            start = skip + ky * WIDE
            full.append(dot(turned, values[start : start + ROWS * WIDE, :]).astype(BF))
        pieces = []
        for elem in range(G):
            of_cell = {source_cell(elem, pos): pos for pos in range(9)}
            rows = []
            for cell in range(9):
                pos = of_cell[cell]
                kx = pos % 3
                rows.append(full[pos // 3][elem * 32 : elem * 32 + 32, kx * F : (kx + 1) * F])
            pieces.append(jnp.concatenate(rows, axis=0))
        folded[index * 288 : (index + 1) * 288, :] = dot(jnp.concatenate(pieces, axis=1), back)
    folded[576:592, :] = jnp.zeros((16, F), F32)
    for part in range(128):
        start, lanes = 9 * (part % 64), (part // 64) * 128
        message[part, :, :] = folded[start : start + 16, lanes : lanes + 128].astype(BF)
    for copy in copies:
        copy.wait()


def wide_mask(mask_rows, step):
    spread = one_hot((iota((WIDE, 16), 0) >> 2) == iota((WIDE, 16), 1))
    parts = []
    for tile_row in range(4):
        at = pl.multiple_of((step * 4 + tile_row) * 16, 16)
        parts.extend([dot(spread, mask_rows[pl.ds(at, 16), :].astype(BF))] * 4)
    return jnp.concatenate(parts, axis=0)


def load_shifted(values, filter_in, edges, base, plain, filter_held, weight, forward, shifted, semaphores):
    cuts = (0, 640, 1152, 1664, 2176)
    pairs = [(filter_in, filter_held)]
    for first, last in zip(cuts[:-1], cuts[1:]):
        pairs.append((values.at[pl.ds(first, last - first)], plain.at[pl.ds(first, last - first)]))
    copies = start_copies(pairs, semaphores)

    def row_of(row, _):
        at = pl.multiple_of(row * WIDE, WIDE)
        value = plain[pl.ds(at, WIDE), :]
        shifted_store(
            shifted, at, value.astype(F32), value,
            edges[pl.ds(base + row, 1), :], edges[pl.ds(base + 40 + row, 1), :],
        )
        return 0

    copies[0].wait()
    build_weight(filter_held, weight, forward)
    for copy in copies[1:]:
        copy.wait()
    lax.fori_loop(0, ROWS + 2, row_of, 0)


def backward_kernel(
    pre_in, filter_in, edges, mask_rows, tiles, low_grad,
    pair, plain, filter_held, bwd_one, pre_shift, semaphores,
):
    two = 2 * WIDE
    load_shifted(pre_in, filter_in, edges, 80, plain, filter_held, bwd_one, False, pre_shift, semaphores)
    order = iota((F, F), 0)
    tile_order = one_hot(
        iota((F, F), 1) == (((order >> 2) & 3) * WIDE + (order >> 4) * 4 + (order & 3))
    )

    def body(step, _):
        at = pl.multiple_of(step * 1024, 1024)
        grad_merged = conv(pre_shift, at, 1024, bwd_one) * wide_mask(mask_rows, step)
        rounded = grad_merged.astype(BF)
        for tile_row in range(4):
            tiles[pl.ds(at + tile_row * F, F), :] = dot(
                tile_order, rounded[tile_row * F : (tile_row + 1) * F, :]
            ).astype(BF)
        for row in range(8):
            both = grad_merged[row * two : row * two + WIDE, :] + grad_merged[row * two + WIDE : row * two + two, :]
            for half in range(2):
                pair[half, row * WIDE : (row + 1) * WIDE, :] = both[:, half * 128 : half * 128 + 128]
        for half in range(2):
            low_grad[pl.ds(pl.multiple_of(step * 256, 256), 256), half * 128 : half * 128 + 128] = (
                pair[half, pl.ds(0, 256, stride=2), :] + pair[half, pl.ds(1, 256, stride=2), :]
            ).astype(BF)
        return 0

    lax.fori_loop(0, 2, body, 0)


def forward_kernel(
    hidden_in, filter_in, edges, mask_rows, output, plain, filter_held, fwd_two, hidden_shift, semaphores
):
    load_shifted(hidden_in, filter_in, edges, 0, plain, filter_held, fwd_two, True, hidden_shift, semaphores)

    def body(step, _):
        at = pl.multiple_of(step * 1024, 1024)
        output[pl.ds(at, 1024), :] = (
            conv(hidden_shift, at, 1024, fwd_two) * wide_mask(mask_rows, step)
        ).astype(BF)
        return 0

    lax.fori_loop(0, 2, body, 0)


def pack_kernel(places, tiles, send):
    def copy(group, _):
        for sub in range(8):
            tile = group * 8 + sub
            place = places[0, tile]
            send[place >> 1, pl.ds(pl.multiple_of((place & 1) * 16, 16), 16), :] = tiles[
                pl.ds(pl.multiple_of(tile * 16, 16), 16), :
            ]
        return 0

    lax.fori_loop(0, 16, copy, 0)


def terms_kernel(send_in, got, slot_rows, send, rows, semaphore):
    total = jnp.zeros((16, 128), F32)
    for part in range(128):
        total = total + got[part, :, :].astype(F32)
    low = total[0:8, :].astype(BF)
    row = iota((8, 128), 0)
    high = jnp.where(row == 0, total[8:16, :], 0.0)
    for part in range(128):
        rows[part, :, 0:128] = low
        rows[part, :, 128:256] = jnp.where(row == 1, slot_rows[part : part + 1, :], high).astype(BF)
    copy = pltpu.make_async_copy(rows, send.at[:, pl.ds(32, 8)], semaphore)
    copy.start()
    copy.wait()


def place_kernel(scale, got, skip_grad, one, two, gathered, sources, folded, table, semaphore):
    for part in range(128):
        terms = got[part, 32:40, :].astype(F32) * scale
        start, lanes = 9 * (part % 64), (part // 64) * 128
        folded[start : start + 8, lanes : lanes + 128] = terms[:, 0:128]
        folded[start + 8 : start + 9, lanes : lanes + 128] = terms[0:1, 128:256]
        gathered[part : part + 1, :] = terms[1:2, 128:256] / scale
    one[...] = folded[0:288, :]
    two[...] = folded[288:576, :]
    slots = gathered[...].T
    wanted = iota((128, 128), 0).astype(F32)
    index = iota((128, 128), 1).astype(F32)
    source = jnp.zeros((128, 128), F32)
    for which in range(2):
        source = source + jnp.where(slots[which : which + 1, :] == wanted, index * 2.0 + which, 0.0)
    sources[...] = jnp.broadcast_to(jnp.sum(source, axis=1, keepdims=True), (128, 128)).T[0:8, :].astype(jnp.int32)
    copy = pltpu.make_async_copy(sources, table, semaphore)
    copy.start()
    copy.wait()

    def put(group, _):
        for sub in range(8):
            slot = group * 8 + sub
            place = table[0, slot]
            tile = got[place >> 1, pl.ds(pl.multiple_of((place & 1) * 16, 16), 16), :]
            skip_grad[slot] = tile.reshape(4, 4, F)
        return 0

    lax.fori_loop(0, 16, put, 0)


def swap(values, axis, first):
    size = lax.axis_size(axis)
    partner = list(range(size))
    for index in range(first, size - 1, 2):
        partner[index], partner[index + 1] = index + 1, index
    return lax.ppermute(values, axis, list(enumerate(partner)))


def on_device(low_feats, skip_feats, tissue_mask, owner_slot, filter_one, filter_two, out_grad):
    everyone = ("rows", "cols")
    height, breadth, features = skip_feats.shape
    pixels = height * breadth
    given = (
        kept(low_feats.reshape(-1, F)), kept(skip_feats.reshape(pixels, F)),
        kept(out_grad.reshape(pixels, F)), kept(tissue_mask),
    )
    near, far_side = call(
        head_kernel, [shape((272, F))] * 2, 4,
        [
            pltpu.VMEM((64, F), BF), pltpu.VMEM((4 * WIDE, F), BF), pltpu.VMEM((4 * WIDE, F), BF),
            pltpu.VMEM((8, 16), jnp.int32), pltpu.VMEM((128, F), F32), pltpu.VMEM((4 * WIDE, F), BF),
            pltpu.VMEM((4 * WIDE, F), BF), pltpu.SemaphoreType.DMA((7,)),
        ],
        specs=[HBM] * 4, name="head",
    )(*given)
    near_rows = swap(near, "rows", 0)
    far_rows = swap(far_side, "rows", 1)
    bases = [f.transpose(1, 2, 0, 3).reshape(288, F) for f in (filter_one, filter_two)]
    merged, grad_two, mask_rows, fwd_one, bwd_two, places, slot_rows = call(
        prepare_kernel,
        [
            shape((pixels, F)), shape((pixels, F)), shape((128, F), F32), shape((9 * F, F)),
            shape((9 * F, F)), shape((8, 128), jnp.int32), shape((128, 128), F32),
        ],
        7,
        [
            pltpu.VMEM((pixels // 4, F), BF), pltpu.VMEM((pixels, F), BF), pltpu.VMEM((pixels, F), BF),
            pltpu.VMEM((8, 16), jnp.int32), pltpu.SemaphoreType.DMA((13,)),
        ],
        specs=[HBM] * 4 + [VMEM] * 3, flops=3 << 30, name="prepare",
    )(*given, owner_slot, *bases)
    left, right, top, bottom, near, far_side = call(
        edge_kernel,
        [shape((5 * STRIP, F))] * 2 + [shape((272, F))] * 2 + [shape((5 * STRIP, F))] * 2,
        5, [pltpu.VMEM((2, 48 * 16, 128), F32), pltpu.VMEM((STRIP, F), F32)], name="edge",
    )(merged, grad_two, near_rows, far_rows, mask_rows)
    near_cols = swap(near, "cols", 0)
    far_cols = swap(far_side, "cols", 1)
    inner = call(
        interior_kernel,
        [
            shape((pixels, 3 * F)), shape((30 * WIDE, F), F32), shape((30 * WIDE, F), F32),
            shape((4 * WIDE, 3 * F)),
        ],
        4, [pltpu.VMEM((pixels, 3 * F), BF)], flops=5 << 30, limit=16 << 20, name="interior",
    )(merged, grad_two, fwd_one, bwd_two)
    hidden, grad_pre, edges, message = call(
        first_kernel,
        [far((34 * WIDE, F)), far((34 * WIDE, F)), shape((160, F), F32), shape((128, 16, 128))],
        15,
        [
            pltpu.VMEM((34 * WIDE, 3 * F), BF), pltpu.VMEM((34 * WIDE, 3 * F), BF),
            pltpu.VMEM((10 * WIDE, F), F32),
            pltpu.VMEM((36 * WIDE, 3 * F), BF), pltpu.VMEM((8 * WIDE, 3 * F), BF),
            pltpu.VMEM((6 * STRIP, F), F32),
            pltpu.VMEM((4 * WIDE, F), F32), pltpu.VMEM((4 * WIDE, F), F32), pltpu.VMEM((160, F), F32),
            pltpu.VMEM((592, F), F32), pltpu.SemaphoreType.DMA((2,)),
        ],
        outs=[HBM, HBM, VMEM, VMEM], flops=10 << 30, limit=36 << 20, name="first",
    )(merged, grad_two, top, bottom, left, right, near_cols, far_cols, mask_rows, fwd_one, bwd_two, *inner)
    got_terms = lax.all_to_all(message, everyone, 0, 0, tiled=True)
    loading = [
        pltpu.VMEM((34 * WIDE, F), BF), pltpu.VMEM((288, F), BF), pltpu.VMEM((9 * F, F), BF),
        pltpu.VMEM((34 * WIDE, 3 * F), BF), pltpu.SemaphoreType.DMA((5,)),
    ]
    tiles, low_grad = call(
        backward_kernel, [shape((pixels, F)), shape((pixels // 4, F))], 4,
        [pltpu.VMEM((2, 8 * WIDE, 128), F32)] + loading, specs=[HBM, HBM, VMEM, VMEM],
        flops=3 << 30, name="backward",
    )(kept(grad_pre), kept(bases[0]), edges, mask_rows)
    output = call(
        forward_kernel, shape((pixels, F)), 4, loading, specs=[HBM, HBM, VMEM, VMEM],
        flops=3 << 30, name="forward",
    )(kept(hidden), kept(bases[1]), edges, mask_rows)
    send = call(pack_kernel, far((128, 40, F)), 2, specs=[SMEM, VMEM], name="pack")(places, tiles)
    send = pl.pallas_call(
        terms_kernel,
        out_shape=far((128, 40, F)),
        in_specs=[HBM, VMEM, VMEM],
        out_specs=HBM,
        scratch_shapes=[pltpu.VMEM((128, 8, F), BF), pltpu.SemaphoreType.DMA],
        input_output_aliases={0: 0},
        compiler_params=pltpu.CompilerParams(vmem_limit_bytes=24 << 20),
        cost_estimate=pl.CostEstimate(flops=1 << 30, bytes_accessed=4 << 20, transcendentals=0),
        name="terms",
    )(kept(send), got_terms, slot_rows)
    got = lax.all_to_all(send, everyone, 0, 0, tiled=True)
    scale = 1.0 / math.sqrt(pixels * lax.axis_size("rows") * lax.axis_size("cols"))
    skip_grad, one, two = call(
        functools.partial(place_kernel, scale),
        [shape((128, 4, 4, F)), shape((288, F), F32), shape((288, F), F32)], 1,
        [
            pltpu.VMEM((128, 128), F32), pltpu.VMEM((8, 128), jnp.int32), pltpu.VMEM((592, F), F32),
            pltpu.SMEM((8, 128), jnp.int32), pltpu.SemaphoreType.DMA,
        ],
        name="place",
    )(got)
    return (
        output.reshape(height, breadth, F),
        skip_grad,
        low_grad.reshape(height // 2, breadth // 2, F),
        one.reshape(3, 3, 32, F).transpose(2, 0, 1, 3),
        two.reshape(3, 3, 32, F).transpose(2, 0, 1, 3),
    )


def solution(mesh):
    placed = (
        P("rows", "cols", None),
        P("rows", "cols", None),
        P("rows", "cols"),
        P("rows", "cols"),
        P(),
        P(),
        P("rows", "cols", None),
    )
    return jax.shard_map(
        on_device,
        mesh=mesh,
        in_specs=placed,
        out_specs=(
            P("rows", "cols", None),
            P(("rows", "cols"), None, None, None),
            P("rows", "cols", None),
            P(),
            P(),
        ),
        check_vma=False,
    )
```

```python
import functools
import math

import jax
import jax.numpy as jnp
import numpy as np
from jax import lax
from jax.experimental import pallas as pl
from jax.experimental.pallas import tpu as pltpu
from jax.sharding import PartitionSpec as P

G = 8
F = 256
ROWS = 32
WIDE = 64
STRIP = 48
MASK_ROWS = 16
BF = jnp.bfloat16
F32 = jnp.float32
VMEM = pl.BlockSpec(memory_space=pltpu.VMEM)
SMEM = pl.BlockSpec(memory_space=pltpu.SMEM)
HBM = pl.BlockSpec(memory_space=pltpu.HBM)


def inverse_of(element):
    return (4 - element % 4) % 4 if element < 4 else element


def product(first, second):
    mirror = (first // 4 + second // 4) % 2
    turns = (first % 4 + (1 - 2 * (first // 4)) * (second % 4)) % 4
    return mirror * 4 + turns


def act(element, row, col):
    if element // 4:
        col = -col
    for _ in range(element % 4):
        row, col = -col, row
    return row, col


def source_cell(elem, pos):
    row, col = act(inverse_of(elem), pos // 3 - 1, pos % 3 - 1)
    return (row + 1) * 3 + col + 1


def iota(shape, dim):
    return lax.broadcasted_iota(jnp.int32, shape, dim)


def one_hot(cond):
    return jnp.where(cond, 1.0, 0.0).astype(BF)


def permuted_index(index, elem):
    inverse = inverse_of(elem)
    mirror, turns = inverse // 4, inverse % 4
    second = index & 7
    new_mirror = (second >> 2) ^ mirror
    spin = second & 3
    new_turns = (turns + (-spin if mirror else spin)) & 3
    return (index & ~7) | (new_mirror << 2) | new_turns


def dot(lhs, rhs):
    return jnp.dot(lhs, rhs, preferred_element_type=F32)


def dot_nt(lhs, rhs):
    return lax.dot_general(lhs, rhs, (((1,), (1,)), ((), ())), preferred_element_type=F32)


def call(
    kernel, out_shape, n_in, scratch=(), specs=None, outs=None, flops=1 << 30, limit=24 << 20, name=None
):
    return pl.pallas_call(
        kernel,
        out_shape=out_shape,
        in_specs=specs or [VMEM] * n_in,
        out_specs=outs or jax.tree.map(lambda _: VMEM, out_shape),
        scratch_shapes=list(scratch),
        compiler_params=pltpu.CompilerParams(vmem_limit_bytes=limit),
        cost_estimate=pl.CostEstimate(flops=flops, bytes_accessed=4 << 20, transcendentals=0),
        name=name,
    )


def shape(dims, dtype=BF):
    return jax.ShapeDtypeStruct(dims, dtype)


def far(dims):
    return pltpu.HBM(dims, BF)


def kept(values):
    return pltpu.with_memory_space_constraint(values, pltpu.HBM)


def start_copies(pairs, semaphores):
    copies = [pltpu.make_async_copy(src, dst, semaphores.at[i]) for i, (src, dst) in enumerate(pairs)]
    for copy in copies:
        copy.start()
    return copies


def fill_mask_rows(tissue, mask_rows, tile_rows):
    same = iota((16, 16), 0) == iota((16, 16), 1)
    for tile_row in tile_rows:
        values = jnp.broadcast_to(tissue[tile_row : tile_row + 1, :].astype(F32), (16, 16))
        column = jnp.sum(jnp.where(same, values, 0.0), axis=1, keepdims=True)
        mask_rows[tile_row * 16 : tile_row * 16 + 16, :] = jnp.broadcast_to(column, (16, F))


def masked_rows(tile_row, half, low, skip, grad, mask_rows, low_at, at, merged, grad_two, put):
    spread = one_hot((iota((WIDE, 16), 0) >> 2) == iota((WIDE, 16), 1))
    twice = one_hot((iota((WIDE, 32), 0) >> 1) == iota((WIDE, 32), 1))
    mask = dot(spread, mask_rows[tile_row * 16 : tile_row * 16 + 16, :].astype(BF))
    coarse = dot(twice, low[low_at : low_at + 32, :])
    for sub in range(2):
        here, there = pl.ds(at + sub * WIDE, WIDE), pl.ds(put + sub * WIDE, WIDE)
        merged[there, :] = ((coarse + skip[here, :].astype(F32)) * mask).astype(BF)
        grad_two[there, :] = (grad[here, :].astype(F32) * mask).astype(BF)


def head_kernel(
    low_in, skip_in, grad_in, tissue_in, near, far_side, low, skip, grad, tissue, mask_rows, merged, grad_two,
    semaphores,
):
    two = 2 * WIDE
    last = ROWS * WIDE - two
    pairs = [(tissue_in, tissue)]
    for part in range(2):
        pairs.append((low_in.at[pl.ds(part * 480, 32)], low.at[pl.ds(part * 32, 32)]))
        pairs.append((skip_in.at[pl.ds(part * last, two)], skip.at[pl.ds(part * two, two)]))
        pairs.append((grad_in.at[pl.ds(part * last, two)], grad.at[pl.ds(part * two, two)]))
    for copy in start_copies(pairs, semaphores):
        copy.wait()
    fill_mask_rows(tissue, mask_rows, (0, 7))
    for part in range(2):
        masked_rows(
            part * 7, part, low, skip, grad, mask_rows, part * 32, part * two, merged, grad_two, part * two
        )
    odd = lax.axis_index("rows") % 2 == 1
    for at, source in ((0, merged), (two, grad_two)):
        head, tail = source[0:two, :], source[two : 2 * two, :]
        near[at : at + two, :] = jnp.where(odd, head, tail)
        far_side[at : at + two, :] = jnp.where(odd, tail, head)
    head, tail = mask_rows[0:16, :].astype(BF), mask_rows[112:128, :].astype(BF)
    near[2 * two : 2 * two + 16, :] = jnp.where(odd, head, tail)
    far_side[2 * two : 2 * two + 16, :] = jnp.where(odd, tail, head)


def build_weight(base, weight, forward):
    across = iota((F, F), 0)
    along = iota((F, F), 1)
    weave = one_hot(((across & 7) * 32 + (across >> 3)) == along)
    turned = [dot(base[...], one_hot(across == permuted_index(along, elem))).astype(BF) for elem in range(G)]
    for pos in range(9):
        rows = []
        for elem in range(G):
            cell = source_cell(elem, pos)
            rows.append(turned[elem][cell * 32 : cell * 32 + 32, :])
        woven = dot(weave, jnp.concatenate(rows, axis=0))
        if forward:
            weight[pos * F : (pos + 1) * F, :] = woven.T.astype(BF)
        else:
            weight[(8 - pos) * F : (9 - pos) * F, :] = woven.astype(BF)


def prepare_kernel(
    low_in, skip_in, grad_in, tissue_in, slots, filter_one, filter_two,
    merged, grad_two, mask_rows, fwd_one, bwd_two, places, slot_rows,
    low, skip, grad, tissue, semaphores,
):
    pairs = [(tissue_in, tissue)]
    for part in range(4):
        fine, coarse = pl.ds(part * 512, 512), pl.ds(part * 128, 128)
        pairs.append((low_in.at[coarse], low.at[coarse]))
        pairs.append((skip_in.at[fine], skip.at[fine]))
        pairs.append((grad_in.at[fine], grad.at[fine]))
    copies = start_copies(pairs, semaphores)
    flat = jnp.concatenate([slots[row : row + 1, :] for row in range(8)], axis=1)
    owner, local = flat >> 7, (flat & 127).astype(F32)
    tile = iota((128, 128), 1)
    match = owner == iota((128, 128), 0)
    index = tile.astype(F32)
    first = jnp.min(jnp.where(match, index, 1000.0), axis=1, keepdims=True)
    second = match & (index > first)
    used = jnp.sum(jnp.where(second, 1.0, 0.0), axis=0, keepdims=True)
    places[...] = jnp.broadcast_to(owner * 2 + used.astype(jnp.int32), (8, 128))
    slot_one = jnp.sum(jnp.where(match & (index == first), local + 1.0, 0.0), axis=1, keepdims=True)
    slot_two = jnp.sum(jnp.where(second, local + 1.0, 0.0), axis=1, keepdims=True)
    slot_rows[...] = jnp.where(tile == 0, slot_one, jnp.where(tile == 1, slot_two, 0.0)) - 1.0
    build_weight(filter_one, fwd_one, True)
    build_weight(filter_two, bwd_two, False)
    copies[0].wait()
    fill_mask_rows(tissue, mask_rows, range(8))
    for copy in copies[1:]:
        copy.wait()
    for low_row in range(16):
        at = low_row * 2 * WIDE
        masked_rows(
            low_row // 2, low_row % 2, low, skip, grad, mask_rows, low_row * 32, at, merged, grad_two, at
        )


def edge_kernel(
    merged, grad_two, near_in, far_in, mask_rows, left, right, top, bottom, near, far_side, tall, masks
):
    two = 2 * WIDE
    at_top = lax.axis_index("rows") == 0
    at_bottom = lax.axis_index("rows") == lax.axis_size("rows") - 1
    odd = lax.axis_index("rows") % 2 == 1
    zero = jnp.zeros((272, F), BF)
    top[...] = jnp.where(at_top, zero, jnp.where(odd, near_in[...], far_in[...]))
    bottom[...] = jnp.where(at_bottom, zero, jnp.where(odd, far_in[...], near_in[...]))
    tall[:, 36 * 16 : 48 * 16, :] = jnp.zeros((2, 12 * 16, 128), F32)

    def keep(row, values):
        for half in range(2):
            tall[half, row * 16 : row * 16 + 16, :] = values[:, half * 128 : half * 128 + 128].astype(F32)

    for side, (target, offset, picks, tile_col) in enumerate(
        ((left, 0, (0, 1), 0), (right, 48, (14, 15), 15))
    ):
        for image, source in enumerate((merged, grad_two)):
            for row in range(2):
                place = image * two + row * WIDE + offset
                keep(row, top[place : place + 16, :])
                keep(34 + row, bottom[place : place + 16, :])
            for row in range(ROWS):
                place = row * WIDE + offset
                keep(row + 2, source[place : place + 16, :])
            for col in range(2):
                strip = (image * 2 + col) * STRIP
                for half in range(2):
                    target[strip : strip + STRIP, half * 128 : half * 128 + 128] = tall[
                        half, pl.ds(picks[col], STRIP, stride=16), :
                    ].astype(BF)
        masks[...] = jnp.zeros((STRIP, F), F32)
        above = top[2 * two : 2 * two + 16, :].astype(F32)
        below = bottom[2 * two : 2 * two + 16, :].astype(F32)
        masks[0:2, :] = jnp.broadcast_to(above[tile_col : tile_col + 1, :], (2, F))
        masks[34:36, :] = jnp.broadcast_to(below[tile_col : tile_col + 1, :], (2, F))
        for tile_row in range(8):
            at = tile_row * 16 + tile_col
            masks[2 + 4 * tile_row : 6 + 4 * tile_row, :] = jnp.broadcast_to(mask_rows[at : at + 1, :], (4, F))
        target[4 * STRIP : 5 * STRIP, :] = masks[...].astype(BF)
    odd = lax.axis_index("cols") % 2 == 1
    near[...] = jnp.where(odd, left[...], right[...])
    far_side[...] = jnp.where(odd, right[...], left[...])


def shifted_store(target, at, value, plain, before, after):
    row = iota((WIDE, F), 0)
    target[pl.ds(at, WIDE), 0:F] = jnp.where(row == 0, before, pltpu.roll(value, 1, 0)).astype(BF)
    target[pl.ds(at, WIDE), F : 2 * F] = plain
    target[pl.ds(at, WIDE), 2 * F : 3 * F] = jnp.where(
        row == WIDE - 1, after, pltpu.roll(value, WIDE - 1, 0)
    ).astype(BF)


def conv(shifted, start, count, weight):
    lhs = jnp.concatenate([shifted[pl.ds(start + ky * WIDE, count), :] for ky in range(3)], axis=1)
    return dot(lhs, weight[...])


def interior_kernel(
    merged, grad_two, fwd_one, bwd_two, merged_shift, pre, grad_hidden, grad_ends, grad_shift
):
    nothing = jnp.zeros((1, F), F32)
    for source, target in ((merged, merged_shift), (grad_two, grad_shift)):

        def shift_row(row, _, source=source, target=target):
            at = pl.multiple_of(row * WIDE, WIDE)
            plain = source[pl.ds(at, WIDE), :]
            shifted_store(target, at, plain.astype(F32), plain, nothing, nothing)
            return 0

        lax.fori_loop(0, ROWS, shift_row, 0)

    pre[...] = conv(merged_shift, 0, 30 * WIDE, fwd_one)
    grad_hidden[...] = conv(grad_shift, 0, 30 * WIDE, bwd_two)
    grad_ends[0 : 2 * WIDE, :] = grad_shift[0 : 2 * WIDE, :]
    grad_ends[2 * WIDE : 4 * WIDE, :] = grad_shift[30 * WIDE : 32 * WIDE, :]


def patched_copy(source, source_at, target, target_at, before, after):
    row = iota((16, F), 0)
    target[pl.ds(target_at, WIDE), :] = source[pl.ds(source_at, WIDE), :]
    first = source[pl.ds(source_at, 16), 0:F].astype(F32)
    target[pl.ds(target_at, 16), 0:F] = jnp.where(row == 0, before, first).astype(BF)
    last = source[pl.ds(source_at + 48, 16), 2 * F : 3 * F].astype(F32)
    target[pl.ds(target_at + 48, 16), 2 * F : 3 * F] = jnp.where(row == 15, after, last).astype(BF)


def first_kernel(
    merged, grad_two, top, bottom, left, right, near, far_side, mask_rows, fwd_one, bwd_two,
    merged_inner, pre, grad_hidden, grad_ends,
    hidden_out, pre_out, edge, message,
    hidden_shift, pre_shift, mask_wide, merged_shift, grad_edges, strips, pre_edge, grad_edge, correction, folded, semaphores,
):
    at_left = lax.axis_index("cols") == 0
    at_right = lax.axis_index("cols") == lax.axis_size("cols") - 1
    odd = lax.axis_index("cols") % 2 == 1
    zero = jnp.zeros((STRIP, F), F32)

    def left_strip(index):
        here = slice(index * STRIP, (index + 1) * STRIP)
        value = jnp.where(odd, near[here, :], far_side[here, :])
        return jnp.where(at_left, zero, value.astype(F32))

    def right_strip(index):
        here = slice(index * STRIP, (index + 1) * STRIP)
        value = jnp.where(odd, far_side[here, :], near[here, :])
        return jnp.where(at_right, zero, value.astype(F32))

    two = 2 * WIDE
    spread = one_hot((iota((WIDE, 16), 0) >> 2) == iota((WIDE, 16), 1))
    mask_wide[0:WIDE, :] = dot(spread, top[2 * two : 2 * two + 16, :])
    mask_wide[9 * WIDE : 10 * WIDE, :] = dot(spread, bottom[2 * two : 2 * two + 16, :])
    for tile_row in range(8):
        mask_wide[(tile_row + 1) * WIDE : (tile_row + 2) * WIDE, :] = dot(
            spread, mask_rows[tile_row * 16 : tile_row * 16 + 16, :].astype(BF)
        )
    strip_pre = []
    quad = 4 * WIDE
    for image, (weight, result) in enumerate(((fwd_one, pre_edge), (bwd_two, grad_edge))):
        first = image * 2
        columns = (
            left_strip(first),
            left_strip(first + 1),
            left[first * STRIP : (first + 1) * STRIP, :].astype(F32),
            right[(first + 1) * STRIP : (first + 2) * STRIP, :].astype(F32),
            right_strip(first),
            right_strip(first + 1),
        )
        for index, column in enumerate(columns):
            strips[index * STRIP : (index + 1) * STRIP, :] = column

        def before(row):
            return strips[pl.ds(STRIP + row, 1), :]

        def after(row):
            return strips[pl.ds(4 * STRIP + row, 1), :]

        for row in range(2):
            at = image * two + row * WIDE
            for halo, place, edge_at in ((top, row, row), (bottom, 34 + row, 6 + row)):
                plain = halo[at : at + WIDE, :]
                target, where_to = (grad_edges, edge_at) if image else (merged_shift, place)
                shifted_store(
                    target, where_to * WIDE, plain.astype(F32), plain, before(place), after(place)
                )
        if image:
            for row in range(4):
                place = (2, 3, 32, 33)[row]
                patched_copy(grad_ends, row * WIDE, grad_edges, (2 + row) * WIDE, before(place), after(place))
            ends = [grad_edges[ky * WIDE : ky * WIDE + two, :] for ky in range(3)]
            tails = [grad_edges[quad + ky * WIDE : quad + ky * WIDE + two, :] for ky in range(3)]
        else:

            def patch(row, _):
                patched_copy(
                    merged_inner, pl.multiple_of(row * WIDE, WIDE), merged_shift,
                    pl.multiple_of((row + 2) * WIDE, WIDE), before(row + 2), after(row + 2),
                )
                return 0

            lax.fori_loop(0, ROWS, patch, 0)
            ends = [merged_shift[ky * WIDE : ky * WIDE + two, :] for ky in range(3)]
            tails = [merged_shift[(32 + ky) * WIDE : (32 + ky) * WIDE + two, :] for ky in range(3)]
        lhs = jnp.concatenate([jnp.concatenate(ends, axis=1), jnp.concatenate(tails, axis=1)], axis=0)
        result[...] = dot(lhs, weight[...])
        row = iota((40, F), 0)
        inner = (row >= 2) & (row < 32)
        for side, (index, kx) in enumerate(((1, 0), (4, 2))):
            column = jnp.concatenate(
                [strips[index * STRIP + ky : index * STRIP + ky + 40, :] for ky in range(3)], axis=1
            ).astype(BF)
            taps = jnp.concatenate(
                [weight[(ky * 3 + kx) * F : (ky * 3 + kx + 1) * F, :] for ky in range(3)], axis=0
            )
            at = (image * 2 + side) * 40
            correction[at : at + 40, :] = jnp.where(inner, dot(column, taps), 0.0)
        parts = []
        for ky in range(3):
            for kx in range(3):
                parts.append(
                    jnp.concatenate(
                        [
                            strips[kx * STRIP + ky : kx * STRIP + ky + 40, :],
                            strips[(kx + 3) * STRIP + ky : (kx + 3) * STRIP + ky + 40, :],
                        ],
                        axis=0,
                    ).astype(BF)
                )
        strip_pre.append(dot(jnp.concatenate(parts, axis=1), weight[...]))
    strips[0:STRIP, :] = left_strip(4)
    strips[STRIP : 2 * STRIP, :] = right_strip(4)
    strip_mask = jnp.concatenate([strips[1:41, :], strips[STRIP + 1 : STRIP + 41, :]], axis=0)
    sigma = jax.nn.sigmoid(strip_pre[0])
    edge[0:80, :] = (strip_pre[0] * sigma * strip_mask).astype(BF).astype(F32)
    edge[80:160, :] = (
        (strip_pre[1] * (sigma * (1.0 + strip_pre[0] * (1.0 - sigma))) * strip_mask).astype(BF).astype(F32)
    )

    column = iota((WIDE, F), 0)

    def activate(row, _, pre_from=None, grad_from=None, source_row=0):
        at = pl.multiple_of(row * WIDE, WIDE)
        here = pl.ds(pl.multiple_of((row - source_row) * WIDE, WIDE), WIDE)

        def corrected(value, base):
            value = jnp.where(column == 0, value + correction[pl.ds(base + row, 1), :], value)
            return jnp.where(column == WIDE - 1, value + correction[pl.ds(base + 40 + row, 1), :], value)

        mask = mask_wide[pl.ds(pl.multiple_of(((row + 3) >> 2) * WIDE, WIDE), WIDE), :]
        value = corrected(pre_from[here, :], 0)
        sigma = jax.nn.sigmoid(value)
        hidden = value * sigma * mask
        slope = sigma * (1.0 + value * (1.0 - sigma))
        grad_value = corrected(grad_from[here, :], 80) * slope * mask
        shifted_store(
            hidden_shift, at, hidden, hidden.astype(BF), edge[pl.ds(row, 1), :], edge[pl.ds(40 + row, 1), :]
        )
        shifted_store(
            pre_shift, at, grad_value, grad_value.astype(BF),
            edge[pl.ds(80 + row, 1), :], edge[pl.ds(120 + row, 1), :],
        )
        return 0

    ends = functools.partial(activate, pre_from=pre_edge, grad_from=grad_edge)
    lax.fori_loop(0, 2, functools.partial(ends, source_row=0), 0)
    lax.fori_loop(2, 32, functools.partial(activate, pre_from=pre, grad_from=grad_hidden, source_row=2), 0)
    lax.fori_loop(32, 34, functools.partial(ends, source_row=30), 0)
    copies = start_copies(
        [(hidden_shift.at[:, F : 2 * F], hidden_out), (pre_shift.at[:, F : 2 * F], pre_out)], semaphores
    )
    across = iota((F, F), 0)
    along = iota((F, F), 1)
    unweave = one_hot(((along & 7) * 32 + (along >> 3)) == across)
    perms = [one_hot(along == permuted_index(across, elem)) for elem in range(G)]
    back = jnp.concatenate(perms, axis=0)
    for index, (values, grads, skip) in enumerate(
        (
            (merged_shift, pre_shift[WIDE : 33 * WIDE, F : 2 * F], WIDE),
            (hidden_shift, grad_two[...], 0),
        )
    ):
        turned = dot_nt(unweave, grads).astype(BF)
        full = []
        for ky in range(3):
            start = skip + ky * WIDE
            full.append(dot(turned, values[start : start + ROWS * WIDE, :]).astype(BF))
        pieces = []
        for elem in range(G):
            of_cell = {source_cell(elem, pos): pos for pos in range(9)}
            rows = []
            for cell in range(9):
                pos = of_cell[cell]
                kx = pos % 3
                rows.append(full[pos // 3][elem * 32 : elem * 32 + 32, kx * F : (kx + 1) * F])
            pieces.append(jnp.concatenate(rows, axis=0))
        folded[index * 288 : (index + 1) * 288, :] = dot(jnp.concatenate(pieces, axis=1), back)
    folded[576:592, :] = jnp.zeros((16, F), F32)
    for part in range(128):
        start, lanes = 9 * (part % 64), (part // 64) * 128
        data = folded[start : start + 16, lanes : lanes + 128].reshape(4, 4, 128)
        message[part] = data[0:3].astype(BF)
    for copy in copies:
        copy.wait()


def wide_mask(mask_rows, step):
    spread = one_hot((iota((WIDE, 16), 0) >> 2) == iota((WIDE, 16), 1))
    parts = []
    for tile_row in range(4):
        at = pl.multiple_of((step * 4 + tile_row) * 16, 16)
        parts.extend([dot(spread, mask_rows[pl.ds(at, 16), :].astype(BF))] * 4)
    return jnp.concatenate(parts, axis=0)


def load_shifted(values, filter_in, edges, base, plain, filter_held, weight, forward, shifted, semaphores):
    cuts = (0, 640, 1152, 1664, 2176)
    pairs = [(filter_in, filter_held)]
    for first, last in zip(cuts[:-1], cuts[1:]):
        pairs.append((values.at[pl.ds(first, last - first)], plain.at[pl.ds(first, last - first)]))
    copies = start_copies(pairs, semaphores)

    def row_of(row, _):
        at = pl.multiple_of(row * WIDE, WIDE)
        value = plain[pl.ds(at, WIDE), :]
        shifted_store(
            shifted, at, value.astype(F32), value,
            edges[pl.ds(base + row, 1), :], edges[pl.ds(base + 40 + row, 1), :],
        )
        return 0

    copies[0].wait()
    build_weight(filter_held, weight, forward)
    for copy in copies[1:]:
        copy.wait()
    lax.fori_loop(0, ROWS + 2, row_of, 0)


def backward_kernel(
    pre_in, filter_in, edges, mask_rows, tiles, low_grad,
    pair, plain, filter_held, bwd_one, pre_shift, semaphores,
):
    two = 2 * WIDE
    load_shifted(pre_in, filter_in, edges, 80, plain, filter_held, bwd_one, False, pre_shift, semaphores)
    order = iota((F, F), 0)
    tile_order = one_hot(
        iota((F, F), 1) == (((order >> 2) & 3) * WIDE + (order >> 4) * 4 + (order & 3))
    )

    def body(step, _):
        at = pl.multiple_of(step * 1024, 1024)
        grad_merged = conv(pre_shift, at, 1024, bwd_one) * wide_mask(mask_rows, step)
        rounded = grad_merged.astype(BF)
        for tile_row in range(4):
            tiles[pl.ds(at + tile_row * F, F), :] = dot(
                tile_order, rounded[tile_row * F : (tile_row + 1) * F, :]
            ).astype(BF)
        for row in range(8):
            both = grad_merged[row * two : row * two + WIDE, :] + grad_merged[row * two + WIDE : row * two + two, :]
            for half in range(2):
                pair[half, row * WIDE : (row + 1) * WIDE, :] = both[:, half * 128 : half * 128 + 128]
        for half in range(2):
            low_grad[pl.ds(pl.multiple_of(step * 256, 256), 256), half * 128 : half * 128 + 128] = (
                pair[half, pl.ds(0, 256, stride=2), :] + pair[half, pl.ds(1, 256, stride=2), :]
            ).astype(BF)
        return 0

    lax.fori_loop(0, 2, body, 0)


def forward_kernel(
    hidden_in, filter_in, edges, mask_rows, output, plain, filter_held, fwd_two, hidden_shift, semaphores
):
    load_shifted(hidden_in, filter_in, edges, 0, plain, filter_held, fwd_two, True, hidden_shift, semaphores)

    def body(step, _):
        at = pl.multiple_of(step * 1024, 1024)
        output[pl.ds(at, 1024), :] = (
            conv(hidden_shift, at, 1024, fwd_two) * wide_mask(mask_rows, step)
        ).astype(BF)
        return 0

    lax.fori_loop(0, 2, body, 0)


def pack_kernel(places, tiles, send):
    def copy(group, _):
        for sub in range(8):
            tile = group * 8 + sub
            place = places[0, tile]
            for half in range(2):
                value = tiles[pl.ds(pl.multiple_of(tile * 16, 16), 16), half * 128 : half * 128 + 128]
                send[place >> 1, pl.ds((place & 1) * 8 + half * 4, 4)] = value.reshape(4, 4, 128)
        return 0

    lax.fori_loop(0, 16, copy, 0)


def terms_kernel(send_in, got, slot_rows, send, rows, semaphore):
    total = jnp.zeros((3, 4, 128), F32)
    for part in range(128):
        total = total + got[part].astype(F32)
    front = total[0:2].astype(BF)
    row = iota((4, 128), 0)
    for part in range(128):
        rows[part, 0:2] = front
        rows[part, 2] = jnp.where(row == 1, slot_rows[part : part + 1, :], total[2]).astype(BF)
    copy = pltpu.make_async_copy(rows, send.at[:, pl.ds(16, 3)], semaphore)
    copy.start()
    copy.wait()


def place_kernel(scale, got, skip_grad, one, two, gathered, sources, folded, table, semaphore):
    for part in range(128):
        start, lanes = 9 * (part % 64), (part // 64) * 128
        terms = got[part, 16:19].astype(F32)
        folded[start : start + 4, lanes : lanes + 128] = terms[0] * scale
        folded[start + 4 : start + 8, lanes : lanes + 128] = terms[1] * scale
        folded[start + 8 : start + 9, lanes : lanes + 128] = terms[2, 0:1] * scale
        gathered[part : part + 1, :] = terms[2, 1:2]
    one[...] = folded[0:288, :]
    two[...] = folded[288:576, :]
    slots = gathered[...].T
    wanted = iota((128, 128), 0).astype(F32)
    index = iota((128, 128), 1).astype(F32)
    source = jnp.zeros((128, 128), F32)
    for which in range(2):
        source = source + jnp.where(slots[which : which + 1, :] == wanted, index * 2.0 + which, 0.0)
    sources[...] = jnp.broadcast_to(jnp.sum(source, axis=1, keepdims=True), (128, 128)).T[0:8, :].astype(jnp.int32)
    copy = pltpu.make_async_copy(sources, table, semaphore)
    copy.start()
    copy.wait()

    def put(group, _):
        for sub in range(8):
            slot = group * 8 + sub
            place = table[0, slot]
            for half in range(2):
                skip_grad[slot, :, :, half * 128 : half * 128 + 128] = got[
                    place >> 1, pl.ds((place & 1) * 8 + half * 4, 4)
                ]
        return 0

    lax.fori_loop(0, 16, put, 0)


def swap(values, axis, first):
    size = lax.axis_size(axis)
    partner = list(range(size))
    for index in range(first, size - 1, 2):
        partner[index], partner[index + 1] = index + 1, index
    return lax.ppermute(values, axis, list(enumerate(partner)))


def on_device(low_feats, skip_feats, tissue_mask, owner_slot, filter_one, filter_two, out_grad):
    everyone = ("rows", "cols")
    height, breadth, features = skip_feats.shape
    pixels = height * breadth
    given = (
        kept(low_feats.reshape(-1, F)), kept(skip_feats.reshape(pixels, F)),
        kept(out_grad.reshape(pixels, F)), kept(tissue_mask),
    )
    near, far_side = call(
        head_kernel, [shape((272, F))] * 2, 4,
        [
            pltpu.VMEM((64, F), BF), pltpu.VMEM((4 * WIDE, F), BF), pltpu.VMEM((4 * WIDE, F), BF),
            pltpu.VMEM((8, 16), jnp.int32), pltpu.VMEM((128, F), F32), pltpu.VMEM((4 * WIDE, F), BF),
            pltpu.VMEM((4 * WIDE, F), BF), pltpu.SemaphoreType.DMA((7,)),
        ],
        specs=[HBM] * 4, name="head",
    )(*given)
    near_rows = swap(near, "rows", 0)
    far_rows = swap(far_side, "rows", 1)
    bases = [f.transpose(1, 2, 0, 3).reshape(288, F) for f in (filter_one, filter_two)]
    merged, grad_two, mask_rows, fwd_one, bwd_two, places, slot_rows = call(
        prepare_kernel,
        [
            shape((pixels, F)), shape((pixels, F)), shape((128, F), F32), shape((9 * F, F)),
            shape((9 * F, F)), shape((8, 128), jnp.int32), shape((128, 128), F32),
        ],
        7,
        [
            pltpu.VMEM((pixels // 4, F), BF), pltpu.VMEM((pixels, F), BF), pltpu.VMEM((pixels, F), BF),
            pltpu.VMEM((8, 16), jnp.int32), pltpu.SemaphoreType.DMA((13,)),
        ],
        specs=[HBM] * 4 + [VMEM] * 3, flops=3 << 30, name="prepare",
    )(*given, owner_slot, *bases)
    left, right, top, bottom, near, far_side = call(
        edge_kernel,
        [shape((5 * STRIP, F))] * 2 + [shape((272, F))] * 2 + [shape((5 * STRIP, F))] * 2,
        5, [pltpu.VMEM((2, 48 * 16, 128), F32), pltpu.VMEM((STRIP, F), F32)], name="edge",
    )(merged, grad_two, near_rows, far_rows, mask_rows)
    near_cols = swap(near, "cols", 0)
    far_cols = swap(far_side, "cols", 1)
    inner = call(
        interior_kernel,
        [
            shape((pixels, 3 * F)), shape((30 * WIDE, F), F32), shape((30 * WIDE, F), F32),
            shape((4 * WIDE, 3 * F)),
        ],
        4, [pltpu.VMEM((pixels, 3 * F), BF)], flops=5 << 30, limit=16 << 20, name="interior",
    )(merged, grad_two, fwd_one, bwd_two)
    hidden, grad_pre, edges, message = call(
        first_kernel,
        [far((34 * WIDE, F)), far((34 * WIDE, F)), shape((160, F), F32), shape((128, 3, 4, 128))],
        15,
        [
            pltpu.VMEM((34 * WIDE, 3 * F), BF), pltpu.VMEM((34 * WIDE, 3 * F), BF),
            pltpu.VMEM((10 * WIDE, F), F32),
            pltpu.VMEM((36 * WIDE, 3 * F), BF), pltpu.VMEM((8 * WIDE, 3 * F), BF),
            pltpu.VMEM((6 * STRIP, F), F32),
            pltpu.VMEM((4 * WIDE, F), F32), pltpu.VMEM((4 * WIDE, F), F32), pltpu.VMEM((160, F), F32),
            pltpu.VMEM((592, F), F32), pltpu.SemaphoreType.DMA((2,)),
        ],
        outs=[HBM, HBM, VMEM, VMEM], flops=10 << 30, limit=36 << 20, name="first",
    )(merged, grad_two, top, bottom, left, right, near_cols, far_cols, mask_rows, fwd_one, bwd_two, *inner)
    got_terms = lax.all_to_all(message, everyone, 0, 0, tiled=True)
    loading = [
        pltpu.VMEM((34 * WIDE, F), BF), pltpu.VMEM((288, F), BF), pltpu.VMEM((9 * F, F), BF),
        pltpu.VMEM((34 * WIDE, 3 * F), BF), pltpu.SemaphoreType.DMA((5,)),
    ]
    tiles, low_grad = call(
        backward_kernel, [shape((pixels, F)), shape((pixels // 4, F))], 4,
        [pltpu.VMEM((2, 8 * WIDE, 128), F32)] + loading, specs=[HBM, HBM, VMEM, VMEM],
        flops=3 << 30, name="backward",
    )(kept(grad_pre), kept(bases[0]), edges, mask_rows)
    output = call(
        forward_kernel, shape((pixels, F)), 4, loading, specs=[HBM, HBM, VMEM, VMEM],
        flops=3 << 30, name="forward",
    )(kept(hidden), kept(bases[1]), edges, mask_rows)
    send = call(pack_kernel, far((128, 19, 4, 128)), 2, specs=[SMEM, VMEM], name="pack")(places, tiles)
    send = pl.pallas_call(
        terms_kernel,
        out_shape=far((128, 19, 4, 128)),
        in_specs=[HBM, VMEM, VMEM],
        out_specs=HBM,
        scratch_shapes=[pltpu.VMEM((128, 3, 4, 128), BF), pltpu.SemaphoreType.DMA],
        input_output_aliases={0: 0},
        compiler_params=pltpu.CompilerParams(vmem_limit_bytes=24 << 20),
        cost_estimate=pl.CostEstimate(flops=1 << 30, bytes_accessed=4 << 20, transcendentals=0),
        name="terms",
    )(kept(send), got_terms, slot_rows)
    got = lax.all_to_all(send, everyone, 0, 0, tiled=True)
    scale = 1.0 / math.sqrt(pixels * lax.axis_size("rows") * lax.axis_size("cols"))
    skip_grad, one, two = call(
        functools.partial(place_kernel, scale),
        [shape((128, 4, 4, F)), shape((288, F), F32), shape((288, F), F32)], 1,
        [
            pltpu.VMEM((128, 128), F32), pltpu.VMEM((8, 128), jnp.int32), pltpu.VMEM((592, F), F32),
            pltpu.SMEM((8, 128), jnp.int32), pltpu.SemaphoreType.DMA,
        ],
        name="place",
    )(got)
    return (
        output.reshape(height, breadth, F),
        skip_grad,
        low_grad.reshape(height // 2, breadth // 2, F),
        one.reshape(3, 3, 32, F).transpose(2, 0, 1, 3),
        two.reshape(3, 3, 32, F).transpose(2, 0, 1, 3),
    )


def solution(mesh):
    placed = (
        P("rows", "cols", None),
        P("rows", "cols", None),
        P("rows", "cols"),
        P("rows", "cols"),
        P(),
        P(),
        P("rows", "cols", None),
    )
    return jax.shard_map(
        on_device,
        mesh=mesh,
        in_specs=placed,
        out_specs=(
            P("rows", "cols", None),
            P(("rows", "cols"), None, None, None),
            P("rows", "cols", None),
            P(),
            P(),
        ),
        check_vma=False,
    )
```

```python
import functools
import math

import jax
import jax.numpy as jnp
import numpy as np
from jax import lax
from jax.experimental import pallas as pl
from jax.experimental.pallas import tpu as pltpu
from jax.sharding import PartitionSpec as P

G = 8
F = 256
ROWS = 32
WIDE = 64
STRIP = 48
MASK_ROWS = 16
BF = jnp.bfloat16
F32 = jnp.float32
VMEM = pl.BlockSpec(memory_space=pltpu.VMEM)
SMEM = pl.BlockSpec(memory_space=pltpu.SMEM)
HBM = pl.BlockSpec(memory_space=pltpu.HBM)


def inverse_of(element):
    return (4 - element % 4) % 4 if element < 4 else element


def product(first, second):
    mirror = (first // 4 + second // 4) % 2
    turns = (first % 4 + (1 - 2 * (first // 4)) * (second % 4)) % 4
    return mirror * 4 + turns


def act(element, row, col):
    if element // 4:
        col = -col
    for _ in range(element % 4):
        row, col = -col, row
    return row, col


def source_cell(elem, pos):
    row, col = act(inverse_of(elem), pos // 3 - 1, pos % 3 - 1)
    return (row + 1) * 3 + col + 1


def iota(shape, dim):
    return lax.broadcasted_iota(jnp.int32, shape, dim)


def one_hot(cond):
    return jnp.where(cond, 1.0, 0.0).astype(BF)


def permuted_index(index, elem):
    inverse = inverse_of(elem)
    mirror, turns = inverse // 4, inverse % 4
    second = index & 7
    new_mirror = (second >> 2) ^ mirror
    spin = second & 3
    new_turns = (turns + (-spin if mirror else spin)) & 3
    return (index & ~7) | (new_mirror << 2) | new_turns


def dot(lhs, rhs):
    return jnp.dot(lhs, rhs, preferred_element_type=F32)


def dot_nt(lhs, rhs):
    return lax.dot_general(lhs, rhs, (((1,), (1,)), ((), ())), preferred_element_type=F32)


def call(
    kernel, out_shape, n_in, scratch=(), specs=None, outs=None, flops=1 << 30, limit=24 << 20, name=None
):
    return pl.pallas_call(
        kernel,
        out_shape=out_shape,
        in_specs=specs or [VMEM] * n_in,
        out_specs=outs or jax.tree.map(lambda _: VMEM, out_shape),
        scratch_shapes=list(scratch),
        compiler_params=pltpu.CompilerParams(vmem_limit_bytes=limit),
        cost_estimate=pl.CostEstimate(flops=flops, bytes_accessed=4 << 20, transcendentals=0),
        name=name,
    )


def shape(dims, dtype=BF):
    return jax.ShapeDtypeStruct(dims, dtype)


def far(dims):
    return pltpu.HBM(dims, BF)


def kept(values):
    return pltpu.with_memory_space_constraint(values, pltpu.HBM)


def start_copies(pairs, semaphores):
    copies = [pltpu.make_async_copy(src, dst, semaphores.at[i]) for i, (src, dst) in enumerate(pairs)]
    for copy in copies:
        copy.start()
    return copies


def fill_mask_rows(tissue, mask_rows, tile_rows):
    same = iota((16, 16), 0) == iota((16, 16), 1)
    for tile_row in tile_rows:
        values = jnp.broadcast_to(tissue[tile_row : tile_row + 1, :].astype(F32), (16, 16))
        column = jnp.sum(jnp.where(same, values, 0.0), axis=1, keepdims=True)
        mask_rows[tile_row * 16 : tile_row * 16 + 16, :] = jnp.broadcast_to(column, (16, F))


def masked_rows(tile_row, half, low, skip, grad, mask_rows, low_at, at, merged, grad_two, put):
    spread = one_hot((iota((WIDE, 16), 0) >> 2) == iota((WIDE, 16), 1))
    twice = one_hot((iota((WIDE, 32), 0) >> 1) == iota((WIDE, 32), 1))
    mask = dot(spread, mask_rows[tile_row * 16 : tile_row * 16 + 16, :].astype(BF))
    coarse = dot(twice, low[low_at : low_at + 32, :])
    for sub in range(2):
        here, there = pl.ds(at + sub * WIDE, WIDE), pl.ds(put + sub * WIDE, WIDE)
        merged[there, :] = ((coarse + skip[here, :].astype(F32)) * mask).astype(BF)
        grad_two[there, :] = (grad[here, :].astype(F32) * mask).astype(BF)


def head_kernel(
    low_in, skip_in, grad_in, tissue_in, near, far_side, low, skip, grad, tissue, mask_rows, merged, grad_two,
    semaphores,
):
    two = 2 * WIDE
    last = ROWS * WIDE - two
    pairs = [(tissue_in, tissue)]
    for part in range(2):
        pairs.append((low_in.at[pl.ds(part * 480, 32)], low.at[pl.ds(part * 32, 32)]))
        pairs.append((skip_in.at[pl.ds(part * last, two)], skip.at[pl.ds(part * two, two)]))
        pairs.append((grad_in.at[pl.ds(part * last, two)], grad.at[pl.ds(part * two, two)]))
    for copy in start_copies(pairs, semaphores):
        copy.wait()
    fill_mask_rows(tissue, mask_rows, (0, 7))
    for part in range(2):
        masked_rows(
            part * 7, part, low, skip, grad, mask_rows, part * 32, part * two, merged, grad_two, part * two
        )
    odd = lax.axis_index("rows") % 2 == 1
    for at, source in ((0, merged), (two, grad_two)):
        head, tail = source[0:two, :], source[two : 2 * two, :]
        near[at : at + two, :] = jnp.where(odd, head, tail)
        far_side[at : at + two, :] = jnp.where(odd, tail, head)
    head, tail = mask_rows[0:16, :].astype(BF), mask_rows[112:128, :].astype(BF)
    near[2 * two : 2 * two + 16, :] = jnp.where(odd, head, tail)
    far_side[2 * two : 2 * two + 16, :] = jnp.where(odd, tail, head)


def build_weight(base, weight, forward):
    across = iota((F, F), 0)
    along = iota((F, F), 1)
    weave = one_hot(((across & 7) * 32 + (across >> 3)) == along)
    turned = [dot(base[...], one_hot(across == permuted_index(along, elem))).astype(BF) for elem in range(G)]
    for pos in range(9):
        rows = []
        for elem in range(G):
            cell = source_cell(elem, pos)
            rows.append(turned[elem][cell * 32 : cell * 32 + 32, :])
        woven = dot(weave, jnp.concatenate(rows, axis=0))
        if forward:
            weight[pos * F : (pos + 1) * F, :] = woven.T.astype(BF)
        else:
            weight[(8 - pos) * F : (9 - pos) * F, :] = woven.astype(BF)


def prepare_kernel(
    low_in, skip_in, grad_in, tissue_in, slots, filter_one, filter_two,
    merged, grad_two, mask_rows, fwd_one, bwd_two, places, slot_rows,
    low, skip, grad, tissue, semaphores,
):
    pairs = [(tissue_in, tissue)]
    for part in range(4):
        fine, coarse = pl.ds(part * 512, 512), pl.ds(part * 128, 128)
        pairs.append((low_in.at[coarse], low.at[coarse]))
        pairs.append((skip_in.at[fine], skip.at[fine]))
        pairs.append((grad_in.at[fine], grad.at[fine]))
    copies = start_copies(pairs, semaphores)
    flat = jnp.concatenate([slots[row : row + 1, :] for row in range(8)], axis=1)
    owner, local = flat >> 7, (flat & 127).astype(F32)
    tile = iota((128, 128), 1)
    match = owner == iota((128, 128), 0)
    index = tile.astype(F32)
    first = jnp.min(jnp.where(match, index, 1000.0), axis=1, keepdims=True)
    second = match & (index > first)
    used = jnp.sum(jnp.where(second, 1.0, 0.0), axis=0, keepdims=True)
    places[...] = jnp.broadcast_to(owner * 2 + used.astype(jnp.int32), (8, 128))
    slot_one = jnp.sum(jnp.where(match & (index == first), local + 1.0, 0.0), axis=1, keepdims=True)
    slot_two = jnp.sum(jnp.where(second, local + 1.0, 0.0), axis=1, keepdims=True)
    slot_rows[...] = jnp.where(tile == 0, slot_one, jnp.where(tile == 1, slot_two, 0.0)) - 1.0
    build_weight(filter_one, fwd_one, True)
    build_weight(filter_two, bwd_two, False)
    copies[0].wait()
    fill_mask_rows(tissue, mask_rows, range(8))
    for copy in copies[1:]:
        copy.wait()
    for low_row in range(16):
        at = low_row * 2 * WIDE
        masked_rows(
            low_row // 2, low_row % 2, low, skip, grad, mask_rows, low_row * 32, at, merged, grad_two, at
        )


def edge_kernel(
    merged, grad_two, near_in, far_in, mask_rows, left, right, top, bottom, near, far_side, tall, masks
):
    two = 2 * WIDE
    at_top = lax.axis_index("rows") == 0
    at_bottom = lax.axis_index("rows") == lax.axis_size("rows") - 1
    odd = lax.axis_index("rows") % 2 == 1
    zero = jnp.zeros((272, F), BF)
    top[...] = jnp.where(at_top, zero, jnp.where(odd, near_in[...], far_in[...]))
    bottom[...] = jnp.where(at_bottom, zero, jnp.where(odd, far_in[...], near_in[...]))
    tall[:, 36 * 16 : 48 * 16, :] = jnp.zeros((2, 12 * 16, 128), F32)

    def keep(row, values):
        for half in range(2):
            tall[half, row * 16 : row * 16 + 16, :] = values[:, half * 128 : half * 128 + 128].astype(F32)

    for side, (target, offset, picks, tile_col) in enumerate(
        ((left, 0, (0, 1), 0), (right, 48, (14, 15), 15))
    ):
        for image, source in enumerate((merged, grad_two)):
            for row in range(2):
                place = image * two + row * WIDE + offset
                keep(row, top[place : place + 16, :])
                keep(34 + row, bottom[place : place + 16, :])
            for row in range(ROWS):
                place = row * WIDE + offset
                keep(row + 2, source[place : place + 16, :])
            for col in range(2):
                strip = (image * 2 + col) * STRIP
                for half in range(2):
                    target[strip : strip + STRIP, half * 128 : half * 128 + 128] = tall[
                        half, pl.ds(picks[col], STRIP, stride=16), :
                    ].astype(BF)
        masks[...] = jnp.zeros((STRIP, F), F32)
        above = top[2 * two : 2 * two + 16, :].astype(F32)
        below = bottom[2 * two : 2 * two + 16, :].astype(F32)
        masks[0:2, :] = jnp.broadcast_to(above[tile_col : tile_col + 1, :], (2, F))
        masks[34:36, :] = jnp.broadcast_to(below[tile_col : tile_col + 1, :], (2, F))
        for tile_row in range(8):
            at = tile_row * 16 + tile_col
            masks[2 + 4 * tile_row : 6 + 4 * tile_row, :] = jnp.broadcast_to(mask_rows[at : at + 1, :], (4, F))
        target[4 * STRIP : 5 * STRIP, :] = masks[...].astype(BF)
    odd = lax.axis_index("cols") % 2 == 1
    near[...] = jnp.where(odd, left[...], right[...])
    far_side[...] = jnp.where(odd, right[...], left[...])


def shifted_store(target, at, value, plain, before, after):
    row = iota((WIDE, F), 0)
    target[pl.ds(at, WIDE), 0:F] = jnp.where(row == 0, before, pltpu.roll(value, 1, 0)).astype(BF)
    target[pl.ds(at, WIDE), F : 2 * F] = plain
    target[pl.ds(at, WIDE), 2 * F : 3 * F] = jnp.where(
        row == WIDE - 1, after, pltpu.roll(value, WIDE - 1, 0)
    ).astype(BF)


def conv(shifted, start, count, weight):
    lhs = jnp.concatenate([shifted[pl.ds(start + ky * WIDE, count), :] for ky in range(3)], axis=1)
    return dot(lhs, weight[...])


def interior_kernel(
    merged, grad_two, fwd_one, bwd_two, merged_shift, pre, grad_hidden, grad_ends, grad_shift
):
    nothing = jnp.zeros((1, F), F32)
    for source, target in ((merged, merged_shift), (grad_two, grad_shift)):

        def shift_row(row, _, source=source, target=target):
            at = pl.multiple_of(row * WIDE, WIDE)
            plain = source[pl.ds(at, WIDE), :]
            shifted_store(target, at, plain.astype(F32), plain, nothing, nothing)
            return 0

        lax.fori_loop(0, ROWS, shift_row, 0, unroll=4)

    pre[...] = conv(merged_shift, 0, 30 * WIDE, fwd_one)
    grad_hidden[...] = conv(grad_shift, 0, 30 * WIDE, bwd_two)
    grad_ends[0 : 2 * WIDE, :] = grad_shift[0 : 2 * WIDE, :]
    grad_ends[2 * WIDE : 4 * WIDE, :] = grad_shift[30 * WIDE : 32 * WIDE, :]


def patched_copy(source, source_at, target, target_at, before, after):
    row = iota((16, F), 0)
    target[pl.ds(target_at, WIDE), :] = source[pl.ds(source_at, WIDE), :]
    first = source[pl.ds(source_at, 16), 0:F].astype(F32)
    target[pl.ds(target_at, 16), 0:F] = jnp.where(row == 0, before, first).astype(BF)
    last = source[pl.ds(source_at + 48, 16), 2 * F : 3 * F].astype(F32)
    target[pl.ds(target_at + 48, 16), 2 * F : 3 * F] = jnp.where(row == 15, after, last).astype(BF)


def first_kernel(
    merged, grad_two, top, bottom, left, right, near, far_side, mask_rows, fwd_one, bwd_two,
    merged_inner, pre, grad_hidden, grad_ends,
    hidden_out, pre_out, edge, message,
    hidden_shift, pre_shift, mask_wide, merged_shift, grad_edges, strips, pre_edge, grad_edge, correction, folded, semaphores,
):
    at_left = lax.axis_index("cols") == 0
    at_right = lax.axis_index("cols") == lax.axis_size("cols") - 1
    odd = lax.axis_index("cols") % 2 == 1
    zero = jnp.zeros((STRIP, F), F32)

    def left_strip(index):
        here = slice(index * STRIP, (index + 1) * STRIP)
        value = jnp.where(odd, near[here, :], far_side[here, :])
        return jnp.where(at_left, zero, value.astype(F32))

    def right_strip(index):
        here = slice(index * STRIP, (index + 1) * STRIP)
        value = jnp.where(odd, far_side[here, :], near[here, :])
        return jnp.where(at_right, zero, value.astype(F32))

    two = 2 * WIDE
    spread = one_hot((iota((WIDE, 16), 0) >> 2) == iota((WIDE, 16), 1))
    mask_wide[0:WIDE, :] = dot(spread, top[2 * two : 2 * two + 16, :])
    mask_wide[9 * WIDE : 10 * WIDE, :] = dot(spread, bottom[2 * two : 2 * two + 16, :])
    for tile_row in range(8):
        mask_wide[(tile_row + 1) * WIDE : (tile_row + 2) * WIDE, :] = dot(
            spread, mask_rows[tile_row * 16 : tile_row * 16 + 16, :].astype(BF)
        )
    strip_pre = []
    quad = 4 * WIDE
    for image, (weight, result) in enumerate(((fwd_one, pre_edge), (bwd_two, grad_edge))):
        first = image * 2
        columns = (
            left_strip(first),
            left_strip(first + 1),
            left[first * STRIP : (first + 1) * STRIP, :].astype(F32),
            right[(first + 1) * STRIP : (first + 2) * STRIP, :].astype(F32),
            right_strip(first),
            right_strip(first + 1),
        )
        for index, column in enumerate(columns):
            strips[index * STRIP : (index + 1) * STRIP, :] = column

        def before(row):
            return strips[pl.ds(STRIP + row, 1), :]

        def after(row):
            return strips[pl.ds(4 * STRIP + row, 1), :]

        for row in range(2):
            at = image * two + row * WIDE
            for halo, place, edge_at in ((top, row, row), (bottom, 34 + row, 6 + row)):
                plain = halo[at : at + WIDE, :]
                target, where_to = (grad_edges, edge_at) if image else (merged_shift, place)
                shifted_store(
                    target, where_to * WIDE, plain.astype(F32), plain, before(place), after(place)
                )
        if image:
            for row in range(4):
                place = (2, 3, 32, 33)[row]
                patched_copy(grad_ends, row * WIDE, grad_edges, (2 + row) * WIDE, before(place), after(place))
            ends = [grad_edges[ky * WIDE : ky * WIDE + two, :] for ky in range(3)]
            tails = [grad_edges[quad + ky * WIDE : quad + ky * WIDE + two, :] for ky in range(3)]
        else:

            def patch(row, _):
                patched_copy(
                    merged_inner, pl.multiple_of(row * WIDE, WIDE), merged_shift,
                    pl.multiple_of((row + 2) * WIDE, WIDE), before(row + 2), after(row + 2),
                )
                return 0

            lax.fori_loop(0, ROWS, patch, 0, unroll=4)
            ends = [merged_shift[ky * WIDE : ky * WIDE + two, :] for ky in range(3)]
            tails = [merged_shift[(32 + ky) * WIDE : (32 + ky) * WIDE + two, :] for ky in range(3)]
        row = iota((40, F), 0)
        inner = (row >= 2) & (row < 32)
        for side, (index, kx) in enumerate(((1, 0), (4, 2))):
            column = jnp.concatenate(
                [strips[index * STRIP + ky : index * STRIP + ky + 40, :] for ky in range(3)], axis=1
            ).astype(BF)
            taps = jnp.concatenate(
                [weight[(ky * 3 + kx) * F : (ky * 3 + kx + 1) * F, :] for ky in range(3)], axis=0
            )
            at = (image * 2 + side) * 40
            correction[at : at + 40, :] = jnp.where(inner, dot(column, taps), 0.0)
        parts = []
        for ky in range(3):
            for kx in range(3):
                parts.append(
                    jnp.concatenate(
                        [
                            strips[kx * STRIP + ky : kx * STRIP + ky + 40, :],
                            strips[(kx + 3) * STRIP + ky : (kx + 3) * STRIP + ky + 40, :],
                        ],
                        axis=0,
                    ).astype(BF)
                )
        lhs = jnp.concatenate([jnp.concatenate(group, axis=1) for group in (ends, tails, parts)], axis=0)
        values = dot(lhs, weight[...])
        result[...] = values[0:quad, :]
        strip_pre.append(values[quad:, :])
    strips[0:STRIP, :] = left_strip(4)
    strips[STRIP : 2 * STRIP, :] = right_strip(4)
    strip_mask = jnp.concatenate([strips[1:41, :], strips[STRIP + 1 : STRIP + 41, :]], axis=0)
    sigma = jax.nn.sigmoid(strip_pre[0])
    edge[0:80, :] = (strip_pre[0] * sigma * strip_mask).astype(BF).astype(F32)
    edge[80:160, :] = (
        (strip_pre[1] * (sigma * (1.0 + strip_pre[0] * (1.0 - sigma))) * strip_mask).astype(BF).astype(F32)
    )

    column = iota((WIDE, F), 0)

    def activate(row, _, pre_from=None, grad_from=None, source_row=0):
        at = pl.multiple_of(row * WIDE, WIDE)
        here = pl.ds(pl.multiple_of((row - source_row) * WIDE, WIDE), WIDE)

        def corrected(value, base):
            value = jnp.where(column == 0, value + correction[pl.ds(base + row, 1), :], value)
            return jnp.where(column == WIDE - 1, value + correction[pl.ds(base + 40 + row, 1), :], value)

        mask = mask_wide[pl.ds(pl.multiple_of(((row + 3) >> 2) * WIDE, WIDE), WIDE), :]
        value = corrected(pre_from[here, :], 0)
        sigma = jax.nn.sigmoid(value)
        hidden = value * sigma * mask
        slope = sigma * (1.0 + value * (1.0 - sigma))
        grad_value = corrected(grad_from[here, :], 80) * slope * mask
        shifted_store(
            hidden_shift, at, hidden, hidden.astype(BF), edge[pl.ds(row, 1), :], edge[pl.ds(40 + row, 1), :]
        )
        shifted_store(
            pre_shift, at, grad_value, grad_value.astype(BF),
            edge[pl.ds(80 + row, 1), :], edge[pl.ds(120 + row, 1), :],
        )
        return 0

    ends = functools.partial(activate, pre_from=pre_edge, grad_from=grad_edge)
    lax.fori_loop(0, 2, functools.partial(ends, source_row=0), 0)
    lax.fori_loop(
        2, 32, functools.partial(activate, pre_from=pre, grad_from=grad_hidden, source_row=2), 0, unroll=2
    )
    lax.fori_loop(32, 34, functools.partial(ends, source_row=30), 0)
    copies = start_copies(
        [(hidden_shift.at[:, F : 2 * F], hidden_out), (pre_shift.at[:, F : 2 * F], pre_out)], semaphores
    )
    across = iota((F, F), 0)
    along = iota((F, F), 1)
    unweave = one_hot(((along & 7) * 32 + (along >> 3)) == across)
    perms = [one_hot(along == permuted_index(across, elem)) for elem in range(G)]
    back = jnp.concatenate(perms, axis=0)
    for index, (values, grads, skip) in enumerate(
        (
            (merged_shift, pre_shift[WIDE : 33 * WIDE, F : 2 * F], WIDE),
            (hidden_shift, grad_two[...], 0),
        )
    ):
        turned = dot_nt(unweave, grads).astype(BF)
        full = []
        for ky in range(3):
            start = skip + ky * WIDE
            full.append(dot(turned, values[start : start + ROWS * WIDE, :]).astype(BF))
        pieces = []
        for elem in range(G):
            of_cell = {source_cell(elem, pos): pos for pos in range(9)}
            rows = []
            for cell in range(9):
                pos = of_cell[cell]
                kx = pos % 3
                rows.append(full[pos // 3][elem * 32 : elem * 32 + 32, kx * F : (kx + 1) * F])
            pieces.append(jnp.concatenate(rows, axis=0))
        folded[index * 288 : (index + 1) * 288, :] = dot(jnp.concatenate(pieces, axis=1), back)
    folded[576:592, :] = jnp.zeros((16, F), F32)
    for part in range(128):
        start, lanes = 9 * (part % 64), (part // 64) * 128
        data = folded[start : start + 16, lanes : lanes + 128].reshape(4, 4, 128)
        message[part] = data[0:3].astype(BF)
    for copy in copies:
        copy.wait()


def wide_mask(mask_rows, step):
    spread = one_hot((iota((WIDE, 16), 0) >> 2) == iota((WIDE, 16), 1))
    parts = []
    for tile_row in range(4):
        at = pl.multiple_of((step * 4 + tile_row) * 16, 16)
        parts.extend([dot(spread, mask_rows[pl.ds(at, 16), :].astype(BF))] * 4)
    return jnp.concatenate(parts, axis=0)


def load_shifted(values, filter_in, edges, base, plain, filter_held, weight, forward, shifted, semaphores):
    cuts = (0, 640, 1152, 1664, 2176)
    pairs = [(filter_in, filter_held)]
    for first, last in zip(cuts[:-1], cuts[1:]):
        pairs.append((values.at[pl.ds(first, last - first)], plain.at[pl.ds(first, last - first)]))
    copies = start_copies(pairs, semaphores)

    def row_of(row, _):
        at = pl.multiple_of(row * WIDE, WIDE)
        value = plain[pl.ds(at, WIDE), :]
        shifted_store(
            shifted, at, value.astype(F32), value,
            edges[pl.ds(base + row, 1), :], edges[pl.ds(base + 40 + row, 1), :],
        )
        return 0

    copies[0].wait()
    build_weight(filter_held, weight, forward)
    for copy in copies[1:]:
        copy.wait()
    lax.fori_loop(0, ROWS + 2, row_of, 0, unroll=2)


def backward_kernel(
    pre_in, filter_in, edges, mask_rows, tiles, low_grad,
    pair, plain, filter_held, bwd_one, pre_shift, semaphores,
):
    two = 2 * WIDE
    load_shifted(pre_in, filter_in, edges, 80, plain, filter_held, bwd_one, False, pre_shift, semaphores)
    order = iota((F, F), 0)
    tile_order = one_hot(
        iota((F, F), 1) == (((order >> 2) & 3) * WIDE + (order >> 4) * 4 + (order & 3))
    )

    def body(step, _):
        at = pl.multiple_of(step * 1024, 1024)
        grad_merged = conv(pre_shift, at, 1024, bwd_one) * wide_mask(mask_rows, step)
        rounded = grad_merged.astype(BF)
        for tile_row in range(4):
            tiles[pl.ds(at + tile_row * F, F), :] = dot(
                tile_order, rounded[tile_row * F : (tile_row + 1) * F, :]
            ).astype(BF)
        for row in range(8):
            both = grad_merged[row * two : row * two + WIDE, :] + grad_merged[row * two + WIDE : row * two + two, :]
            for half in range(2):
                pair[half, row * WIDE : (row + 1) * WIDE, :] = both[:, half * 128 : half * 128 + 128]
        for half in range(2):
            low_grad[pl.ds(pl.multiple_of(step * 256, 256), 256), half * 128 : half * 128 + 128] = (
                pair[half, pl.ds(0, 256, stride=2), :] + pair[half, pl.ds(1, 256, stride=2), :]
            ).astype(BF)
        return 0

    lax.fori_loop(0, 2, body, 0)


def forward_kernel(
    hidden_in, filter_in, edges, mask_rows, output, plain, filter_held, fwd_two, hidden_shift, semaphores
):
    load_shifted(hidden_in, filter_in, edges, 0, plain, filter_held, fwd_two, True, hidden_shift, semaphores)

    def body(step, _):
        at = pl.multiple_of(step * 1024, 1024)
        output[pl.ds(at, 1024), :] = (
            conv(hidden_shift, at, 1024, fwd_two) * wide_mask(mask_rows, step)
        ).astype(BF)
        return 0

    lax.fori_loop(0, 2, body, 0)


def pack_kernel(places, tiles, send):
    def copy(group, _):
        for sub in range(8):
            tile = group * 8 + sub
            place = places[0, tile]
            for half in range(2):
                value = tiles[pl.ds(pl.multiple_of(tile * 16, 16), 16), half * 128 : half * 128 + 128]
                send[place >> 1, pl.ds((place & 1) * 8 + half * 4, 4)] = value.reshape(4, 4, 128)
        return 0

    lax.fori_loop(0, 16, copy, 0)


def terms_kernel(send_in, got, slot_rows, send, rows, semaphore):
    total = jnp.zeros((3, 4, 128), F32)
    for part in range(128):
        total = total + got[part].astype(F32)
    front = total[0:2].astype(BF)
    row = iota((4, 128), 0)
    for part in range(128):
        rows[part, 0:2] = front
        rows[part, 2] = jnp.where(row == 1, slot_rows[part : part + 1, :], total[2]).astype(BF)
    copy = pltpu.make_async_copy(rows, send.at[:, pl.ds(16, 3)], semaphore)
    copy.start()
    copy.wait()


def place_kernel(scale, got, skip_grad, one, two, gathered, sources, folded, table, semaphore):
    for part in range(128):
        start, lanes = 9 * (part % 64), (part // 64) * 128
        terms = got[part, 16:19].astype(F32)
        folded[start : start + 4, lanes : lanes + 128] = terms[0] * scale
        folded[start + 4 : start + 8, lanes : lanes + 128] = terms[1] * scale
        folded[start + 8 : start + 9, lanes : lanes + 128] = terms[2, 0:1] * scale
        gathered[part : part + 1, :] = terms[2, 1:2]
    one[...] = folded[0:288, :]
    two[...] = folded[288:576, :]
    slots = gathered[...].T
    wanted = iota((128, 128), 0).astype(F32)
    index = iota((128, 128), 1).astype(F32)
    source = jnp.zeros((128, 128), F32)
    for which in range(2):
        source = source + jnp.where(slots[which : which + 1, :] == wanted, index * 2.0 + which, 0.0)
    sources[...] = jnp.broadcast_to(jnp.sum(source, axis=1, keepdims=True), (128, 128)).T[0:8, :].astype(jnp.int32)
    copy = pltpu.make_async_copy(sources, table, semaphore)
    copy.start()
    copy.wait()

    def put(group, _):
        for sub in range(8):
            slot = group * 8 + sub
            place = table[0, slot]
            for half in range(2):
                skip_grad[slot, :, :, half * 128 : half * 128 + 128] = got[
                    place >> 1, pl.ds((place & 1) * 8 + half * 4, 4)
                ]
        return 0

    lax.fori_loop(0, 16, put, 0)


def swap(values, axis, first):
    size = lax.axis_size(axis)
    partner = list(range(size))
    for index in range(first, size - 1, 2):
        partner[index], partner[index + 1] = index + 1, index
    return lax.ppermute(values, axis, list(enumerate(partner)))


def on_device(low_feats, skip_feats, tissue_mask, owner_slot, filter_one, filter_two, out_grad):
    everyone = ("rows", "cols")
    height, breadth, features = skip_feats.shape
    pixels = height * breadth
    given = (
        kept(low_feats.reshape(-1, F)), kept(skip_feats.reshape(pixels, F)),
        kept(out_grad.reshape(pixels, F)), kept(tissue_mask),
    )
    near, far_side = call(
        head_kernel, [shape((272, F))] * 2, 4,
        [
            pltpu.VMEM((64, F), BF), pltpu.VMEM((4 * WIDE, F), BF), pltpu.VMEM((4 * WIDE, F), BF),
            pltpu.VMEM((8, 16), jnp.int32), pltpu.VMEM((128, F), F32), pltpu.VMEM((4 * WIDE, F), BF),
            pltpu.VMEM((4 * WIDE, F), BF), pltpu.SemaphoreType.DMA((7,)),
        ],
        specs=[HBM] * 4, name="head",
    )(*given)
    near_rows = swap(near, "rows", 0)
    far_rows = swap(far_side, "rows", 1)
    bases = [f.transpose(1, 2, 0, 3).reshape(288, F) for f in (filter_one, filter_two)]
    merged, grad_two, mask_rows, fwd_one, bwd_two, places, slot_rows = call(
        prepare_kernel,
        [
            shape((pixels, F)), shape((pixels, F)), shape((128, F), F32), shape((9 * F, F)),
            shape((9 * F, F)), shape((8, 128), jnp.int32), shape((128, 128), F32),
        ],
        7,
        [
            pltpu.VMEM((pixels // 4, F), BF), pltpu.VMEM((pixels, F), BF), pltpu.VMEM((pixels, F), BF),
            pltpu.VMEM((8, 16), jnp.int32), pltpu.SemaphoreType.DMA((13,)),
        ],
        specs=[HBM] * 4 + [VMEM] * 3, flops=3 << 30, name="prepare",
    )(*given, owner_slot, *bases)
    left, right, top, bottom, near, far_side = call(
        edge_kernel,
        [shape((5 * STRIP, F))] * 2 + [shape((272, F))] * 2 + [shape((5 * STRIP, F))] * 2,
        5, [pltpu.VMEM((2, 48 * 16, 128), F32), pltpu.VMEM((STRIP, F), F32)], name="edge",
    )(merged, grad_two, near_rows, far_rows, mask_rows)
    near_cols = swap(near, "cols", 0)
    far_cols = swap(far_side, "cols", 1)
    inner = call(
        interior_kernel,
        [
            shape((pixels, 3 * F)), shape((30 * WIDE, F), F32), shape((30 * WIDE, F), F32),
            shape((4 * WIDE, 3 * F)),
        ],
        4, [pltpu.VMEM((pixels, 3 * F), BF)], flops=5 << 30, limit=16 << 20, name="interior",
    )(merged, grad_two, fwd_one, bwd_two)
    hidden, grad_pre, edges, message = call(
        first_kernel,
        [far((34 * WIDE, F)), far((34 * WIDE, F)), shape((160, F), F32), shape((128, 3, 4, 128))],
        15,
        [
            pltpu.VMEM((34 * WIDE, 3 * F), BF), pltpu.VMEM((34 * WIDE, 3 * F), BF),
            pltpu.VMEM((10 * WIDE, F), F32),
            pltpu.VMEM((36 * WIDE, 3 * F), BF), pltpu.VMEM((8 * WIDE, 3 * F), BF),
            pltpu.VMEM((6 * STRIP, F), F32),
            pltpu.VMEM((4 * WIDE, F), F32), pltpu.VMEM((4 * WIDE, F), F32), pltpu.VMEM((160, F), F32),
            pltpu.VMEM((592, F), F32), pltpu.SemaphoreType.DMA((2,)),
        ],
        outs=[HBM, HBM, VMEM, VMEM], flops=10 << 30, limit=36 << 20, name="first",
    )(merged, grad_two, top, bottom, left, right, near_cols, far_cols, mask_rows, fwd_one, bwd_two, *inner)
    got_terms = lax.all_to_all(message, everyone, 0, 0, tiled=True)
    loading = [
        pltpu.VMEM((34 * WIDE, F), BF), pltpu.VMEM((288, F), BF), pltpu.VMEM((9 * F, F), BF),
        pltpu.VMEM((34 * WIDE, 3 * F), BF), pltpu.SemaphoreType.DMA((5,)),
    ]
    tiles, low_grad = call(
        backward_kernel, [shape((pixels, F)), shape((pixels // 4, F))], 4,
        [pltpu.VMEM((2, 8 * WIDE, 128), F32)] + loading, specs=[HBM, HBM, VMEM, VMEM],
        flops=3 << 30, name="backward",
    )(kept(grad_pre), kept(bases[0]), edges, mask_rows)
    output = call(
        forward_kernel, shape((pixels, F)), 4, loading, specs=[HBM, HBM, VMEM, VMEM],
        flops=3 << 30, name="forward",
    )(kept(hidden), kept(bases[1]), edges, mask_rows)
    send = call(pack_kernel, far((128, 19, 4, 128)), 2, specs=[SMEM, VMEM], name="pack")(places, tiles)
    send = pl.pallas_call(
        terms_kernel,
        out_shape=far((128, 19, 4, 128)),
        in_specs=[HBM, VMEM, VMEM],
        out_specs=HBM,
        scratch_shapes=[pltpu.VMEM((128, 3, 4, 128), BF), pltpu.SemaphoreType.DMA],
        input_output_aliases={0: 0},
        compiler_params=pltpu.CompilerParams(vmem_limit_bytes=24 << 20),
        cost_estimate=pl.CostEstimate(flops=1 << 30, bytes_accessed=4 << 20, transcendentals=0),
        name="terms",
    )(kept(send), got_terms, slot_rows)
    got = lax.all_to_all(send, everyone, 0, 0, tiled=True)
    scale = 1.0 / math.sqrt(pixels * lax.axis_size("rows") * lax.axis_size("cols"))
    skip_grad, one, two = call(
        functools.partial(place_kernel, scale),
        [shape((128, 4, 4, F)), shape((288, F), F32), shape((288, F), F32)], 1,
        [
            pltpu.VMEM((128, 128), F32), pltpu.VMEM((8, 128), jnp.int32), pltpu.VMEM((592, F), F32),
            pltpu.SMEM((8, 128), jnp.int32), pltpu.SemaphoreType.DMA,
        ],
        name="place",
    )(got)
    return (
        output.reshape(height, breadth, F),
        skip_grad,
        low_grad.reshape(height // 2, breadth // 2, F),
        one.reshape(3, 3, 32, F).transpose(2, 0, 1, 3),
        two.reshape(3, 3, 32, F).transpose(2, 0, 1, 3),
    )


def solution(mesh):
    placed = (
        P("rows", "cols", None),
        P("rows", "cols", None),
        P("rows", "cols"),
        P("rows", "cols"),
        P(),
        P(),
        P("rows", "cols", None),
    )
    return jax.shard_map(
        on_device,
        mesh=mesh,
        in_specs=placed,
        out_specs=(
            P("rows", "cols", None),
            P(("rows", "cols"), None, None, None),
            P("rows", "cols", None),
            P(),
            P(),
        ),
        check_vma=False,
    )
```

```python
import functools
import math

import jax
import jax.numpy as jnp
import numpy as np
from jax import lax
from jax.experimental import pallas as pl
from jax.experimental.pallas import tpu as pltpu
from jax.sharding import PartitionSpec as P

G = 8
F = 256
ROWS = 32
WIDE = 64
STRIP = 48
MASK_ROWS = 16
BF = jnp.bfloat16
F32 = jnp.float32
VMEM = pl.BlockSpec(memory_space=pltpu.VMEM)
SMEM = pl.BlockSpec(memory_space=pltpu.SMEM)
HBM = pl.BlockSpec(memory_space=pltpu.HBM)


def inverse_of(element):
    return (4 - element % 4) % 4 if element < 4 else element


def product(first, second):
    mirror = (first // 4 + second // 4) % 2
    turns = (first % 4 + (1 - 2 * (first // 4)) * (second % 4)) % 4
    return mirror * 4 + turns


def act(element, row, col):
    if element // 4:
        col = -col
    for _ in range(element % 4):
        row, col = -col, row
    return row, col


def source_cell(elem, pos):
    row, col = act(inverse_of(elem), pos // 3 - 1, pos % 3 - 1)
    return (row + 1) * 3 + col + 1


def iota(shape, dim):
    return lax.broadcasted_iota(jnp.int32, shape, dim)


def one_hot(cond):
    return jnp.where(cond, 1.0, 0.0).astype(BF)


def permuted_index(index, elem):
    inverse = inverse_of(elem)
    mirror, turns = inverse // 4, inverse % 4
    second = index & 7
    new_mirror = (second >> 2) ^ mirror
    spin = second & 3
    new_turns = (turns + (-spin if mirror else spin)) & 3
    return (index & ~7) | (new_mirror << 2) | new_turns


def dot(lhs, rhs):
    return jnp.dot(lhs, rhs, preferred_element_type=F32)


def dot_nt(lhs, rhs):
    return lax.dot_general(lhs, rhs, (((1,), (1,)), ((), ())), preferred_element_type=F32)


def call(
    kernel, out_shape, n_in, scratch=(), specs=None, outs=None, flops=1 << 30, limit=24 << 20, name=None
):
    return pl.pallas_call(
        kernel,
        out_shape=out_shape,
        in_specs=specs or [VMEM] * n_in,
        out_specs=outs or jax.tree.map(lambda _: VMEM, out_shape),
        scratch_shapes=list(scratch),
        compiler_params=pltpu.CompilerParams(vmem_limit_bytes=limit),
        cost_estimate=pl.CostEstimate(flops=flops, bytes_accessed=4 << 20, transcendentals=0),
        name=name,
    )


def shape(dims, dtype=BF):
    return jax.ShapeDtypeStruct(dims, dtype)


def far(dims):
    return pltpu.HBM(dims, BF)


def kept(values):
    return pltpu.with_memory_space_constraint(values, pltpu.HBM)


def start_copies(pairs, semaphores):
    copies = [pltpu.make_async_copy(src, dst, semaphores.at[i]) for i, (src, dst) in enumerate(pairs)]
    for copy in copies:
        copy.start()
    return copies


def fill_mask_rows(tissue, mask_rows, tile_rows):
    same = iota((16, 16), 0) == iota((16, 16), 1)
    for tile_row in tile_rows:
        values = jnp.broadcast_to(tissue[tile_row : tile_row + 1, :].astype(F32), (16, 16))
        column = jnp.sum(jnp.where(same, values, 0.0), axis=1, keepdims=True)
        mask_rows[tile_row * 16 : tile_row * 16 + 16, :] = jnp.broadcast_to(column, (16, F))


def masked_rows(tile_row, half, low, skip, grad, mask_rows, low_at, at, merged, grad_two, put):
    spread = one_hot((iota((WIDE, 16), 0) >> 2) == iota((WIDE, 16), 1))
    twice = one_hot((iota((WIDE, 32), 0) >> 1) == iota((WIDE, 32), 1))
    mask = dot(spread, mask_rows[tile_row * 16 : tile_row * 16 + 16, :].astype(BF))
    coarse = dot(twice, low[low_at : low_at + 32, :])
    for sub in range(2):
        here, there = pl.ds(at + sub * WIDE, WIDE), pl.ds(put + sub * WIDE, WIDE)
        merged[there, :] = ((coarse + skip[here, :].astype(F32)) * mask).astype(BF)
        grad_two[there, :] = (grad[here, :].astype(F32) * mask).astype(BF)


def head_kernel(
    low_in, skip_in, grad_in, tissue_in, near, far_side, low, skip, grad, tissue, mask_rows, merged, grad_two,
    semaphores,
):
    two = 2 * WIDE
    last = ROWS * WIDE - two
    pairs = [(tissue_in, tissue)]
    for part in range(2):
        pairs.append((low_in.at[pl.ds(part * 480, 32)], low.at[pl.ds(part * 32, 32)]))
        pairs.append((skip_in.at[pl.ds(part * last, two)], skip.at[pl.ds(part * two, two)]))
        pairs.append((grad_in.at[pl.ds(part * last, two)], grad.at[pl.ds(part * two, two)]))
    for copy in start_copies(pairs, semaphores):
        copy.wait()
    fill_mask_rows(tissue, mask_rows, (0, 7))
    for part in range(2):
        masked_rows(
            part * 7, part, low, skip, grad, mask_rows, part * 32, part * two, merged, grad_two, part * two
        )
    odd = lax.axis_index("rows") % 2 == 1
    for at, source in ((0, merged), (two, grad_two)):
        head, tail = source[0:two, :], source[two : 2 * two, :]
        near[at : at + two, :] = jnp.where(odd, head, tail)
        far_side[at : at + two, :] = jnp.where(odd, tail, head)
    head, tail = mask_rows[0:16, :].astype(BF), mask_rows[112:128, :].astype(BF)
    near[2 * two : 2 * two + 16, :] = jnp.where(odd, head, tail)
    far_side[2 * two : 2 * two + 16, :] = jnp.where(odd, tail, head)


def build_weight(base, weight, forward):
    across = iota((F, F), 0)
    along = iota((F, F), 1)
    weave = one_hot(((across & 7) * 32 + (across >> 3)) == along)
    turned = [dot(base[...], one_hot(across == permuted_index(along, elem))).astype(BF) for elem in range(G)]
    for pos in range(9):
        rows = []
        for elem in range(G):
            cell = source_cell(elem, pos)
            rows.append(turned[elem][cell * 32 : cell * 32 + 32, :])
        woven = dot(weave, jnp.concatenate(rows, axis=0))
        if forward:
            weight[pos * F : (pos + 1) * F, :] = woven.T.astype(BF)
        else:
            weight[(8 - pos) * F : (9 - pos) * F, :] = woven.astype(BF)


def prepare_kernel(
    low_in, skip_in, grad_in, tissue_in, slots, filter_one, filter_two,
    merged, grad_two, mask_rows, fwd_one, bwd_two, places, slot_rows,
    low, skip, grad, tissue, semaphores,
):
    pairs = [(tissue_in, tissue)]
    for part in range(4):
        fine, coarse = pl.ds(part * 512, 512), pl.ds(part * 128, 128)
        pairs.append((low_in.at[coarse], low.at[coarse]))
        pairs.append((skip_in.at[fine], skip.at[fine]))
        pairs.append((grad_in.at[fine], grad.at[fine]))
    copies = start_copies(pairs, semaphores)
    flat = jnp.concatenate([slots[row : row + 1, :] for row in range(8)], axis=1)
    owner, local = flat >> 7, (flat & 127).astype(F32)
    tile = iota((128, 128), 1)
    match = owner == iota((128, 128), 0)
    index = tile.astype(F32)
    first = jnp.min(jnp.where(match, index, 1000.0), axis=1, keepdims=True)
    second = match & (index > first)
    used = jnp.sum(jnp.where(second, 1.0, 0.0), axis=0, keepdims=True)
    places[...] = jnp.broadcast_to(owner * 2 + used.astype(jnp.int32), (8, 128))
    slot_one = jnp.sum(jnp.where(match & (index == first), local + 1.0, 0.0), axis=1, keepdims=True)
    slot_two = jnp.sum(jnp.where(second, local + 1.0, 0.0), axis=1, keepdims=True)
    slot_rows[...] = jnp.where(tile == 0, slot_one, jnp.where(tile == 1, slot_two, 0.0)) - 1.0
    build_weight(filter_one, fwd_one, True)
    build_weight(filter_two, bwd_two, False)
    copies[0].wait()
    fill_mask_rows(tissue, mask_rows, range(8))
    for copy in copies[1:]:
        copy.wait()
    for low_row in range(16):
        at = low_row * 2 * WIDE
        masked_rows(
            low_row // 2, low_row % 2, low, skip, grad, mask_rows, low_row * 32, at, merged, grad_two, at
        )


def edge_kernel(
    merged, grad_two, near_in, far_in, mask_rows, left, right, top, bottom, near, far_side, tall, masks
):
    two = 2 * WIDE
    at_top = lax.axis_index("rows") == 0
    at_bottom = lax.axis_index("rows") == lax.axis_size("rows") - 1
    odd = lax.axis_index("rows") % 2 == 1
    zero = jnp.zeros((272, F), BF)
    top[...] = jnp.where(at_top, zero, jnp.where(odd, near_in[...], far_in[...]))
    bottom[...] = jnp.where(at_bottom, zero, jnp.where(odd, far_in[...], near_in[...]))
    tall[:, 36 * 16 : 48 * 16, :] = jnp.zeros((2, 12 * 16, 128), F32)

    def keep(row, values):
        for half in range(2):
            tall[half, row * 16 : row * 16 + 16, :] = values[:, half * 128 : half * 128 + 128].astype(F32)

    for side, (target, offset, picks, tile_col) in enumerate(
        ((left, 0, (0, 1), 0), (right, 48, (14, 15), 15))
    ):
        for image, source in enumerate((merged, grad_two)):
            for row in range(2):
                place = image * two + row * WIDE + offset
                keep(row, top[place : place + 16, :])
                keep(34 + row, bottom[place : place + 16, :])
            for row in range(ROWS):
                place = row * WIDE + offset
                keep(row + 2, source[place : place + 16, :])
            for col in range(2):
                strip = (image * 2 + col) * STRIP
                for half in range(2):
                    target[strip : strip + STRIP, half * 128 : half * 128 + 128] = tall[
                        half, pl.ds(picks[col], STRIP, stride=16), :
                    ].astype(BF)
        masks[...] = jnp.zeros((STRIP, F), F32)
        above = top[2 * two : 2 * two + 16, :].astype(F32)
        below = bottom[2 * two : 2 * two + 16, :].astype(F32)
        masks[0:2, :] = jnp.broadcast_to(above[tile_col : tile_col + 1, :], (2, F))
        masks[34:36, :] = jnp.broadcast_to(below[tile_col : tile_col + 1, :], (2, F))
        for tile_row in range(8):
            at = tile_row * 16 + tile_col
            masks[2 + 4 * tile_row : 6 + 4 * tile_row, :] = jnp.broadcast_to(mask_rows[at : at + 1, :], (4, F))
        target[4 * STRIP : 5 * STRIP, :] = masks[...].astype(BF)
    odd = lax.axis_index("cols") % 2 == 1
    near[...] = jnp.where(odd, left[...], right[...])
    far_side[...] = jnp.where(odd, right[...], left[...])


def shifted_store(target, at, value, plain, before, after):
    row = iota((WIDE, F), 0)
    target[pl.ds(at, WIDE), 0:F] = jnp.where(row == 0, before, pltpu.roll(value, 1, 0)).astype(BF)
    target[pl.ds(at, WIDE), F : 2 * F] = plain
    target[pl.ds(at, WIDE), 2 * F : 3 * F] = jnp.where(
        row == WIDE - 1, after, pltpu.roll(value, WIDE - 1, 0)
    ).astype(BF)


def conv(shifted, start, count, weight):
    lhs = jnp.concatenate([shifted[pl.ds(start + ky * WIDE, count), :] for ky in range(3)], axis=1)
    return dot(lhs, weight[...])


def interior_kernel(
    merged, grad_two, fwd_one, bwd_two, merged_shift, pre, grad_hidden, grad_ends, grad_shift
):
    nothing = jnp.zeros((1, F), F32)
    for source, target in ((merged, merged_shift), (grad_two, grad_shift)):

        def shift_row(row, _, source=source, target=target):
            at = pl.multiple_of(row * WIDE, WIDE)
            plain = source[pl.ds(at, WIDE), :]
            shifted_store(target, at, plain.astype(F32), plain, nothing, nothing)
            return 0

        lax.fori_loop(0, ROWS, shift_row, 0, unroll=4)

    pre[...] = conv(merged_shift, 0, 30 * WIDE, fwd_one)
    grad_hidden[...] = conv(grad_shift, 0, 30 * WIDE, bwd_two)
    grad_ends[0 : 2 * WIDE, :] = grad_shift[0 : 2 * WIDE, :]
    grad_ends[2 * WIDE : 4 * WIDE, :] = grad_shift[30 * WIDE : 32 * WIDE, :]


def patched_copy(source, source_at, target, target_at, before, after):
    row = iota((16, F), 0)
    target[pl.ds(target_at, WIDE), :] = source[pl.ds(source_at, WIDE), :]
    first = source[pl.ds(source_at, 16), 0:F].astype(F32)
    target[pl.ds(target_at, 16), 0:F] = jnp.where(row == 0, before, first).astype(BF)
    last = source[pl.ds(source_at + 48, 16), 2 * F : 3 * F].astype(F32)
    target[pl.ds(target_at + 48, 16), 2 * F : 3 * F] = jnp.where(row == 15, after, last).astype(BF)


def first_kernel(
    merged, grad_two, top, bottom, left, right, near, far_side, mask_rows, fwd_one, bwd_two,
    merged_inner, pre, grad_hidden, grad_ends,
    hidden_out, pre_out, edge, message,
    hidden_shift, pre_shift, mask_wide, merged_shift, grad_edges, strips, pre_edge, grad_edge, correction, folded, semaphores,
):
    at_left = lax.axis_index("cols") == 0
    at_right = lax.axis_index("cols") == lax.axis_size("cols") - 1
    odd = lax.axis_index("cols") % 2 == 1
    zero = jnp.zeros((STRIP, F), F32)

    def left_strip(index):
        here = slice(index * STRIP, (index + 1) * STRIP)
        value = jnp.where(odd, near[here, :], far_side[here, :])
        return jnp.where(at_left, zero, value.astype(F32))

    def right_strip(index):
        here = slice(index * STRIP, (index + 1) * STRIP)
        value = jnp.where(odd, far_side[here, :], near[here, :])
        return jnp.where(at_right, zero, value.astype(F32))

    two = 2 * WIDE
    spread = one_hot((iota((WIDE, 16), 0) >> 2) == iota((WIDE, 16), 1))
    mask_wide[0:WIDE, :] = dot(spread, top[2 * two : 2 * two + 16, :])
    mask_wide[9 * WIDE : 10 * WIDE, :] = dot(spread, bottom[2 * two : 2 * two + 16, :])
    for tile_row in range(8):
        mask_wide[(tile_row + 1) * WIDE : (tile_row + 2) * WIDE, :] = dot(
            spread, mask_rows[tile_row * 16 : tile_row * 16 + 16, :].astype(BF)
        )
    strip_pre = []
    quad = 4 * WIDE
    for image, (weight, result) in enumerate(((fwd_one, pre_edge), (bwd_two, grad_edge))):
        first = image * 2
        columns = (
            left_strip(first),
            left_strip(first + 1),
            left[first * STRIP : (first + 1) * STRIP, :].astype(F32),
            right[(first + 1) * STRIP : (first + 2) * STRIP, :].astype(F32),
            right_strip(first),
            right_strip(first + 1),
        )
        for index, column in enumerate(columns):
            strips[index * STRIP : (index + 1) * STRIP, :] = column

        def before(row):
            return strips[pl.ds(STRIP + row, 1), :]

        def after(row):
            return strips[pl.ds(4 * STRIP + row, 1), :]

        for row in range(2):
            at = image * two + row * WIDE
            for halo, place, edge_at in ((top, row, row), (bottom, 34 + row, 6 + row)):
                plain = halo[at : at + WIDE, :]
                target, where_to = (grad_edges, edge_at) if image else (merged_shift, place)
                shifted_store(
                    target, where_to * WIDE, plain.astype(F32), plain, before(place), after(place)
                )
        if image:
            for row in range(4):
                place = (2, 3, 32, 33)[row]
                patched_copy(grad_ends, row * WIDE, grad_edges, (2 + row) * WIDE, before(place), after(place))
            ends = [grad_edges[ky * WIDE : ky * WIDE + two, :] for ky in range(3)]
            tails = [grad_edges[quad + ky * WIDE : quad + ky * WIDE + two, :] for ky in range(3)]
        else:

            def patch(row, _):
                patched_copy(
                    merged_inner, pl.multiple_of(row * WIDE, WIDE), merged_shift,
                    pl.multiple_of((row + 2) * WIDE, WIDE), before(row + 2), after(row + 2),
                )
                return 0

            lax.fori_loop(0, ROWS, patch, 0, unroll=4)
            ends = [merged_shift[ky * WIDE : ky * WIDE + two, :] for ky in range(3)]
            tails = [merged_shift[(32 + ky) * WIDE : (32 + ky) * WIDE + two, :] for ky in range(3)]
        row = iota((40, F), 0)
        inner = (row >= 2) & (row < 32)
        for side, (index, kx) in enumerate(((1, 0), (4, 2))):
            column = jnp.concatenate(
                [strips[index * STRIP + ky : index * STRIP + ky + 40, :] for ky in range(3)], axis=1
            ).astype(BF)
            taps = jnp.concatenate(
                [weight[(ky * 3 + kx) * F : (ky * 3 + kx + 1) * F, :] for ky in range(3)], axis=0
            )
            at = (image * 2 + side) * 40
            correction[at : at + 40, :] = jnp.where(inner, dot(column, taps), 0.0)
        parts = []
        for ky in range(3):
            for kx in range(3):
                parts.append(
                    jnp.concatenate(
                        [
                            strips[kx * STRIP + ky : kx * STRIP + ky + 40, :],
                            strips[(kx + 3) * STRIP + ky : (kx + 3) * STRIP + ky + 40, :],
                        ],
                        axis=0,
                    ).astype(BF)
                )
        lhs = jnp.concatenate([jnp.concatenate(group, axis=1) for group in (ends, tails, parts)], axis=0)
        values = dot(lhs, weight[...])
        result[...] = values[0:quad, :]
        strip_pre.append(values[quad:, :])
    strips[0:STRIP, :] = left_strip(4)
    strips[STRIP : 2 * STRIP, :] = right_strip(4)
    strip_mask = jnp.concatenate([strips[1:41, :], strips[STRIP + 1 : STRIP + 41, :]], axis=0)
    sigma = jax.nn.sigmoid(strip_pre[0])
    edge[0:80, :] = (strip_pre[0] * sigma * strip_mask).astype(BF).astype(F32)
    edge[80:160, :] = (
        (strip_pre[1] * (sigma * (1.0 + strip_pre[0] * (1.0 - sigma))) * strip_mask).astype(BF).astype(F32)
    )

    column = iota((WIDE, F), 0)

    def activate(row, _, pre_from=None, grad_from=None, source_row=0):
        at = pl.multiple_of(row * WIDE, WIDE)
        here = pl.ds(pl.multiple_of((row - source_row) * WIDE, WIDE), WIDE)

        def corrected(value, base):
            value = jnp.where(column == 0, value + correction[pl.ds(base + row, 1), :], value)
            return jnp.where(column == WIDE - 1, value + correction[pl.ds(base + 40 + row, 1), :], value)

        mask = mask_wide[pl.ds(pl.multiple_of(((row + 3) >> 2) * WIDE, WIDE), WIDE), :]
        value = corrected(pre_from[here, :], 0)
        sigma = jax.nn.sigmoid(value)
        hidden = value * sigma * mask
        slope = sigma * (1.0 + value * (1.0 - sigma))
        grad_value = corrected(grad_from[here, :], 80) * slope * mask
        shifted_store(
            hidden_shift, at, hidden, hidden.astype(BF), edge[pl.ds(row, 1), :], edge[pl.ds(40 + row, 1), :]
        )
        shifted_store(
            pre_shift, at, grad_value, grad_value.astype(BF),
            edge[pl.ds(80 + row, 1), :], edge[pl.ds(120 + row, 1), :],
        )
        return 0

    ends = functools.partial(activate, pre_from=pre_edge, grad_from=grad_edge)
    lax.fori_loop(0, 2, functools.partial(ends, source_row=0), 0)
    lax.fori_loop(
        2, 32, functools.partial(activate, pre_from=pre, grad_from=grad_hidden, source_row=2), 0, unroll=3
    )
    lax.fori_loop(32, 34, functools.partial(ends, source_row=30), 0)
    copies = start_copies(
        [(hidden_shift.at[:, F : 2 * F], hidden_out), (pre_shift.at[:, F : 2 * F], pre_out)], semaphores
    )
    across = iota((F, F), 0)
    along = iota((F, F), 1)
    unweave = one_hot(((along & 7) * 32 + (along >> 3)) == across)
    perms = [one_hot(along == permuted_index(across, elem)) for elem in range(G)]
    back = jnp.concatenate(perms, axis=0)
    for index, (values, grads, skip) in enumerate(
        (
            (merged_shift, pre_shift[WIDE : 33 * WIDE, F : 2 * F], WIDE),
            (hidden_shift, grad_two[...], 0),
        )
    ):
        turned = dot_nt(unweave, grads).astype(BF)
        full = []
        for ky in range(3):
            start = skip + ky * WIDE
            full.append(dot(turned, values[start : start + ROWS * WIDE, :]).astype(BF))
        pieces = []
        for elem in range(G):
            of_cell = {source_cell(elem, pos): pos for pos in range(9)}
            rows = []
            for cell in range(9):
                pos = of_cell[cell]
                kx = pos % 3
                rows.append(full[pos // 3][elem * 32 : elem * 32 + 32, kx * F : (kx + 1) * F])
            pieces.append(jnp.concatenate(rows, axis=0))
        folded[index * 288 : (index + 1) * 288, :] = dot(jnp.concatenate(pieces, axis=1), back)
    folded[576:592, :] = jnp.zeros((16, F), F32)
    for part in range(128):
        start, lanes = 9 * (part % 64), (part // 64) * 128
        data = folded[start : start + 16, lanes : lanes + 128].reshape(4, 4, 128)
        message[part] = data[0:3].astype(BF)
    for copy in copies:
        copy.wait()


def wide_mask(mask_rows, step):
    spread = one_hot((iota((WIDE, 16), 0) >> 2) == iota((WIDE, 16), 1))
    parts = []
    for tile_row in range(4):
        at = pl.multiple_of((step * 4 + tile_row) * 16, 16)
        parts.extend([dot(spread, mask_rows[pl.ds(at, 16), :].astype(BF))] * 4)
    return jnp.concatenate(parts, axis=0)


def load_shifted(values, filter_in, edges, base, plain, filter_held, weight, forward, shifted, semaphores):
    cuts = (0, 640, 1152, 1664, 2176)
    pairs = [(filter_in, filter_held)]
    for first, last in zip(cuts[:-1], cuts[1:]):
        pairs.append((values.at[pl.ds(first, last - first)], plain.at[pl.ds(first, last - first)]))
    copies = start_copies(pairs, semaphores)

    def row_of(row, _):
        at = pl.multiple_of(row * WIDE, WIDE)
        value = plain[pl.ds(at, WIDE), :]
        shifted_store(
            shifted, at, value.astype(F32), value,
            edges[pl.ds(base + row, 1), :], edges[pl.ds(base + 40 + row, 1), :],
        )
        return 0

    copies[0].wait()
    build_weight(filter_held, weight, forward)
    for copy in copies[1:]:
        copy.wait()
    lax.fori_loop(0, ROWS + 2, row_of, 0, unroll=2)


def backward_kernel(
    pre_in, filter_in, edges, mask_rows, tiles, low_grad,
    pair, plain, filter_held, bwd_one, pre_shift, semaphores,
):
    two = 2 * WIDE
    load_shifted(pre_in, filter_in, edges, 80, plain, filter_held, bwd_one, False, pre_shift, semaphores)
    order = iota((F, F), 0)
    tile_order = one_hot(
        iota((F, F), 1) == (((order >> 2) & 3) * WIDE + (order >> 4) * 4 + (order & 3))
    )

    def body(step, _):
        at = pl.multiple_of(step * 1024, 1024)
        grad_merged = conv(pre_shift, at, 1024, bwd_one) * wide_mask(mask_rows, step)
        rounded = grad_merged.astype(BF)
        for tile_row in range(4):
            tiles[pl.ds(at + tile_row * F, F), :] = dot(
                tile_order, rounded[tile_row * F : (tile_row + 1) * F, :]
            ).astype(BF)
        for row in range(8):
            both = grad_merged[row * two : row * two + WIDE, :] + grad_merged[row * two + WIDE : row * two + two, :]
            for half in range(2):
                pair[half, row * WIDE : (row + 1) * WIDE, :] = both[:, half * 128 : half * 128 + 128]
        for half in range(2):
            low_grad[pl.ds(pl.multiple_of(step * 256, 256), 256), half * 128 : half * 128 + 128] = (
                pair[half, pl.ds(0, 256, stride=2), :] + pair[half, pl.ds(1, 256, stride=2), :]
            ).astype(BF)
        return 0

    lax.fori_loop(0, 2, body, 0)


def forward_kernel(
    hidden_in, filter_in, edges, mask_rows, output, plain, filter_held, fwd_two, hidden_shift, semaphores
):
    load_shifted(hidden_in, filter_in, edges, 0, plain, filter_held, fwd_two, True, hidden_shift, semaphores)

    def body(step, _):
        at = pl.multiple_of(step * 1024, 1024)
        output[pl.ds(at, 1024), :] = (
            conv(hidden_shift, at, 1024, fwd_two) * wide_mask(mask_rows, step)
        ).astype(BF)
        return 0

    lax.fori_loop(0, 2, body, 0)


def pack_kernel(places, tiles, send):
    def copy(group, _):
        for sub in range(8):
            tile = group * 8 + sub
            place = places[0, tile]
            for half in range(2):
                value = tiles[pl.ds(pl.multiple_of(tile * 16, 16), 16), half * 128 : half * 128 + 128]
                send[place >> 1, pl.ds((place & 1) * 8 + half * 4, 4)] = value.reshape(4, 4, 128)
        return 0

    lax.fori_loop(0, 16, copy, 0)


def terms_kernel(send_in, got, slot_rows, send, rows, semaphore):
    total = jnp.zeros((3, 4, 128), F32)
    for part in range(128):
        total = total + got[part].astype(F32)
    front = total[0:2].astype(BF)
    row = iota((4, 128), 0)
    for part in range(128):
        rows[part, 0:2] = front
        rows[part, 2] = jnp.where(row == 1, slot_rows[part : part + 1, :], total[2]).astype(BF)
    copy = pltpu.make_async_copy(rows, send.at[:, pl.ds(16, 3)], semaphore)
    copy.start()
    copy.wait()


def place_kernel(scale, got, skip_grad, one, two, gathered, sources, folded, table, semaphore):
    for part in range(128):
        start, lanes = 9 * (part % 64), (part // 64) * 128
        terms = got[part, 16:19].astype(F32)
        folded[start : start + 4, lanes : lanes + 128] = terms[0] * scale
        folded[start + 4 : start + 8, lanes : lanes + 128] = terms[1] * scale
        folded[start + 8 : start + 9, lanes : lanes + 128] = terms[2, 0:1] * scale
        gathered[part : part + 1, :] = terms[2, 1:2]
    one[...] = folded[0:288, :]
    two[...] = folded[288:576, :]
    slots = gathered[...].T
    wanted = iota((128, 128), 0).astype(F32)
    index = iota((128, 128), 1).astype(F32)
    source = jnp.zeros((128, 128), F32)
    for which in range(2):
        source = source + jnp.where(slots[which : which + 1, :] == wanted, index * 2.0 + which, 0.0)
    sources[...] = jnp.broadcast_to(jnp.sum(source, axis=1, keepdims=True), (128, 128)).T[0:8, :].astype(jnp.int32)
    copy = pltpu.make_async_copy(sources, table, semaphore)
    copy.start()
    copy.wait()

    def put(group, _):
        for sub in range(32):
            slot = group * 32 + sub
            place = table[0, slot]
            for half in range(2):
                skip_grad[slot, :, :, half * 128 : half * 128 + 128] = got[
                    place >> 1, pl.ds((place & 1) * 8 + half * 4, 4)
                ]
        return 0

    lax.fori_loop(0, 4, put, 0)


def swap(values, axis, first):
    size = lax.axis_size(axis)
    partner = list(range(size))
    for index in range(first, size - 1, 2):
        partner[index], partner[index + 1] = index + 1, index
    return lax.ppermute(values, axis, list(enumerate(partner)))


def on_device(low_feats, skip_feats, tissue_mask, owner_slot, filter_one, filter_two, out_grad):
    everyone = ("rows", "cols")
    height, breadth, features = skip_feats.shape
    pixels = height * breadth
    given = (
        kept(low_feats.reshape(-1, F)), kept(skip_feats.reshape(pixels, F)),
        kept(out_grad.reshape(pixels, F)), kept(tissue_mask),
    )
    near, far_side = call(
        head_kernel, [shape((272, F))] * 2, 4,
        [
            pltpu.VMEM((64, F), BF), pltpu.VMEM((4 * WIDE, F), BF), pltpu.VMEM((4 * WIDE, F), BF),
            pltpu.VMEM((8, 16), jnp.int32), pltpu.VMEM((128, F), F32), pltpu.VMEM((4 * WIDE, F), BF),
            pltpu.VMEM((4 * WIDE, F), BF), pltpu.SemaphoreType.DMA((7,)),
        ],
        specs=[HBM] * 4, name="head",
    )(*given)
    near_rows = swap(near, "rows", 0)
    far_rows = swap(far_side, "rows", 1)
    bases = [f.transpose(1, 2, 0, 3).reshape(288, F) for f in (filter_one, filter_two)]
    merged, grad_two, mask_rows, fwd_one, bwd_two, places, slot_rows = call(
        prepare_kernel,
        [
            shape((pixels, F)), shape((pixels, F)), shape((128, F), F32), shape((9 * F, F)),
            shape((9 * F, F)), shape((8, 128), jnp.int32), shape((128, 128), F32),
        ],
        7,
        [
            pltpu.VMEM((pixels // 4, F), BF), pltpu.VMEM((pixels, F), BF), pltpu.VMEM((pixels, F), BF),
            pltpu.VMEM((8, 16), jnp.int32), pltpu.SemaphoreType.DMA((13,)),
        ],
        specs=[HBM] * 4 + [VMEM] * 3, flops=3 << 30, name="prepare",
    )(*given, owner_slot, *bases)
    left, right, top, bottom, near, far_side = call(
        edge_kernel,
        [shape((5 * STRIP, F))] * 2 + [shape((272, F))] * 2 + [shape((5 * STRIP, F))] * 2,
        5, [pltpu.VMEM((2, 48 * 16, 128), F32), pltpu.VMEM((STRIP, F), F32)], name="edge",
    )(merged, grad_two, near_rows, far_rows, mask_rows)
    near_cols = swap(near, "cols", 0)
    far_cols = swap(far_side, "cols", 1)
    inner = call(
        interior_kernel,
        [
            shape((pixels, 3 * F)), shape((30 * WIDE, F), F32), shape((30 * WIDE, F), F32),
            shape((4 * WIDE, 3 * F)),
        ],
        4, [pltpu.VMEM((pixels, 3 * F), BF)], flops=5 << 30, limit=16 << 20, name="interior",
    )(merged, grad_two, fwd_one, bwd_two)
    hidden, grad_pre, edges, message = call(
        first_kernel,
        [far((34 * WIDE, F)), far((34 * WIDE, F)), shape((160, F), F32), shape((128, 3, 4, 128))],
        15,
        [
            pltpu.VMEM((34 * WIDE, 3 * F), BF), pltpu.VMEM((34 * WIDE, 3 * F), BF),
            pltpu.VMEM((10 * WIDE, F), F32),
            pltpu.VMEM((36 * WIDE, 3 * F), BF), pltpu.VMEM((8 * WIDE, 3 * F), BF),
            pltpu.VMEM((6 * STRIP, F), F32),
            pltpu.VMEM((4 * WIDE, F), F32), pltpu.VMEM((4 * WIDE, F), F32), pltpu.VMEM((160, F), F32),
            pltpu.VMEM((592, F), F32), pltpu.SemaphoreType.DMA((2,)),
        ],
        outs=[HBM, HBM, VMEM, VMEM], flops=10 << 30, limit=36 << 20, name="first",
    )(merged, grad_two, top, bottom, left, right, near_cols, far_cols, mask_rows, fwd_one, bwd_two, *inner)
    got_terms = lax.all_to_all(message, everyone, 0, 0, tiled=True)
    loading = [
        pltpu.VMEM((34 * WIDE, F), BF), pltpu.VMEM((288, F), BF), pltpu.VMEM((9 * F, F), BF),
        pltpu.VMEM((34 * WIDE, 3 * F), BF), pltpu.SemaphoreType.DMA((5,)),
    ]
    tiles, low_grad = call(
        backward_kernel, [shape((pixels, F)), shape((pixels // 4, F))], 4,
        [pltpu.VMEM((2, 8 * WIDE, 128), F32)] + loading, specs=[HBM, HBM, VMEM, VMEM],
        flops=3 << 30, name="backward",
    )(kept(grad_pre), kept(bases[0]), edges, mask_rows)
    output = call(
        forward_kernel, shape((pixels, F)), 4, loading, specs=[HBM, HBM, VMEM, VMEM],
        flops=3 << 30, name="forward",
    )(kept(hidden), kept(bases[1]), edges, mask_rows)
    send = call(pack_kernel, far((128, 19, 4, 128)), 2, specs=[SMEM, VMEM], name="pack")(places, tiles)
    send = pl.pallas_call(
        terms_kernel,
        out_shape=far((128, 19, 4, 128)),
        in_specs=[HBM, VMEM, VMEM],
        out_specs=HBM,
        scratch_shapes=[pltpu.VMEM((128, 3, 4, 128), BF), pltpu.SemaphoreType.DMA],
        input_output_aliases={0: 0},
        compiler_params=pltpu.CompilerParams(vmem_limit_bytes=24 << 20),
        cost_estimate=pl.CostEstimate(flops=1 << 30, bytes_accessed=4 << 20, transcendentals=0),
        name="terms",
    )(kept(send), got_terms, slot_rows)
    got = lax.all_to_all(send, everyone, 0, 0, tiled=True)
    scale = 1.0 / math.sqrt(pixels * lax.axis_size("rows") * lax.axis_size("cols"))
    skip_grad, one, two = call(
        functools.partial(place_kernel, scale),
        [shape((128, 4, 4, F)), shape((288, F), F32), shape((288, F), F32)], 1,
        [
            pltpu.VMEM((128, 128), F32), pltpu.VMEM((8, 128), jnp.int32), pltpu.VMEM((592, F), F32),
            pltpu.SMEM((8, 128), jnp.int32), pltpu.SemaphoreType.DMA,
        ],
        name="place",
    )(got)
    return (
        output.reshape(height, breadth, F),
        skip_grad,
        low_grad.reshape(height // 2, breadth // 2, F),
        one.reshape(3, 3, 32, F).transpose(2, 0, 1, 3),
        two.reshape(3, 3, 32, F).transpose(2, 0, 1, 3),
    )


def solution(mesh):
    placed = (
        P("rows", "cols", None),
        P("rows", "cols", None),
        P("rows", "cols"),
        P("rows", "cols"),
        P(),
        P(),
        P("rows", "cols", None),
    )
    return jax.shard_map(
        on_device,
        mesh=mesh,
        in_specs=placed,
        out_specs=(
            P("rows", "cols", None),
            P(("rows", "cols"), None, None, None),
            P("rows", "cols", None),
            P(),
            P(),
        ),
        check_vma=False,
    )
```
